128 devices in a mesh: dp: 16 (over y_lo, x, core), mp: 8 (over z, y_hi).
Axes of the slice: x: 4, y: 4 (y_hi: 2, y_lo: 2; y = y_hi * 2 + y_lo), z: 4, core: 2. Of those that a mesh axis runs over, the one named last changes fastest.
Arguments:
- tokens: bfloat16 [16384, 2048], P(('dp', 'mp')), may hold values from -6 to 6
- seg_ids: int32 [16, 1024], P('dp'), may hold values from 0 to 7, never falling along the last dimension, each value on 1 to 256 neighbouring positions
- first_gain: bfloat16 [2048], replicated, may hold values from 0.099609375 to 1.8984375
- gelu_weight: bfloat16 [2048, 2560], P(None, 'mp'), may hold values from -0.125 to 0.125
- gelu_bias: bfloat16 [2560], P('mp'), may hold values from -3 to 3
- input_weight: bfloat16 [2048, 2560], P(None, 'mp'), may hold values from -0.125 to 0.125
- input_bias: bfloat16 [2560], P('mp'), may hold values from -3 to 3
- conv_weight: bfloat16 [4, 2560], P(None, 'mp'), may hold values from -3 to 3
- conv_bias: bfloat16 [2560], P('mp'), may hold values from -2 to 2
- rate_weight: bfloat16 [16, 160, 160], P('mp'), may hold values from -0.5 to 0.5
- rate_bias: bfloat16 [2560], P('mp'), may hold values from -3 to 3
- inflow_weight: bfloat16 [16, 160, 160], P('mp'), may hold values from -0.5 to 0.5
- inflow_bias: bfloat16 [2560], P('mp'), may hold values from -3 to 3
- decay_param: bfloat16 [2560], P('mp'), may hold values from 1 to 7
- mix_weight: bfloat16 [2560, 2048], P('mp'), may hold values from -0.3125 to 0.3125
- second_gain: bfloat16 [2048], replicated, may hold values from 0.099609375 to 1.8984375
- gate_weight: bfloat16 [2048, 6144], P(None, 'mp'), may hold values from -0.125 to 0.125
- up_weight: bfloat16 [2048, 6144], P(None, 'mp'), may hold values from -0.125 to 0.125
- down_weight: bfloat16 [6144, 2048], P('mp'), may hold values from -0.109375 to 0.109375
- cotangent: bfloat16 [16384, 2048], P(('dp', 'mp')), may hold values from -6 to 6
Outputs:
- result: bfloat16 [16384, 2048], P(('dp', 'mp'))
- tokens_grad: float32 [16384, 2048], P(('dp', 'mp'))
- grad_first_gain: float32 [2048], replicated
- grad_gelu_weight: float32 [2048, 2560], P('dp', 'mp')
- grad_gelu_bias: float32 [2560], P('mp')
- grad_input_weight: float32 [2048, 2560], P('dp', 'mp')
- grad_input_bias: float32 [2560], P('mp')
- grad_conv_weight: float32 [4, 2560], P(None, 'mp')
- grad_conv_bias: float32 [2560], P('mp')
- grad_rate_weight: float32 [16, 160, 160], P('mp')
- grad_rate_bias: float32 [2560], P('mp')
- grad_inflow_weight: float32 [16, 160, 160], P('mp')
- grad_inflow_bias: float32 [2560], P('mp')
- grad_decay_param: float32 [2560], P('mp')
- grad_mix_weight: float32 [2560, 2048], P('mp', 'dp')
- grad_second_gain: float32 [2048], replicated
- grad_gate_weight: float32 [2048, 6144], P('dp', 'mp')
- grad_up_weight: float32 [2048, 6144], P('dp', 'mp')
- grad_down_weight: float32 [6144, 2048], P('mp', 'dp')
The draws below stay inside these ranges and needn't reach their ends.
Inputs may be any that keep to these rules, and one draw needn't show every extreme that they name: `seg_ids`: along each row the ids never fall; each id covers 1 to 256 consecutive positions, and some id covers exactly 256.
All inputs are finite; a program needn't handle non-finite values.
Results may differ from the reference program's by a relative error of at most 0.022.
Values may be sent and summed in bfloat16 or wider, within the bound.
No kernel may reach another device: no remote copies, remote signals or barrier semaphores. Data moves between devices by JAX's collectives and lax.ppermute only.
A program may use at most 192 MiB of HBM per device.

```python
import math
import jax
import jax.numpy as jnp
import numpy as np
from jax import lax

D = 2048
RW = 2560
HEADS = 16
FF = 6144
KW = 4
DOCS = 8
ROWS_DP = 1024
BLK = 160
MOST = 256
TOKENS = 16384
N_DP = 16


def shard_levels(key, extent, shards, least, high):
    loudness = 1.0
    for position, shards_of in shards:
        heights = jax.random.uniform(jax.random.fold_in(jax.random.fold_in(key, 6), position), (shards_of,), jnp.float32, least / len(shards), high / len(shards))
        loudness = loudness * jnp.repeat(jnp.exp(heights), extent[position] // shards_of).reshape((-1,) + (1,) * (len(extent) - 1 - position))
    return loudness


def split_up(count, total, reach, skew):
    portions = [(1 << 20) // math.isqrt(grade ** skew) + 1 for grade in range(2, count + 1)]
    rest, given = total - reach - (count - 1), [1] * (count - 1)
    while rest > 0:
        candidates = [i for i in range(count - 1) if given[i] < reach]
        pool, budget = sum([portions[i] for i in candidates]), rest
        for i in candidates:
            addition = min(reach - given[i], max(1, budget * portions[i] // pool), rest)
            given[i] = given[i] + addition
            rest = rest - addition
    return np.array([reach] + given)


def uneven_parts(stream_key, number_of, total, most, slope):
    if number_of == 2:
        one = jax.random.randint(stream_key, (), max(1, total - most), min(most, total - 1) + 1)
        return jnp.stack([one, total - one])
    tallies = jnp.asarray(split_up(number_of, total, most, slope), jnp.int32)
    twos = (number_of - 1) // 2
    giver, taker = tallies[1:1 + 2 * twos:2], tallies[2:2 + 2 * twos:2]
    margin = jnp.minimum(giver - 1, most - taker)
    shifted = jax.random.randint(jax.random.fold_in(stream_key, 1), (twos,), 0, 1 << 20) % (margin + 1)
    tallies = tallies.at[1:1 + 2 * twos:2].set(giver - shifted).at[2:2 + 2 * twos:2].set(taker + shifted)
    return tallies[jax.random.permutation(jax.random.fold_in(stream_key, 2), number_of)]


def bell_draw(own_key, dims, spread, reach, pieces=(), kind=jnp.bfloat16):
    values = jax.random.normal(own_key, dims, jnp.float32) * spread
    if len(pieces) > 0:
        values = shard_levels(own_key, dims, pieces, -0.22, 0.18) * values
    return jnp.clip(values, min=-reach, max=reach).astype(kind)


def setup_inputs(seed: int = 0) -> dict:
    key_list = jax.random.split(jax.random.key(seed), 21)
    return {
        "tokens": bell_draw(key_list[0], (TOKENS, D), 1.0, 6.0, ((0, 128),)),
        "seg_ids": jax.vmap(lambda own: jnp.searchsorted(jnp.cumsum(uneven_parts(own, DOCS, ROWS_DP, MOST, 1)), jnp.arange(ROWS_DP), side="right"))(jax.random.split(key_list[1], N_DP)).reshape((N_DP, ROWS_DP)).astype(jnp.int32),
        "first_gain": jnp.clip(1.0 + 0.18 * jax.random.normal(key_list[2], (D,), jnp.float32), 0.099609375, 1.8984375).astype(jnp.bfloat16),
        "gelu_weight": bell_draw(key_list[3], (D, RW), D ** -0.5, 0.125, ((1, 8),)),
        "gelu_bias": bell_draw(key_list[4], (RW,), 0.5, 3.0, ((0, 8),)),
        "input_weight": bell_draw(key_list[5], (D, RW), D ** -0.5, 0.125, ((1, 8),)),
        "input_bias": bell_draw(key_list[6], (RW,), 0.5, 3.0, ((0, 8),)),
        "conv_weight": bell_draw(key_list[7], (KW, RW), 0.5, 3.0, ((1, 8),)),
        "conv_bias": bell_draw(key_list[8], (RW,), 0.3, 2.0, ((0, 8),)),
        "rate_weight": bell_draw(key_list[9], (HEADS, BLK, BLK), BLK ** -0.5, 0.5, ((0, 8),)),
        "rate_bias": bell_draw(key_list[10], (RW,), 0.5, 3.0, ((0, 8),)),
        "inflow_weight": bell_draw(key_list[11], (HEADS, BLK, BLK), BLK ** -0.5, 0.5, ((0, 8),)),
        "inflow_bias": bell_draw(key_list[12], (RW,), 0.5, 3.0, ((0, 8),)),
        "decay_param": jnp.clip(1.0 + 6.0 * jax.random.uniform(key_list[13], (RW,), jnp.float32) ** shard_levels(key_list[13], (RW,), ((0, 8),), -0.2, 0.2), 1.0, 7.0).astype(jnp.bfloat16),
        "mix_weight": bell_draw(key_list[14], (RW, D), (RW // 8) ** -0.5, 0.3125, ((0, 8),)),
        "second_gain": jnp.clip(1.0 + 0.18 * jax.random.normal(key_list[15], (D,), jnp.float32), 0.099609375, 1.8984375).astype(jnp.bfloat16),
        "gate_weight": bell_draw(key_list[16], (D, FF), D ** -0.5, 0.125, ((1, 8),)),
        "up_weight": bell_draw(key_list[17], (D, FF), D ** -0.5, 0.125, ((1, 8),)),
        "down_weight": bell_draw(key_list[18], (FF, D), (FF // 2) ** -0.5, 0.109375, ((0, 8),)),
        "cotangent": bell_draw(key_list[19], (TOKENS, D), 1.0, 6.0, ((0, 128),)),
    }


@jax.custom_vjp
def low(v):
    return lax.optimization_barrier(v.astype(jnp.bfloat16)).astype(jnp.float32)

@jax.custom_vjp
def low_back(v):
    return v

def low_keep(v):
    return (low(v), None)

def low_pass(kept, grad):
    return (grad,)

def back_keep(v):
    return (v, None)

def back_low(kept, grad):
    return (low(grad),)
low.defvjp(low_keep, low_pass)
low_back.defvjp(back_keep, back_low)
EPSILON = 1e-06
DECAY_SCALE = 8.0
HIGHEST = lax.Precision.HIGHEST

def product(left, right):
    return jnp.dot(left, right, precision=HIGHEST)

def rms_scaled(values, gain):
    return values * lax.rsqrt(lax.optimization_barrier(jnp.mean(values * values, axis=-1, keepdims=True)) + EPSILON) * gain

def earlier(values, steps):
    return jnp.concatenate([jnp.zeros((steps,) + values.shape[1:], values.dtype), values[:-steps]], 0)

def segment_keeps(seg_row):
    seg_int = seg_row.astype(jnp.int32)
    keeps = [jnp.ones((seg_int.shape[0], 1), jnp.float32)]
    for steps in range(1, KW):
        before = jnp.concatenate([jnp.full((steps,), -1, jnp.int32), seg_int[:-steps]])
        keeps.append((before == seg_int).astype(jnp.float32)[:, None])
    return jnp.stack(keeps)

def linear_step(earlier_pair, later_pair):
    decay_one, state_one = earlier_pair
    decay_two, state_two = later_pair
    return (decay_one * decay_two, decay_two * state_one + state_two)

def convolve(values, kernel, bias, keeps):
    total = bias + kernel[0] * values
    for steps in range(1, KW):
        total = total + kernel[steps] * earlier(values, steps) * keeps[steps]
    return total

def gate_core(rate_logit, inflow_logit, conv_vals, decay_param, reset):
    log_rate = -DECAY_SCALE * jax.nn.sigmoid(rate_logit) * jax.nn.softplus(-decay_param)
    decay = jnp.exp(log_rate) * (1.0 - reset)
    factor = jnp.sqrt(-jnp.expm1(2.0 * log_rate)) * (1.0 - reset) + reset
    return (decay, factor * jax.nn.sigmoid(inflow_logit) * conv_vals)

def block(params, tokens, keeps):
    first_gain, gelu_weight, gelu_bias, input_weight, input_bias, conv_weight, conv_bias, rate_weight, rate_bias, inflow_weight, inflow_bias, decay_param, mix_weight, second_gain, gate_weight, up_weight, down_weight = params
    length = tokens.shape[0]
    first_normed = low(rms_scaled(tokens, first_gain))
    gelu_pre = low_back(product(first_normed, gelu_weight) + gelu_bias)
    input_pre = low_back(product(first_normed, input_weight) + input_bias)
    conv_vals = low(convolve(input_pre, conv_weight, conv_bias, keeps))
    blocks_in = conv_vals.reshape(length, HEADS, BLK)
    rate_logit = low_back(jnp.einsum('thb,hbc->thc', blocks_in, rate_weight, precision=HIGHEST).reshape(length, RW) + rate_bias)
    inflow_logit = low_back(jnp.einsum('thb,hbc->thc', blocks_in, inflow_weight, precision=HIGHEST).reshape(length, RW) + inflow_bias)
    decay, inject = gate_core(rate_logit, inflow_logit, conv_vals, decay_param, 1.0 - keeps[1])
    state = lax.associative_scan(linear_step, (decay, inject))[1]
    gated = low(jax.nn.gelu(gelu_pre, approximate=True) * state)
    middle = tokens + low_back(product(gated, mix_weight))
    second_normed = low(rms_scaled(middle, second_gain))
    gate_pre = low_back(product(second_normed, gate_weight))
    up_pre = low_back(product(second_normed, up_weight))
    hidden = low(jax.nn.gelu(gate_pre, approximate=True) * up_pre)
    return middle + product(hidden, down_weight)

def reference(tokens, seg_ids, first_gain, gelu_weight, gelu_bias, input_weight, input_bias, conv_weight, conv_bias, rate_weight, rate_bias, inflow_weight, inflow_bias, decay_param, mix_weight, second_gain, gate_weight, up_weight, down_weight, cotangent):
    weights = tuple((w.astype(jnp.float32) for w in (first_gain, gelu_weight, gelu_bias, input_weight, input_bias, conv_weight, conv_bias, rate_weight, rate_bias, inflow_weight, inflow_bias, decay_param, mix_weight, second_gain, gate_weight, up_weight, down_weight)))
    sequences = tokens.astype(jnp.float32).reshape(N_DP, ROWS_DP, D)
    cot_rows = cotangent.astype(jnp.float32).reshape(N_DP, ROWS_DP, D)

    def one_sequence(total, item):
        rows, seg_row, grad_rows = item
        keeps = segment_keeps(seg_row)
        output, backward = jax.vjp(lambda params, values: block(params, values, keeps), weights, rows)
        param_grads, rows_grad = backward(grad_rows)
        total = jax.tree.map(lambda left, right: left + right, total, param_grads)
        return (total, (output, rows_grad))
    zeros = jax.tree.map(jnp.zeros_like, weights)
    totals, (outputs, row_grads) = lax.scan(one_sequence, zeros, (sequences, seg_ids, cot_rows))
    result = outputs.reshape(N_DP * ROWS_DP, D).astype(jnp.bfloat16)
    tokens_grad = row_grads.reshape(N_DP * ROWS_DP, D)
    return (result, tokens_grad, totals[0], totals[1], totals[2], totals[3], totals[4], totals[5], totals[6], totals[7], totals[8], totals[9], totals[10], totals[11], totals[12], totals[13], totals[14], totals[15], totals[16])
```

```python
import jax
import jax.numpy as jnp
from jax import lax
from jax.experimental import pallas as pl
from jax.experimental.pallas import tpu as pltpu
from jax.sharding import PartitionSpec as P

EPSILON = 1e-06
DECAY_SCALE = 8.0
GELU_SCALE = 0.7978845608028654
GELU_CUBE = 0.044715
CHUNK = 64
PARTS = 8


def one_minus_exp(double_rate, exp_square):
    y = -double_rate
    series = 1.0 - y * (1.0 / 7.0)
    for order in (6.0, 5.0, 4.0, 3.0, 2.0):
        series = 1.0 - y * (1.0 / order) * series
    return jnp.where(y < 0.5, y * series, 1.0 - exp_square)


def gelu_parts(values):
    square = values * values
    slope = GELU_SCALE + (GELU_SCALE * GELU_CUBE) * square
    bend = jnp.tanh(values * slope)
    half = 0.5 + 0.5 * bend
    return half, bend, square


def recurrent_forward(
    offsets, pre, keep, params, gate_weight, gated, conv, rate, inflow, decay, root, state,
    padded, logits, decays, injects, products, ends,
):
    rows, width = conv.shape
    piece = rows // PARTS

    padded[0:8, :] = jnp.zeros((8, width), jnp.float32)
    for part in range(PARTS):
        place = pl.multiple_of(offsets[part] + 8, 8)
        padded[pl.ds(place, piece), :] = (
            pre[part * piece : (part + 1) * piece, width:] + params[1:2, :]
        )

    def conv_chunk(index, carry):
        base = pl.multiple_of(index * CHUNK, CHUNK)
        window = padded[pl.ds(base, CHUNK + 8), :]
        keeps = keep[pl.ds(base, CHUNK), :]
        total = params[2:3, :] + params[3:4, :] * window[8:, :]
        for steps in (1, 2, 3):
            shifted = window[8 - steps : 8 - steps + CHUNK, :]
            total = total + params[3 + steps : 4 + steps, :] * shifted * keeps[:, steps - 1 : steps]
        conv[pl.ds(base, CHUNK), :] = total.astype(jnp.bfloat16)
        return carry

    lax.fori_loop(0, rows // CHUNK, conv_chunk, 0)

    logits[...] = jnp.dot(conv[...], gate_weight[...], preferred_element_type=jnp.float32)

    def gate_chunk(index, carry):
        base = pl.multiple_of(index * CHUNK, CHUNK)
        here = pl.ds(base, CHUNK)
        kept = keep[here, 0:1]
        rate_sig = jax.nn.sigmoid(logits[here, :width] + params[7:8, :])
        inflow_sig = jax.nn.sigmoid(logits[here, width:] + params[8:9, :])
        log_rate = rate_sig * params[9:10, :]
        plain = jnp.exp(log_rate)
        hole = jnp.sqrt(one_minus_exp(2.0 * log_rate, plain * plain))
        factor = hole * kept + (1.0 - kept)
        rate[here, :] = rate_sig
        inflow[here, :] = inflow_sig
        decay[here, :] = plain
        root[here, :] = hole
        kept_decay = plain * kept
        inject = factor * inflow_sig * conv[here, :].astype(jnp.float32)
        for lane in range(width // 128):
            decays[lane, here, :] = kept_decay[:, lane * 128 : (lane + 1) * 128]
            injects[lane, here, :] = inject[:, lane * 128 : (lane + 1) * 128]
        return carry

    lax.fori_loop(0, rows // CHUNK, gate_chunk, 0)

    lanes = width // 128
    zero = jnp.zeros((PARTS, 128), jnp.float32)
    one = jnp.ones((PARTS, 128), jnp.float32)

    def scan_step(step, carry):
        result = []
        for lane in range(lanes):
            value, product = carry[lane]
            factor = decays[lane, pl.ds(step, PARTS, stride=piece), :]
            value = factor * value + injects[lane, pl.ds(step, PARTS, stride=piece), :]
            product = factor * product
            injects[lane, pl.ds(step, PARTS, stride=piece), :] = value
            products[lane, pl.ds(step, PARTS, stride=piece), :] = product
            result.append((value, product))
        return tuple(result)

    last = lax.fori_loop(0, piece, scan_step, ((zero, one),) * lanes, unroll=8)
    for lane in range(lanes):
        value, product = last[lane]
        entering = jnp.zeros((1, 128), jnp.float32)
        for part in range(PARTS):
            ends[part, 0:1, lane * 128 : (lane + 1) * 128] = entering
            entering = value[part : part + 1, :] + product[part : part + 1, :] * entering

    def finish_part(part, carry):
        start = pl.multiple_of(offsets[part], piece)
        segment = offsets[part] // piece
        for half in range(piece // CHUNK):
            there = pl.ds(pl.multiple_of(start + half * CHUNK, CHUNK), CHUNK)
            local = pl.ds(pl.multiple_of(part * piece + half * CHUNK, CHUNK), CHUNK)
            for lane in range(lanes):
                cols = slice(lane * 128, (lane + 1) * 128)
                whole = (
                    injects[lane, there, :]
                    + products[lane, there, :] * ends[segment, 0:1, cols]
                )
                state[there, cols] = whole
                values = pre[local, cols] + params[0:1, cols]
                act = values * gelu_parts(values)[0]
                gated[local, cols] = (act * whole).astype(jnp.bfloat16)
        return carry

    lax.fori_loop(0, PARTS, finish_part, 0)


def recurrent_backward(
    offsets, gated_grad, pre, keep, params, gate_weight, conv, rate, inflow, decay, root, state,
    branch_grad, gate_grad, sums,
    padded, carried, decays, products, ends, before, logit_grad, conv_grad, shifted_grad,
):
    rows, width = conv.shape
    piece = rows // PARTS
    lanes = width // 128
    zero_rows = jnp.zeros((8, width), jnp.float32)

    padded[0:8, :] = zero_rows
    before[0:8, :] = zero_rows
    for lane in range(lanes):
        decays[lane, rows : rows + 8, :] = jnp.zeros((8, 128), jnp.float32)
    shifted_grad[:, rows : rows + 8, :] = jnp.zeros((3, 8, width), jnp.float32)

    def enter_part(part, total):
        start = pl.multiple_of(offsets[part], piece)
        for half in range(piece // CHUNK):
            there = pl.ds(pl.multiple_of(start + half * CHUNK, CHUNK), CHUNK)
            ahead = pl.ds(pl.multiple_of(start + half * CHUNK + 8, 8), CHUNK)
            local = pl.ds(pl.multiple_of(part * piece + half * CHUNK, CHUNK), CHUNK)
            kept = keep[there, 0:1]
            padded[ahead, :] = pre[local, width:] + params[1:2, :]
            values = pre[local, :width] + params[0:1, :]
            upper, bend, square = gelu_parts(values)
            slope = upper + 0.5 * values * (1.0 - bend * bend) * (
                GELU_SCALE + (3.0 * GELU_SCALE * GELU_CUBE) * square
            )
            grad = gated_grad[local, :]
            here_state = state[there, :]
            before[ahead, :] = here_state
            gelu_grad = (grad * here_state * slope).astype(jnp.bfloat16)
            branch_grad[local, :width] = gelu_grad
            total = total + jnp.sum(
                gelu_grad.astype(jnp.float32).reshape(CHUNK // 8, 8, width), axis=0
            )
            state_grad = grad * values * upper
            kept_decay = decay[there, :] * kept
            for lane in range(lanes):
                cols = slice(lane * 128, (lane + 1) * 128)
                carried[lane, there, :] = state_grad[:, cols]
                decays[lane, there, :] = kept_decay[:, cols]
        return total

    gelu_sum = lax.fori_loop(0, PARTS, enter_part, zero_rows)

    zero = jnp.zeros((PARTS, 128), jnp.float32)
    one = jnp.ones((PARTS, 128), jnp.float32)

    def scan_step(count, carry):
        step = piece - 1 - count
        result = []
        for lane in range(lanes):
            value, product = carry[lane]
            factor = decays[lane, pl.ds(step + 1, PARTS, stride=piece), :]
            value = factor * value + carried[lane, pl.ds(step, PARTS, stride=piece), :]
            product = factor * product
            carried[lane, pl.ds(step, PARTS, stride=piece), :] = value
            products[lane, pl.ds(step, PARTS, stride=piece), :] = product
            result.append((value, product))
        return tuple(result)

    last = lax.fori_loop(0, piece, scan_step, ((zero, one),) * lanes, unroll=8)
    for lane in range(lanes):
        value, product = last[lane]
        entering = jnp.zeros((1, 128), jnp.float32)
        for part in range(PARTS - 1, -1, -1):
            ends[part, 0:1, lane * 128 : (lane + 1) * 128] = entering
            entering = value[part : part + 1, :] + product[part : part + 1, :] * entering

    def gate_chunk(index, totals):
        rate_sum, inflow_sum, decay_sum = totals
        base = pl.multiple_of(index * CHUNK, CHUNK)
        here = pl.ds(base, CHUNK)
        segment = base // piece
        kept = keep[here, 0:1]
        grad = jnp.concatenate(
            [
                carried[lane, here, :]
                + products[lane, here, :]
                * ends[segment, 0:1, lane * 128 : (lane + 1) * 128]
                for lane in range(lanes)
            ],
            axis=1,
        )
        earlier = before[pl.ds(base, CHUNK + 8), :][7 : 7 + CHUNK, :]
        plain = decay[here, :]
        hole = root[here, :]
        rate_sig = rate[here, :]
        inflow_sig = inflow[here, :]
        conv_vals = conv[here, :].astype(jnp.float32)
        factor = hole * kept + (1.0 - kept)
        scaled = grad * inflow_sig
        log_grad = (
            (grad * earlier * plain - scaled * conv_vals * (plain * plain) / hole) * kept
        )
        rate_low = (
            log_grad * params[9:10, :] * rate_sig * (1.0 - rate_sig)
        ).astype(jnp.bfloat16)
        elem = scaled * factor
        inflow_low = (elem * conv_vals * (1.0 - inflow_sig)).astype(jnp.bfloat16)
        logit_grad[here, :width] = rate_low
        logit_grad[here, width:] = inflow_low
        conv_grad[here, :] = elem

        def fold(values):
            return jnp.sum(values.reshape(CHUNK // 8, 8, width), axis=0)

        return (
            rate_sum + fold(rate_low.astype(jnp.float32)),
            inflow_sum + fold(inflow_low.astype(jnp.float32)),
            decay_sum + fold(log_grad * rate_sig),
        )

    rate_sum, inflow_sum, decay_sum = lax.fori_loop(
        0, rows // CHUNK, gate_chunk, (zero_rows, zero_rows, zero_rows)
    )

    conv_grad[...] += lax.dot_general(
        logit_grad[...],
        gate_weight[...],
        (((1,), (1,)), ((), ())),
        preferred_element_type=jnp.float32,
    )
    gate_grad[...] = lax.dot_general(
        conv[...],
        logit_grad[...],
        (((0,), (0,)), ((), ())),
        preferred_element_type=jnp.float32,
    )

    def tap_chunk(index, totals):
        base = pl.multiple_of(index * CHUNK, CHUNK)
        here = pl.ds(base, CHUNK)
        grad = conv_grad[here, :]
        keeps = keep[here, :]
        window = padded[pl.ds(base, CHUNK + 8), :]

        def fold(values):
            return jnp.sum(values.reshape(CHUNK // 8, 8, width), axis=0)

        result = [totals[0] + fold(grad), totals[1] + fold(grad * window[8:, :])]
        for steps in (1, 2, 3):
            kept_grad = grad * keeps[:, steps - 1 : steps]
            shifted_grad[steps - 1, here, :] = kept_grad
            result.append(
                totals[1 + steps] + fold(kept_grad * window[8 - steps : 8 - steps + CHUNK, :])
            )
        return tuple(result)

    taps = lax.fori_loop(0, rows // CHUNK, tap_chunk, (zero_rows,) * 5)

    def leave_part(part, total):
        start = pl.multiple_of(offsets[part], piece)
        for half in range(piece // CHUNK):
            base = pl.multiple_of(start + half * CHUNK, CHUNK)
            local = pl.ds(pl.multiple_of(part * piece + half * CHUNK, CHUNK), CHUNK)
            grad = params[3:4, :] * conv_grad[pl.ds(base, CHUNK), :]
            for steps in (1, 2, 3):
                window = shifted_grad[steps - 1, pl.ds(base, CHUNK + 8), :]
                grad = grad + params[3 + steps : 4 + steps, :] * window[steps : steps + CHUNK, :]
            low = grad.astype(jnp.bfloat16)
            branch_grad[local, width:] = low
            total = total + jnp.sum(low.astype(jnp.float32).reshape(CHUNK // 8, 8, width), axis=0)
        return total

    input_sum = lax.fori_loop(0, PARTS, leave_part, zero_rows)

    all_sums = (
        gelu_sum, input_sum, taps[1], taps[2], taps[3], taps[4], taps[0], rate_sum, inflow_sum,
    )
    for row, total in enumerate(all_sums):
        sums[row : row + 1, :] = jnp.sum(total, axis=0, keepdims=True)
    sums[9:10, :] = jnp.sum(decay_sum, axis=0, keepdims=True) * params[10:11, :]
    sums[10:16, :] = jnp.zeros((6, width), jnp.float32)


VMEM_SPEC = pl.BlockSpec(memory_space=pltpu.VMEM)
SMEM_SPEC = pl.BlockSpec(memory_space=pltpu.SMEM)


def run_forward(offsets, pre, keep, params, gate_weight):
    rows, width = pre.shape[0], pre.shape[1] // 2
    lanes = width // 128
    f32, low = jnp.float32, jnp.bfloat16
    full = jax.ShapeDtypeStruct((rows, width), f32)
    half = jax.ShapeDtypeStruct((rows, width), low)
    return pl.pallas_call(
        recurrent_forward,
        out_shape=(half, half, full, full, full, full, full),
        in_specs=[SMEM_SPEC] + [VMEM_SPEC] * 4,
        out_specs=(VMEM_SPEC,) * 7,
        scratch_shapes=[
            pltpu.VMEM((rows + 8, width), f32),
            pltpu.VMEM((rows, 2 * width), f32),
            pltpu.VMEM((lanes, rows, 128), f32),
            pltpu.VMEM((lanes, rows, 128), f32),
            pltpu.VMEM((lanes, rows, 128), f32),
            pltpu.VMEM((PARTS, 8, width), f32),
        ],
        compiler_params=pltpu.CompilerParams(vmem_limit_bytes=40 * 1024 * 1024),
        cost_estimate=pl.CostEstimate(
            flops=2 * rows * width * 2 * width, bytes_accessed=20 * rows * width * 4,
            transcendentals=5 * rows * width,
        ),
    )(offsets, pre, keep, params, gate_weight)


def run_backward(offsets, gated_grad, pre, keep, params, gate_weight, kept):
    rows, width = pre.shape[0], pre.shape[1] // 2
    lanes = width // 128
    f32, low = jnp.float32, jnp.bfloat16
    return pl.pallas_call(
        recurrent_backward,
        out_shape=(
            jax.ShapeDtypeStruct((rows, 2 * width), low),
            jax.ShapeDtypeStruct((width, 2 * width), f32),
            jax.ShapeDtypeStruct((16, width), f32),
        ),
        in_specs=[SMEM_SPEC] + [VMEM_SPEC] * 11,
        out_specs=(VMEM_SPEC,) * 3,
        scratch_shapes=[
            pltpu.VMEM((rows + 8, width), f32),
            pltpu.VMEM((lanes, rows, 128), f32),
            pltpu.VMEM((lanes, rows + 8, 128), f32),
            pltpu.VMEM((lanes, rows, 128), f32),
            pltpu.VMEM((PARTS, 8, width), f32),
            pltpu.VMEM((rows + 8, width), f32),
            pltpu.VMEM((rows, 2 * width), low),
            pltpu.VMEM((rows, width), f32),
            pltpu.VMEM((3, rows + 8, width), f32),
        ],
        compiler_params=pltpu.CompilerParams(vmem_limit_bytes=48 * 1024 * 1024),
        cost_estimate=pl.CostEstimate(
            flops=8 * rows * width * 2 * width, bytes_accessed=30 * rows * width * 4,
            transcendentals=5 * rows * width,
        ),
    )(offsets, gated_grad, pre, keep, params, gate_weight, *kept)


RING = 4
PIECES = ((0, 0), (0, 1), (-1, 0), (-1, 1), (1, 0), (1, 1), (2, 0), (2, 1))


def mp_shift(values, along, across):
    pairs = [
        (ring * 2 + side, ((ring + along) % RING) * 2 + (side + across) % 2)
        for ring in range(RING)
        for side in range(2)
    ]
    return lax.ppermute(values, "mp", pairs)


def swap_sum(values, axis, size, steps, low):
    for step in steps:
        if low:
            values = values.astype(jnp.bfloat16)
        other = lax.ppermute(values, axis, [(place, place ^ step) for place in range(size)])
        values = values.astype(jnp.float32) + other.astype(jnp.float32)
    return values


def gather_pieces(mine):
    across = mp_shift(mine, 0, 1)
    below = mp_shift(mine, 1, 0)
    above = mp_shift(mine, -1, 0)
    below_across = mp_shift(across, 1, 0)
    above_across = mp_shift(across, -1, 0)
    far = mp_shift(below, 1, 0)
    far_across = mp_shift(above_across, -1, 0)
    return [mine, across, below, below_across, above, above_across, far, far_across]


def scatter_sum(make, rows):
    low = jnp.bfloat16
    far = make(6, 8)
    middle = make(2, 6)
    near = make(0, 2)
    far_one = mp_shift(far[:rows].astype(low), 1, 0)
    far_two = mp_shift(far[rows:].astype(low), -1, 0)
    side_up = mp_shift(middle[3 * rows :].astype(low), 1, 0)
    side_down = mp_shift(middle[:rows].astype(low), -1, 0)
    joined_down = mp_shift(
        (middle[rows : 2 * rows] + far_two.astype(jnp.float32)).astype(low), -1, 0
    )
    joined_up = mp_shift(
        (middle[2 * rows : 3 * rows] + far_one.astype(jnp.float32)).astype(low), 1, 0
    )
    other = near[rows:] + joined_down.astype(jnp.float32) + side_up.astype(jnp.float32)
    other = mp_shift(other.astype(low), 0, 1)
    return (
        near[:rows]
        + joined_up.astype(jnp.float32)
        + side_down.astype(jnp.float32)
        + other.astype(jnp.float32)
    )


def direct_sum(parts, rows):
    total = parts[:rows].astype(jnp.float32)
    for place, (along, across) in enumerate(PIECES):
        if place:
            total = total + mp_shift(
                parts[place * rows : (place + 1) * rows], along, across
            ).astype(jnp.float32)
    return total


def rms_forward(values, gain):
    scale = lax.rsqrt(jnp.mean(values * values, axis=-1, keepdims=True) + EPSILON)
    return (values * scale * gain, scale)


def rms_backward(values, scale, gain, grad):
    scaled_grad = grad * gain
    inner = jnp.mean(scaled_grad * values, axis=-1, keepdims=True)
    return scale * scaled_grad - values * scale * scale * scale * inner


def gelu_tanh(values):
    return jax.nn.gelu(values, approximate=True)


def tie(values, anchor):
    return lax.optimization_barrier((values, anchor))[0]


def block_diagonal(weight, width):
    size = weight.shape[1]
    return jnp.concatenate(
        [
            jnp.pad(weight[0], ((0, 0), (0, width - size))),
            jnp.pad(weight[1], ((0, 0), (size, width - 2 * size))),
            jnp.zeros((width - 2 * size, width), weight.dtype),
        ],
        0,
    )


def on_device(
    tokens,
    seg_ids,
    first_gain,
    gelu_weight,
    gelu_bias,
    input_weight,
    input_bias,
    conv_weight,
    conv_bias,
    rate_weight,
    rate_bias,
    inflow_weight,
    inflow_bias,
    decay_param,
    mix_weight,
    second_gain,
    gate_weight,
    up_weight,
    down_weight,
    cotangent,
):
    f32, low = jnp.float32, jnp.bfloat16
    seg_row = seg_ids[0]
    rows = tokens.shape[0]
    model = tokens.shape[1]
    width = gelu_weight.shape[1]
    hidden_width = gate_weight.shape[1]
    size = rate_weight.shape[1]
    wide = -(-width // 128) * 128
    place = lax.axis_index("mp")
    ring, side = place // 2, place % 2
    offsets = jnp.stack(
        [
            (((ring + along + RING) % RING) * 2 + (side + across) % 2) * rows
            for along, across in PIECES
        ]
    ).astype(jnp.int32)

    def dot(left, right):
        return jnp.dot(left, right, preferred_element_type=f32)

    def dot_rows(left, right):
        return lax.dot_general(left, right, (((0,), (0,)), ((), ())), preferred_element_type=f32)

    def dot_back(left, right):
        return lax.dot_general(left, right, (((1,), (1,)), ((), ())), preferred_element_type=f32)

    rows_in = tokens.astype(f32)
    first_scale_gain = first_gain.astype(f32)
    second_scale_gain = second_gain.astype(f32)
    cot_rows = cotangent.astype(f32)
    first_normed, first_scale = rms_forward(rows_in, first_scale_gain)
    normed_pieces = gather_pieces(first_normed.astype(low))

    keep_list = []
    for steps in (1, 2, 3):
        before = jnp.concatenate([jnp.full((steps,), -1, jnp.int32), seg_row[:-steps]])
        keep_list.append((before == seg_row).astype(f32))
    keep = jnp.stack(keep_list + [jnp.zeros_like(keep_list[0])] * 5, axis=1)
    decay_vals = jnp.pad(decay_param.astype(f32), (0, wide - width), constant_values=1.0)

    def row(values):
        return jnp.pad(values.astype(f32), (0, wide - width))

    params = jnp.stack(
        [row(gelu_bias), row(input_bias), row(conv_bias)]
        + [row(conv_weight[tap]) for tap in range(4)]
        + [
            row(rate_bias),
            row(inflow_bias),
            -DECAY_SCALE * jax.nn.softplus(-decay_vals),
            DECAY_SCALE * jax.nn.sigmoid(-decay_vals),
        ]
        + [jnp.zeros((wide,), f32)] * 5
    )
    lane_pad = ((0, 0), (0, wide - width))
    branch_weight = jnp.concatenate(
        [jnp.pad(gelu_weight, lane_pad), jnp.pad(input_weight, lane_pad)], 1
    )
    mix_wide = jnp.pad(mix_weight, ((0, wide - width), (0, 0)))
    gates_weight = jnp.concatenate(
        [block_diagonal(rate_weight, wide), block_diagonal(inflow_weight, wide)], 1
    )

    normed_full = jnp.concatenate(normed_pieces, 0)
    cot_full = lax.all_gather(tie(cotangent, normed_pieces[6]), "mp", axis=0, tiled=True)
    pre = dot(normed_full, branch_weight)
    gated, *kept = run_forward(offsets, pre, keep, params, gates_weight)

    mixed = scatter_sum(
        lambda start, stop: dot(gated[start * rows : stop * rows], mix_wide), rows
    )
    middle = rows_in + mixed
    second_normed, second_scale = rms_forward(middle, second_scale_gain)
    second_full = jnp.concatenate(gather_pieces(second_normed.astype(low)), 0)
    cot_turned = jnp.concatenate(
        [lax.dynamic_slice_in_dim(cot_full, offsets[part], rows, 0) for part in range(PARTS)], 0
    )

    gate_pre = dot(second_full, gate_weight)
    up_pre = dot(second_full, up_weight)
    gate_act, gate_back = jax.vjp(gelu_tanh, gate_pre)
    hidden = (gate_act * up_pre).astype(low)
    hidden_grad = dot_back(cot_turned, down_weight)
    gate_grad = gate_back(hidden_grad * up_pre)[0].astype(low)
    up_grad = (hidden_grad * gate_act).astype(low)

    def second_back(start, stop):
        here = slice(start * rows, stop * rows)
        return dot_back(gate_grad[here], gate_weight) + dot_back(up_grad[here], up_weight)

    second_grad = scatter_sum(second_back, rows)
    middle_grad = cot_rows + rms_backward(middle, second_scale, second_scale_gain, second_grad)
    second_gain_local = jnp.sum(second_grad * middle * second_scale, axis=0)
    mixer_pieces = gather_pieces(middle_grad.astype(low))
    mixer_full = jnp.concatenate(mixer_pieces, 0)

    feed_grads = lax.psum_scatter(
        jnp.concatenate(
            [
                dot_rows(second_full, gate_grad).astype(low),
                dot_rows(second_full, up_grad).astype(low),
                dot_rows(cot_turned, hidden).astype(low),
            ],
            1,
        ),
        "dp",
        scatter_dimension=0,
        tiled=True,
    )
    down_parts = dot(hidden, down_weight).astype(low)
    final = middle + direct_sum(tie(down_parts, mixer_pieces[6]), rows)
    result = final.astype(low)

    gated_grad = dot_back(mixer_full, mix_wide)
    branch_grad, gates_grad, sums = run_backward(
        offsets, gated_grad, pre, keep, params, gates_weight, kept
    )
    first_grad = scatter_sum(
        lambda start, stop: dot_back(branch_grad[start * rows : stop * rows], branch_weight), rows
    )
    tokens_grad = middle_grad + rms_backward(rows_in, first_scale, first_scale_gain, first_grad)

    branch_sum = dot_rows(normed_full, branch_grad)
    mix_sum = dot_rows(mixer_full, gated)
    first_gain_local = (
        jnp.sum(branch_sum * branch_weight.astype(f32), axis=1) / first_scale_gain
    )
    branch_grads = lax.psum_scatter(
        jnp.concatenate(
            [branch_sum[:, :width], branch_sum[:, wide : wide + width], mix_sum[:, :width]], 1
        ).astype(low),
        "dp",
        scatter_dimension=0,
        tiled=True,
    )
    gate_blocks = jnp.concatenate(
        [
            gates_grad[:size, :size],
            gates_grad[size : 2 * size, size : 2 * size],
            gates_grad[:size, wide : wide + size],
            gates_grad[size : 2 * size, wide + size : wide + 2 * size],
        ],
        1,
    )
    small = jnp.concatenate(
        [gate_blocks, jnp.pad(sums[:, :width], ((0, 0), (0, 4 * size - width)))], 0
    )
    small = swap_sum(small, "dp", 16, (1, 2, 4, 8), True)
    gains = jnp.stack([first_gain_local, second_gain_local])
    gains = swap_sum(gains, "dp", 16, (1, 2, 4, 8), False)
    gains = swap_sum(gains, "mp", 8, (1, 2, 4), False)
    sums = small[size:, :width]
    branch_grads = branch_grads.astype(f32)
    feed_grads = feed_grads.astype(f32)
    return (
        result,
        tokens_grad,
        gains[0],
        branch_grads[:, :width],
        sums[0],
        branch_grads[:, width : 2 * width],
        sums[1],
        sums[2:6],
        sums[6],
        jnp.stack([small[:size, :size], small[:size, size : 2 * size]]),
        sums[7],
        jnp.stack([small[:size, 2 * size : 3 * size], small[:size, 3 * size : 4 * size]]),
        sums[8],
        sums[9],
        branch_grads[:, 2 * width :].T,
        gains[1],
        feed_grads[:, :hidden_width],
        feed_grads[:, hidden_width : 2 * hidden_width],
        feed_grads[:, 2 * hidden_width :].T,
    )


def solution(mesh):
    return jax.shard_map(
        on_device,
        mesh=mesh,
        in_specs=(
            P(("dp", "mp"), None),
            P("dp", None),
            P(),
            P(None, "mp"),
            P("mp"),
            P(None, "mp"),
            P("mp"),
            P(None, "mp"),
            P("mp"),
            P("mp", None, None),
            P("mp"),
            P("mp", None, None),
            P("mp"),
            P("mp"),
            P("mp", None),
            P(),
            P(None, "mp"),
            P(None, "mp"),
            P("mp", None),
            P(("dp", "mp"), None),
        ),
        out_specs=(
            P(("dp", "mp"), None),
            P(("dp", "mp"), None),
            P(),
            P("dp", "mp"),
            P("mp"),
            P("dp", "mp"),
            P("mp"),
            P(None, "mp"),
            P("mp"),
            P("mp", None, None),
            P("mp"),
            P("mp", None, None),
            P("mp"),
            P("mp"),
            P("mp", "dp"),
            P(),
            P("dp", "mp"),
            P("dp", "mp"),
            P("mp", "dp"),
        ),
        check_vma=False,
    )
```

```python
import jax
import jax.numpy as jnp
from jax import lax
from jax.experimental import pallas as pl
from jax.experimental.pallas import tpu as pltpu
from jax.sharding import PartitionSpec as P

EPSILON = 1e-06
DECAY_SCALE = 8.0
GELU_SCALE = 0.7978845608028654
GELU_CUBE = 0.044715
CHUNK = 64
PARTS = 8


def one_minus_exp(double_rate, exp_square):
    y = -double_rate
    series = 1.0 - y * (1.0 / 7.0)
    for order in (6.0, 5.0, 4.0, 3.0, 2.0):
        series = 1.0 - y * (1.0 / order) * series
    return jnp.where(y < 0.5, y * series, 1.0 - exp_square)


def gelu_parts(values):
    square = values * values
    slope = GELU_SCALE + (GELU_SCALE * GELU_CUBE) * square
    bend = jnp.tanh(values * slope)
    half = 0.5 + 0.5 * bend
    return half, bend, square


def recurrent_forward(
    offsets, pre, keep, params, gate_weight, gated, conv, rate, inflow, decay, root, state,
    padded, logits, decays, injects, products, ends,
):
    rows, width = conv.shape
    piece = rows // PARTS

    padded[0:8, :] = jnp.zeros((8, width), jnp.float32)
    for part in range(PARTS):
        place = pl.multiple_of(offsets[part] + 8, 8)
        padded[pl.ds(place, piece), :] = (
            pre[part * piece : (part + 1) * piece, width:] + params[1:2, :]
        )

    def conv_chunk(index, carry):
        base = pl.multiple_of(index * CHUNK, CHUNK)
        window = padded[pl.ds(base, CHUNK + 8), :]
        keeps = keep[pl.ds(base, CHUNK), :]
        total = params[2:3, :] + params[3:4, :] * window[8:, :]
        for steps in (1, 2, 3):
            shifted = window[8 - steps : 8 - steps + CHUNK, :]
            total = total + params[3 + steps : 4 + steps, :] * shifted * keeps[:, steps - 1 : steps]
        conv[pl.ds(base, CHUNK), :] = total.astype(jnp.bfloat16)
        return carry

    lax.fori_loop(0, rows // CHUNK, conv_chunk, 0)

    logits[...] = jnp.dot(conv[...], gate_weight[...], preferred_element_type=jnp.float32)

    def gate_chunk(index, carry):
        base = pl.multiple_of(index * CHUNK, CHUNK)
        here = pl.ds(base, CHUNK)
        kept = keep[here, 0:1]
        rate_sig = jax.nn.sigmoid(logits[here, :width] + params[7:8, :])
        inflow_sig = jax.nn.sigmoid(logits[here, width:] + params[8:9, :])
        log_rate = rate_sig * params[9:10, :]
        plain = jnp.exp(log_rate)
        hole = jnp.sqrt(one_minus_exp(2.0 * log_rate, plain * plain))
        factor = hole * kept + (1.0 - kept)
        rate[here, :] = rate_sig
        inflow[here, :] = inflow_sig
        decay[here, :] = plain
        root[here, :] = hole
        kept_decay = plain * kept
        inject = factor * inflow_sig * conv[here, :].astype(jnp.float32)
        for lane in range(width // 128):
            decays[lane, here, :] = kept_decay[:, lane * 128 : (lane + 1) * 128]
            injects[lane, here, :] = inject[:, lane * 128 : (lane + 1) * 128]
        return carry

    lax.fori_loop(0, rows // CHUNK, gate_chunk, 0)

    lanes = width // 128
    zero = jnp.zeros((PARTS, 128), jnp.float32)
    one = jnp.ones((PARTS, 128), jnp.float32)

    def scan_step(step, carry):
        result = []
        for lane in range(lanes):
            value, product = carry[lane]
            factor = decays[lane, pl.ds(step, PARTS, stride=piece), :]
            value = factor * value + injects[lane, pl.ds(step, PARTS, stride=piece), :]
            product = factor * product
            injects[lane, pl.ds(step, PARTS, stride=piece), :] = value
            products[lane, pl.ds(step, PARTS, stride=piece), :] = product
            result.append((value, product))
        return tuple(result)

    last = lax.fori_loop(0, piece, scan_step, ((zero, one),) * lanes, unroll=8)
    for lane in range(lanes):
        value, product = last[lane]
        entering = jnp.zeros((1, 128), jnp.float32)
        for part in range(PARTS):
            ends[part, 0:1, lane * 128 : (lane + 1) * 128] = entering
            entering = value[part : part + 1, :] + product[part : part + 1, :] * entering

    def finish_part(part, carry):
        start = pl.multiple_of(offsets[part], piece)
        segment = offsets[part] // piece
        for half in range(piece // CHUNK):
            there = pl.ds(pl.multiple_of(start + half * CHUNK, CHUNK), CHUNK)
            local = pl.ds(pl.multiple_of(part * piece + half * CHUNK, CHUNK), CHUNK)
            for lane in range(lanes):
                cols = slice(lane * 128, (lane + 1) * 128)
                whole = (
                    injects[lane, there, :]
                    + products[lane, there, :] * ends[segment, 0:1, cols]
                )
                state[there, cols] = whole
                values = pre[local, cols] + params[0:1, cols]
                act = values * gelu_parts(values)[0]
                gated[local, cols] = (act * whole).astype(jnp.bfloat16)
        return carry

    lax.fori_loop(0, PARTS, finish_part, 0)


def recurrent_backward(
    offsets, gated_grad, pre, keep, params, gate_weight, conv, rate, inflow, decay, root, state,
    branch_grad, gate_grad, sums,
    padded, carried, decays, products, ends, before, logit_grad, conv_grad, shifted_grad,
):
    rows, width = conv.shape
    piece = rows // PARTS
    lanes = width // 128
    zero_rows = jnp.zeros((8, width), jnp.float32)

    padded[0:8, :] = zero_rows
    before[0:8, :] = zero_rows
    for lane in range(lanes):
        decays[lane, rows : rows + 8, :] = jnp.zeros((8, 128), jnp.float32)
    shifted_grad[:, rows : rows + 8, :] = jnp.zeros((3, 8, width), jnp.float32)

    def enter_part(part, total):
        start = pl.multiple_of(offsets[part], piece)
        for half in range(piece // CHUNK):
            there = pl.ds(pl.multiple_of(start + half * CHUNK, CHUNK), CHUNK)
            ahead = pl.ds(pl.multiple_of(start + half * CHUNK + 8, 8), CHUNK)
            local = pl.ds(pl.multiple_of(part * piece + half * CHUNK, CHUNK), CHUNK)
            kept = keep[there, 0:1]
            padded[ahead, :] = pre[local, width:] + params[1:2, :]
            values = pre[local, :width] + params[0:1, :]
            upper, bend, square = gelu_parts(values)
            slope = upper + 0.5 * values * (1.0 - bend * bend) * (
                GELU_SCALE + (3.0 * GELU_SCALE * GELU_CUBE) * square
            )
            grad = gated_grad[local, :]
            here_state = state[there, :]
            before[ahead, :] = here_state
            gelu_grad = (grad * here_state * slope).astype(jnp.bfloat16)
            branch_grad[local, :width] = gelu_grad
            total = total + jnp.sum(
                gelu_grad.astype(jnp.float32).reshape(CHUNK // 8, 8, width), axis=0
            )
            state_grad = grad * values * upper
            kept_decay = decay[there, :] * kept
            for lane in range(lanes):
                cols = slice(lane * 128, (lane + 1) * 128)
                carried[lane, there, :] = state_grad[:, cols]
                decays[lane, there, :] = kept_decay[:, cols]
        return total

    gelu_sum = lax.fori_loop(0, PARTS, enter_part, zero_rows)

    zero = jnp.zeros((PARTS, 128), jnp.float32)
    one = jnp.ones((PARTS, 128), jnp.float32)

    def scan_step(count, carry):
        step = piece - 1 - count
        result = []
        for lane in range(lanes):
            value, product = carry[lane]
            factor = decays[lane, pl.ds(step + 1, PARTS, stride=piece), :]
            value = factor * value + carried[lane, pl.ds(step, PARTS, stride=piece), :]
            product = factor * product
            carried[lane, pl.ds(step, PARTS, stride=piece), :] = value
            products[lane, pl.ds(step, PARTS, stride=piece), :] = product
            result.append((value, product))
        return tuple(result)

    last = lax.fori_loop(0, piece, scan_step, ((zero, one),) * lanes, unroll=8)
    for lane in range(lanes):
        value, product = last[lane]
        entering = jnp.zeros((1, 128), jnp.float32)
        for part in range(PARTS - 1, -1, -1):
            ends[part, 0:1, lane * 128 : (lane + 1) * 128] = entering
            entering = value[part : part + 1, :] + product[part : part + 1, :] * entering

    def gate_chunk(index, totals):
        rate_sum, inflow_sum, decay_sum = totals
        base = pl.multiple_of(index * CHUNK, CHUNK)
        here = pl.ds(base, CHUNK)
        segment = base // piece
        kept = keep[here, 0:1]
        grad = jnp.concatenate(
            [
                carried[lane, here, :]
                + products[lane, here, :]
                * ends[segment, 0:1, lane * 128 : (lane + 1) * 128]
                for lane in range(lanes)
            ],
            axis=1,
        )
        earlier = before[pl.ds(base, CHUNK + 8), :][7 : 7 + CHUNK, :]
        plain = decay[here, :]
        hole = root[here, :]
        rate_sig = rate[here, :]
        inflow_sig = inflow[here, :]
        conv_vals = conv[here, :].astype(jnp.float32)
        factor = hole * kept + (1.0 - kept)
        scaled = grad * inflow_sig
        log_grad = (
            (grad * earlier * plain - scaled * conv_vals * (plain * plain) / hole) * kept
        )
        rate_low = (
            log_grad * params[9:10, :] * rate_sig * (1.0 - rate_sig)
        ).astype(jnp.bfloat16)
        elem = scaled * factor
        inflow_low = (elem * conv_vals * (1.0 - inflow_sig)).astype(jnp.bfloat16)
        logit_grad[here, :width] = rate_low
        logit_grad[here, width:] = inflow_low
        conv_grad[here, :] = elem

        def fold(values):
            return jnp.sum(values.reshape(CHUNK // 8, 8, width), axis=0)

        return (
            rate_sum + fold(rate_low.astype(jnp.float32)),
            inflow_sum + fold(inflow_low.astype(jnp.float32)),
            decay_sum + fold(log_grad * rate_sig),
        )

    rate_sum, inflow_sum, decay_sum = lax.fori_loop(
        0, rows // CHUNK, gate_chunk, (zero_rows, zero_rows, zero_rows)
    )

    conv_grad[...] += lax.dot_general(
        logit_grad[...],
        gate_weight[...],
        (((1,), (1,)), ((), ())),
        preferred_element_type=jnp.float32,
    )
    gate_grad[...] = lax.dot_general(
        conv[...],
        logit_grad[...],
        (((0,), (0,)), ((), ())),
        preferred_element_type=jnp.float32,
    )

    def tap_chunk(index, totals):
        base = pl.multiple_of(index * CHUNK, CHUNK)
        here = pl.ds(base, CHUNK)
        grad = conv_grad[here, :]
        keeps = keep[here, :]
        window = padded[pl.ds(base, CHUNK + 8), :]

        def fold(values):
            return jnp.sum(values.reshape(CHUNK // 8, 8, width), axis=0)

        result = [totals[0] + fold(grad), totals[1] + fold(grad * window[8:, :])]
        for steps in (1, 2, 3):
            kept_grad = grad * keeps[:, steps - 1 : steps]
            shifted_grad[steps - 1, here, :] = kept_grad
            result.append(
                totals[1 + steps] + fold(kept_grad * window[8 - steps : 8 - steps + CHUNK, :])
            )
        return tuple(result)

    taps = lax.fori_loop(0, rows // CHUNK, tap_chunk, (zero_rows,) * 5)

    def leave_part(part, total):
        start = pl.multiple_of(offsets[part], piece)
        for half in range(piece // CHUNK):
            base = pl.multiple_of(start + half * CHUNK, CHUNK)
            local = pl.ds(pl.multiple_of(part * piece + half * CHUNK, CHUNK), CHUNK)
            grad = params[3:4, :] * conv_grad[pl.ds(base, CHUNK), :]
            for steps in (1, 2, 3):
                window = shifted_grad[steps - 1, pl.ds(base, CHUNK + 8), :]
                grad = grad + params[3 + steps : 4 + steps, :] * window[steps : steps + CHUNK, :]
            low = grad.astype(jnp.bfloat16)
            branch_grad[local, width:] = low
            total = total + jnp.sum(low.astype(jnp.float32).reshape(CHUNK // 8, 8, width), axis=0)
        return total

    input_sum = lax.fori_loop(0, PARTS, leave_part, zero_rows)

    all_sums = (
        gelu_sum, input_sum, taps[1], taps[2], taps[3], taps[4], taps[0], rate_sum, inflow_sum,
    )
    for row, total in enumerate(all_sums):
        sums[row : row + 1, :] = jnp.sum(total, axis=0, keepdims=True)
    sums[9:10, :] = jnp.sum(decay_sum, axis=0, keepdims=True) * params[10:11, :]
    sums[10:16, :] = jnp.zeros((6, width), jnp.float32)


def dot_rows(left, right):
    return lax.dot_general(
        left, right, (((0,), (0,)), ((), ())), preferred_element_type=jnp.float32
    )


def column_grads(left, right, total):
    total[...] = dot_rows(left[...], right[...]).astype(jnp.bfloat16)


def more_column_grads(left, right, earlier_total, total):
    total[...] = dot_rows(left[...], right[...]).astype(jnp.bfloat16)


def branch_grads(normed, mixer, branch_grad, gated, weight, total, gain):
    wide = gated.shape[1]
    width = total.shape[1] // 3
    branch = dot_rows(normed[...], branch_grad[...])
    mix = dot_rows(mixer[...], gated[...])
    weighted = jnp.sum(branch * weight[...].astype(jnp.float32), axis=1, keepdims=True)
    gain[...] = jnp.broadcast_to(weighted, gain.shape)
    total[...] = jnp.concatenate(
        [branch[:, :width], branch[:, wide : wide + width], mix[:, :width]], axis=1
    ).astype(jnp.bfloat16)


VMEM_SPEC = pl.BlockSpec(memory_space=pltpu.VMEM)
SMEM_SPEC = pl.BlockSpec(memory_space=pltpu.SMEM)


def run_forward(offsets, pre, keep, params, gate_weight):
    rows, width = pre.shape[0], pre.shape[1] // 2
    lanes = width // 128
    f32, low = jnp.float32, jnp.bfloat16
    full = jax.ShapeDtypeStruct((rows, width), f32)
    half = jax.ShapeDtypeStruct((rows, width), low)
    return pl.pallas_call(
        recurrent_forward,
        out_shape=(half, half, full, full, full, full, full),
        in_specs=[SMEM_SPEC] + [VMEM_SPEC] * 4,
        out_specs=(VMEM_SPEC,) * 7,
        scratch_shapes=[
            pltpu.VMEM((rows + 8, width), f32),
            pltpu.VMEM((rows, 2 * width), f32),
            pltpu.VMEM((lanes, rows, 128), f32),
            pltpu.VMEM((lanes, rows, 128), f32),
            pltpu.VMEM((lanes, rows, 128), f32),
            pltpu.VMEM((PARTS, 8, width), f32),
        ],
        compiler_params=pltpu.CompilerParams(vmem_limit_bytes=40 * 1024 * 1024),
        cost_estimate=pl.CostEstimate(
            flops=2 * rows * width * 2 * width, bytes_accessed=20 * rows * width * 4,
            transcendentals=5 * rows * width,
        ),
    )(offsets, pre, keep, params, gate_weight)


def run_backward(offsets, gated_grad, pre, keep, params, gate_weight, kept):
    rows, width = pre.shape[0], pre.shape[1] // 2
    lanes = width // 128
    f32, low = jnp.float32, jnp.bfloat16
    return pl.pallas_call(
        recurrent_backward,
        out_shape=(
            jax.ShapeDtypeStruct((rows, 2 * width), low),
            jax.ShapeDtypeStruct((width, 2 * width), f32),
            jax.ShapeDtypeStruct((16, width), f32),
        ),
        in_specs=[SMEM_SPEC] + [VMEM_SPEC] * 11,
        out_specs=(VMEM_SPEC,) * 3,
        scratch_shapes=[
            pltpu.VMEM((rows + 8, width), f32),
            pltpu.VMEM((lanes, rows, 128), f32),
            pltpu.VMEM((lanes, rows + 8, 128), f32),
            pltpu.VMEM((lanes, rows, 128), f32),
            pltpu.VMEM((PARTS, 8, width), f32),
            pltpu.VMEM((rows + 8, width), f32),
            pltpu.VMEM((rows, 2 * width), low),
            pltpu.VMEM((rows, width), f32),
            pltpu.VMEM((3, rows + 8, width), f32),
        ],
        compiler_params=pltpu.CompilerParams(vmem_limit_bytes=48 * 1024 * 1024),
        cost_estimate=pl.CostEstimate(
            flops=8 * rows * width * 2 * width, bytes_accessed=30 * rows * width * 4,
            transcendentals=5 * rows * width,
        ),
    )(offsets, gated_grad, pre, keep, params, gate_weight, *kept)


MEGA = 1024 * 1024
TILE = 256


def column_spec(rows):
    return pl.BlockSpec((rows, TILE), lambda step: (0, step))


def row_spec(columns):
    return pl.BlockSpec((TILE, columns), lambda step: (step, 0))


def whole_spec(array):
    return pl.BlockSpec(array.shape, lambda step: (0, 0))


def run_gate_grads(second, both_grad, more):
    rows, model = second.shape
    width = both_grad.shape[1]
    return pl.pallas_call(
        column_grads,
        grid=(model // TILE,),
        out_shape=jax.ShapeDtypeStruct((model, width + more), jnp.bfloat16),
        in_specs=[column_spec(rows), whole_spec(both_grad)],
        out_specs=row_spec(width),
        compiler_params=pltpu.CompilerParams(vmem_limit_bytes=24 * MEGA),
        cost_estimate=pl.CostEstimate(
            flops=2 * rows * width * model, bytes_accessed=20 * MEGA, transcendentals=0
        ),
    )(second, both_grad)


def run_down_grads(cots, hidden, total):
    rows, model = cots.shape
    width = hidden.shape[1]
    place = total.shape[1] // width - 1
    return pl.pallas_call(
        more_column_grads,
        grid=(model // TILE,),
        out_shape=jax.ShapeDtypeStruct(total.shape, total.dtype),
        in_specs=[column_spec(rows), whole_spec(hidden), pl.BlockSpec(memory_space=pl.ANY)],
        out_specs=pl.BlockSpec((TILE, width), lambda step: (step, place)),
        input_output_aliases={2: 0},
        compiler_params=pltpu.CompilerParams(vmem_limit_bytes=24 * MEGA),
        cost_estimate=pl.CostEstimate(
            flops=2 * rows * width * model, bytes_accessed=10 * MEGA, transcendentals=0
        ),
    )(cots, hidden, total)


def run_branch_grads(normed, mixer, branch_grad, gated, weight, width):
    rows, model = normed.shape
    return pl.pallas_call(
        branch_grads,
        grid=(model // TILE,),
        out_shape=(
            jax.ShapeDtypeStruct((model, 3 * width), jnp.bfloat16),
            jax.ShapeDtypeStruct((model, 128), jnp.float32),
        ),
        in_specs=[column_spec(rows)] * 2
        + [whole_spec(branch_grad), whole_spec(gated), row_spec(weight.shape[1])],
        out_specs=(row_spec(3 * width), row_spec(128)),
        compiler_params=pltpu.CompilerParams(vmem_limit_bytes=24 * MEGA),
        cost_estimate=pl.CostEstimate(
            flops=6 * rows * width * model, bytes_accessed=20 * MEGA, transcendentals=0
        ),
    )(normed, mixer, branch_grad, gated, weight)


RING = 4
PIECES = ((0, 0), (0, 1), (-1, 0), (-1, 1), (1, 0), (1, 1), (2, 0), (2, 1))


def mp_shift(values, along, across):
    pairs = [
        (ring * 2 + side, ((ring + along) % RING) * 2 + (side + across) % 2)
        for ring in range(RING)
        for side in range(2)
    ]
    return lax.ppermute(values, "mp", pairs)


def swap_sum(values, axis, size, steps, low):
    for step in steps:
        if low:
            values = values.astype(jnp.bfloat16)
        other = lax.ppermute(values, axis, [(place, place ^ step) for place in range(size)])
        values = values.astype(jnp.float32) + other.astype(jnp.float32)
    return values


def gather_pieces(mine):
    across = mp_shift(mine, 0, 1)
    below = mp_shift(mine, 1, 0)
    above = mp_shift(mine, -1, 0)
    across, below, above = lax.optimization_barrier((across, below, above))
    below_across = mp_shift(across, 1, 0)
    above_across = mp_shift(across, -1, 0)
    far = mp_shift(below, 1, 0)
    far_across = mp_shift(above_across, -1, 0)
    return [mine, across, below, below_across, above, above_across, far, far_across]


def send_far(far, rows):
    one, two = far[:rows].astype(jnp.bfloat16), far[rows:].astype(jnp.bfloat16)
    return mp_shift(one, 1, 0), mp_shift(two, -1, 0)


def send_middle(middle, far_one, far_two, rows):
    low, f32 = jnp.bfloat16, jnp.float32
    middle, far_one, far_two = lax.optimization_barrier((middle, far_one, far_two))
    side_up = mp_shift(middle[3 * rows :].astype(low), 1, 0)
    joined_down = (middle[rows : 2 * rows].astype(f32) + far_two.astype(f32)).astype(low)
    joined_down = mp_shift(joined_down, -1, 0)
    joined_up = (middle[2 * rows : 3 * rows].astype(f32) + far_one.astype(f32)).astype(low)
    side_down = middle[:rows].astype(low)
    side_up, joined_down, joined_up, side_down = lax.optimization_barrier(
        (side_up, joined_down, joined_up, side_down)
    )
    return side_up, mp_shift(side_down, -1, 0), joined_down, mp_shift(joined_up, 1, 0)


def send_near(near, side_up, side_down, joined_down, joined_up, rows):
    f32 = jnp.float32
    other = near[rows:].astype(f32) + joined_down.astype(f32) + side_up.astype(f32)
    other = mp_shift(other.astype(jnp.bfloat16), 0, 1)
    return (
        near[:rows].astype(f32)
        + joined_up.astype(f32)
        + side_down.astype(f32)
        + other.astype(f32)
    )


def scatter_sum(make, rows):
    far_one, far_two = send_far(make(6, 8), rows)
    moved = send_middle(make(2, 6), far_one, far_two, rows)
    return send_near(make(0, 2), *moved, rows)


def rms_forward(values, gain):
    scale = lax.rsqrt(jnp.mean(values * values, axis=-1, keepdims=True) + EPSILON)
    return (values * scale * gain, scale)


def rms_backward(values, scale, gain, grad):
    scaled_grad = grad * gain
    inner = jnp.mean(scaled_grad * values, axis=-1, keepdims=True)
    return scale * scaled_grad - values * scale * scale * scale * inner


def gelu_tanh(values):
    return jax.nn.gelu(values, approximate=True)


def tie(values, anchor):
    return lax.optimization_barrier((values, anchor))[0]


def block_diagonal(weight, width):
    size = weight.shape[1]
    return jnp.concatenate(
        [
            jnp.pad(weight[0], ((0, 0), (0, width - size))),
            jnp.pad(weight[1], ((0, 0), (size, width - 2 * size))),
            jnp.zeros((width - 2 * size, width), weight.dtype),
        ],
        0,
    )


def on_device(
    tokens,
    seg_ids,
    first_gain,
    gelu_weight,
    gelu_bias,
    input_weight,
    input_bias,
    conv_weight,
    conv_bias,
    rate_weight,
    rate_bias,
    inflow_weight,
    inflow_bias,
    decay_param,
    mix_weight,
    second_gain,
    gate_weight,
    up_weight,
    down_weight,
    cotangent,
):
    f32, low = jnp.float32, jnp.bfloat16
    seg_row = seg_ids[0]
    rows = tokens.shape[0]
    model = tokens.shape[1]
    width = gelu_weight.shape[1]
    hidden_width = gate_weight.shape[1]
    size = rate_weight.shape[1]
    wide = -(-width // 128) * 128
    place = lax.axis_index("mp")
    ring, side = place // 2, place % 2
    offsets = jnp.stack(
        [
            (((ring + along + RING) % RING) * 2 + (side + across) % 2) * rows
            for along, across in PIECES
        ]
    ).astype(jnp.int32)

    def dot(left, right):
        return jnp.dot(left, right, preferred_element_type=f32)

    def dot_back(left, right):
        return lax.dot_general(left, right, (((1,), (1,)), ((), ())), preferred_element_type=f32)

    rows_in = tokens.astype(f32)
    first_scale_gain = first_gain.astype(f32)
    second_scale_gain = second_gain.astype(f32)
    cot_rows = cotangent.astype(f32)
    first_normed, first_scale = rms_forward(rows_in, first_scale_gain)
    normed_pieces = gather_pieces(first_normed.astype(low))

    keep_list = []
    for steps in (1, 2, 3):
        before = jnp.concatenate([jnp.full((steps,), -1, jnp.int32), seg_row[:-steps]])
        keep_list.append((before == seg_row).astype(f32))
    keep = jnp.stack(keep_list + [jnp.zeros_like(keep_list[0])] * 5, axis=1)
    decay_vals = jnp.pad(decay_param.astype(f32), (0, wide - width), constant_values=1.0)

    def row(values):
        return jnp.pad(values.astype(f32), (0, wide - width))

    params = jnp.stack(
        [row(gelu_bias), row(input_bias), row(conv_bias)]
        + [row(conv_weight[tap]) for tap in range(4)]
        + [
            row(rate_bias),
            row(inflow_bias),
            -DECAY_SCALE * jax.nn.softplus(-decay_vals),
            DECAY_SCALE * jax.nn.sigmoid(-decay_vals),
        ]
        + [jnp.zeros((wide,), f32)] * 5
    )
    lane_pad = ((0, 0), (0, wide - width))
    branch_weight = jnp.concatenate(
        [jnp.pad(gelu_weight, lane_pad), jnp.pad(input_weight, lane_pad)], 1
    )
    mix_wide = jnp.pad(mix_weight, ((0, wide - width), (0, 0)))
    gates_weight = jnp.concatenate(
        [block_diagonal(rate_weight, wide), block_diagonal(inflow_weight, wide)], 1
    )

    cot_across = mp_shift(tie(cotangent, normed_pieces[1]), 0, 1)
    normed_pieces, (cot_mine, cot_across) = lax.optimization_barrier(
        (normed_pieces, (cotangent, cot_across))
    )
    cot_below = mp_shift(cot_mine, 1, 0)
    cot_above = mp_shift(cot_mine, -1, 0)
    cot_below_across = mp_shift(cot_across, 1, 0)
    cot_above_across = mp_shift(cot_across, -1, 0)

    normed_full = jnp.concatenate(normed_pieces, 0)
    pre = dot(normed_full, branch_weight)
    gated, *kept = run_forward(offsets, pre, keep, params, gates_weight)
    cot_near = [cot_mine, cot_across, cot_below, cot_below_across, cot_above, cot_above_across]
    gated, cot_near = lax.optimization_barrier((gated, cot_near))

    mixed = scatter_sum(
        lambda start, stop: dot(gated[start * rows : stop * rows], mix_wide), rows
    )
    middle = rows_in + mixed
    second_normed, second_scale = rms_forward(middle, second_scale_gain)
    second_pieces = gather_pieces(second_normed.astype(low))
    second_pieces, (cot_far, cot_far_across) = lax.optimization_barrier(
        (second_pieces, (cot_near[2], cot_near[5]))
    )
    cot_far = mp_shift(cot_far, 1, 0)
    cot_far_across = mp_shift(cot_far_across, -1, 0)
    second_full = jnp.concatenate(second_pieces, 0)

    gate_pre = dot(second_full, gate_weight)
    up_pre = dot(second_full, up_weight)
    gate_act, gate_back = jax.vjp(gelu_tanh, gate_pre)
    hidden = (gate_act * up_pre).astype(low)
    hidden, cot_far, cot_far_across = lax.optimization_barrier((hidden, cot_far, cot_far_across))
    cot_turned = jnp.concatenate(cot_near + [cot_far, cot_far_across], 0)

    def down_part(start, stop):
        return dot(hidden[start * rows : stop * rows], down_weight).astype(low)

    down_far = send_far(down_part(6, 8), rows)
    hidden_grad = dot_back(cot_turned, down_weight)
    gate_grad = gate_back(hidden_grad * up_pre)[0].astype(low)
    up_grad = (hidden_grad * gate_act).astype(low)

    def second_back(start, stop):
        here = slice(start * rows, stop * rows)
        return dot_back(gate_grad[here], gate_weight) + dot_back(up_grad[here], up_weight)

    second_far = second_back(6, 8)
    second_far, down_far = lax.optimization_barrier((second_far, down_far))
    both_grad = jnp.concatenate([gate_grad, up_grad], 1)
    both_grad, second_far, second_middle = lax.optimization_barrier(
        (both_grad, second_far, second_back(2, 6))
    )
    second_far = send_far(second_far, rows)
    feed_sum = run_gate_grads(second_full, both_grad, hidden.shape[1])
    feed_sum = run_down_grads(cot_turned, hidden, feed_sum)
    second_middle, feed_sum = lax.optimization_barrier((second_middle, feed_sum))
    second_moved = send_middle(second_middle, *second_far, rows)
    second_near = second_back(0, 2)
    second_grad = send_near(second_near, *second_moved, rows)
    middle_grad = cot_rows + rms_backward(middle, second_scale, second_scale_gain, second_grad)
    second_gain_local = jnp.sum(second_grad * middle * second_scale, axis=0)
    mixer_low = middle_grad.astype(low)
    feed_sum = lax.psum_scatter(feed_sum, "dp", scatter_dimension=0, tiled=True)
    mixer_pieces = gather_pieces(mixer_low)
    mixer_pieces, down_far = lax.optimization_barrier((mixer_pieces, down_far))
    down_moved = send_middle(down_part(2, 6), *down_far, rows)
    mixer_full = jnp.concatenate(mixer_pieces, 0)

    gated_grad = dot_back(mixer_full, mix_wide)
    branch_grad, gates_grad, sums = run_backward(
        offsets, gated_grad, pre, keep, params, gates_weight, kept
    )
    branch_grad, down_moved = lax.optimization_barrier((branch_grad, down_moved))
    result = (middle + send_near(down_part(0, 2), *down_moved, rows)).astype(low)

    def first_back(start, stop):
        return dot_back(branch_grad[start * rows : stop * rows], branch_weight)

    branch_grad, first_far, first_middle = lax.optimization_barrier(
        (branch_grad, first_back(6, 8), first_back(2, 6))
    )
    branch_sum, gain_rows = run_branch_grads(
        normed_full, mixer_full, branch_grad, gated, branch_weight, width
    )
    first_far = send_far(first_far, rows)
    first_middle, branch_sum, gain_rows = lax.optimization_barrier(
        (first_middle, branch_sum, gain_rows)
    )
    first_moved = send_middle(first_middle, *first_far, rows)
    first_grad = send_near(first_back(0, 2), *first_moved, rows)
    tokens_grad = middle_grad + rms_backward(rows_in, first_scale, first_scale_gain, first_grad)

    first_gain_local = gain_rows[:, 0] / first_scale_gain
    branch_sum, feed_sum = lax.optimization_barrier((branch_sum, feed_sum))
    branch_sum = lax.psum_scatter(branch_sum, "dp", scatter_dimension=0, tiled=True)
    gates_grad, sums, first_gain_local = tie(
        (gates_grad, sums, first_gain_local), first_moved[2]
    )
    gate_blocks = jnp.concatenate(
        [
            gates_grad[:size, :size],
            gates_grad[size : 2 * size, size : 2 * size],
            gates_grad[:size, wide : wide + size],
            gates_grad[size : 2 * size, wide + size : wide + 2 * size],
        ],
        1,
    )
    small = jnp.concatenate(
        [gate_blocks, jnp.pad(sums[:, :width], ((0, 0), (0, 4 * size - width)))], 0
    )
    small = swap_sum(small, "dp", 16, (1, 2, 4, 8), True)
    gains = jnp.stack([first_gain_local, second_gain_local])
    gains = swap_sum(gains, "dp", 16, (1, 2, 4, 8), False)
    gains = swap_sum(gains, "mp", 8, (1, 2, 4), False)
    sums = small[size:, :width]
    branch_sum = branch_sum.astype(f32)
    feed_sum = feed_sum.astype(f32)
    return (
        result,
        tokens_grad,
        gains[0],
        branch_sum[:, :width],
        sums[0],
        branch_sum[:, width : 2 * width],
        sums[1],
        sums[2:6],
        sums[6],
        jnp.stack([small[:size, :size], small[:size, size : 2 * size]]),
        sums[7],
        jnp.stack([small[:size, 2 * size : 3 * size], small[:size, 3 * size : 4 * size]]),
        sums[8],
        sums[9],
        branch_sum[:, 2 * width :].T,
        gains[1],
        feed_sum[:, :hidden_width],
        feed_sum[:, hidden_width : 2 * hidden_width],
        feed_sum[:, 2 * hidden_width :].T,
    )


def solution(mesh):
    return jax.shard_map(
        on_device,
        mesh=mesh,
        in_specs=(
            P(("dp", "mp"), None),
            P("dp", None),
            P(),
            P(None, "mp"),
            P("mp"),
            P(None, "mp"),
            P("mp"),
            P(None, "mp"),
            P("mp"),
            P("mp", None, None),
            P("mp"),
            P("mp", None, None),
            P("mp"),
            P("mp"),
            P("mp", None),
            P(),
            P(None, "mp"),
            P(None, "mp"),
            P("mp", None),
            P(("dp", "mp"), None),
        ),
        out_specs=(
            P(("dp", "mp"), None),
            P(("dp", "mp"), None),
            P(),
            P("dp", "mp"),
            P("mp"),
            P("dp", "mp"),
            P("mp"),
            P(None, "mp"),
            P("mp"),
            P("mp", None, None),
            P("mp"),
            P("mp", None, None),
            P("mp"),
            P("mp"),
            P("mp", "dp"),
            P(),
            P("dp", "mp"),
            P("dp", "mp"),
            P("mp", "dp"),
        ),
        check_vma=False,
    )
```

```python
import jax
import jax.numpy as jnp
from jax import lax
from jax.experimental import pallas as pl
from jax.experimental.pallas import tpu as pltpu
from jax.sharding import PartitionSpec as P

EPSILON = 1e-06
DECAY_SCALE = 8.0
GELU_SCALE = 0.7978845608028654
GELU_CUBE = 0.044715
CHUNK = 64
PARTS = 8


def one_minus_exp(double_rate, exp_square):
    y = -double_rate
    series = 1.0 - y * (1.0 / 7.0)
    for order in (6.0, 5.0, 4.0, 3.0, 2.0):
        series = 1.0 - y * (1.0 / order) * series
    return jnp.where(y < 0.5, y * series, 1.0 - exp_square)


def gelu_parts(values):
    square = values * values
    slope = GELU_SCALE + (GELU_SCALE * GELU_CUBE) * square
    bend = jnp.tanh(values * slope)
    half = 0.5 + 0.5 * bend
    return half, bend, square


def recurrent_forward(
    offsets, pre_one, pre_two, pre_three, pre_four, keep, params, gate_weight,
    gated, conv, rate, inflow, decay, root, state,
    padded, logits, decays, injects, products, ends,
):
    rows, width = conv.shape
    piece = rows // PARTS
    pairs = (pre_one, pre_two, pre_three, pre_four)

    padded[0:8, :] = jnp.zeros((8, width), jnp.float32)
    for part in range(PARTS):
        place = pl.multiple_of(offsets[part] + 8, 8)
        half = slice(part % 2 * piece, (part % 2 + 1) * piece)
        padded[pl.ds(place, piece), :] = pairs[part // 2][half, width:] + params[1:2, :]

    def conv_chunk(index, carry):
        base = pl.multiple_of(index * CHUNK, CHUNK)
        window = padded[pl.ds(base, CHUNK + 8), :]
        keeps = keep[pl.ds(base, CHUNK), :]
        total = params[2:3, :] + params[3:4, :] * window[8:, :]
        for steps in (1, 2, 3):
            shifted = window[8 - steps : 8 - steps + CHUNK, :]
            total = total + params[3 + steps : 4 + steps, :] * shifted * keeps[:, steps - 1 : steps]
        conv[pl.ds(base, CHUNK), :] = total.astype(jnp.bfloat16)
        return carry

    lax.fori_loop(0, rows // CHUNK, conv_chunk, 0)

    logits[...] = jnp.dot(conv[...], gate_weight[...], preferred_element_type=jnp.float32)

    def gate_chunk(index, carry):
        base = pl.multiple_of(index * CHUNK, CHUNK)
        here = pl.ds(base, CHUNK)
        kept = keep[here, 0:1]
        rate_sig = jax.nn.sigmoid(logits[here, :width] + params[7:8, :])
        inflow_sig = jax.nn.sigmoid(logits[here, width:] + params[8:9, :])
        log_rate = rate_sig * params[9:10, :]
        plain = jnp.exp(log_rate)
        hole = jnp.sqrt(one_minus_exp(2.0 * log_rate, plain * plain))
        factor = hole * kept + (1.0 - kept)
        rate[here, :] = rate_sig
        inflow[here, :] = inflow_sig
        decay[here, :] = plain
        root[here, :] = hole
        kept_decay = plain * kept
        inject = factor * inflow_sig * conv[here, :].astype(jnp.float32)
        for lane in range(width // 128):
            decays[lane, here, :] = kept_decay[:, lane * 128 : (lane + 1) * 128]
            injects[lane, here, :] = inject[:, lane * 128 : (lane + 1) * 128]
        return carry

    lax.fori_loop(0, rows // CHUNK, gate_chunk, 0)

    lanes = width // 128
    zero = jnp.zeros((PARTS, 128), jnp.float32)
    one = jnp.ones((PARTS, 128), jnp.float32)

    def scan_step(step, carry):
        result = []
        for lane in range(lanes):
            value, product = carry[lane]
            factor = decays[lane, pl.ds(step, PARTS, stride=piece), :]
            value = factor * value + injects[lane, pl.ds(step, PARTS, stride=piece), :]
            product = factor * product
            injects[lane, pl.ds(step, PARTS, stride=piece), :] = value
            products[lane, pl.ds(step, PARTS, stride=piece), :] = product
            result.append((value, product))
        return tuple(result)

    last = lax.fori_loop(0, piece, scan_step, ((zero, one),) * lanes, unroll=8)
    for lane in range(lanes):
        value, product = last[lane]
        entering = jnp.zeros((1, 128), jnp.float32)
        for part in range(PARTS):
            ends[part, 0:1, lane * 128 : (lane + 1) * 128] = entering
            entering = value[part : part + 1, :] + product[part : part + 1, :] * entering

    for part in range(PARTS):
        start = pl.multiple_of(offsets[part], piece)
        segment = offsets[part] // piece
        pre = pairs[part // 2]

        def finish_chunk(index, carry, part=part, start=start, segment=segment, pre=pre):
            there = pl.ds(pl.multiple_of(start + index * CHUNK, CHUNK), CHUNK)
            near = pl.ds(pl.multiple_of(part % 2 * piece + index * CHUNK, CHUNK), CHUNK)
            local = pl.ds(pl.multiple_of(part * piece + index * CHUNK, CHUNK), CHUNK)
            for lane in range(lanes):
                cols = slice(lane * 128, (lane + 1) * 128)
                whole = (
                    injects[lane, there, :]
                    + products[lane, there, :] * ends[segment, 0:1, cols]
                )
                state[there, cols] = whole
                values = pre[near, cols] + params[0:1, cols]
                act = values * gelu_parts(values)[0]
                gated[local, cols] = (act * whole).astype(jnp.bfloat16)
            return carry

        lax.fori_loop(0, piece // CHUNK, finish_chunk, 0)


def recurrent_backward(
    offsets, grad_one, grad_two, grad_three, grad_four, pre_one, pre_two, pre_three, pre_four,
    keep, params, gate_weight, conv, rate, inflow, decay, root, state,
    branch_grad, gate_grad, sums,
    padded, carried, decays, products, ends, before, logit_grad, conv_grad, shifted_grad,
):
    rows, width = conv.shape
    piece = rows // PARTS
    lanes = width // 128
    grad_pairs = (grad_one, grad_two, grad_three, grad_four)
    pre_pairs = (pre_one, pre_two, pre_three, pre_four)
    zero_rows = jnp.zeros((8, width), jnp.float32)

    padded[0:8, :] = zero_rows
    before[0:8, :] = zero_rows
    for lane in range(lanes):
        decays[lane, rows : rows + 8, :] = jnp.zeros((8, 128), jnp.float32)
    shifted_grad[:, rows : rows + 8, :] = jnp.zeros((3, 8, width), jnp.float32)

    gelu_sum = zero_rows
    for part in range(PARTS):
        start = pl.multiple_of(offsets[part], piece)
        pre, gated_grad = pre_pairs[part // 2], grad_pairs[part // 2]

        def enter_chunk(index, total, part=part, start=start, pre=pre, gated_grad=gated_grad):
            there = pl.ds(pl.multiple_of(start + index * CHUNK, CHUNK), CHUNK)
            ahead = pl.ds(pl.multiple_of(start + index * CHUNK + 8, 8), CHUNK)
            near = pl.ds(pl.multiple_of(part % 2 * piece + index * CHUNK, CHUNK), CHUNK)
            local = pl.ds(pl.multiple_of(part * piece + index * CHUNK, CHUNK), CHUNK)
            kept = keep[there, 0:1]
            padded[ahead, :] = pre[near, width:] + params[1:2, :]
            values = pre[near, :width] + params[0:1, :]
            upper, bend, square = gelu_parts(values)
            slope = upper + 0.5 * values * (1.0 - bend * bend) * (
                GELU_SCALE + (3.0 * GELU_SCALE * GELU_CUBE) * square
            )
            grad = gated_grad[near, :]
            here_state = state[there, :]
            before[ahead, :] = here_state
            gelu_grad = (grad * here_state * slope).astype(jnp.bfloat16)
            branch_grad[local, :width] = gelu_grad
            state_grad = grad * values * upper
            kept_decay = decay[there, :] * kept
            for lane in range(lanes):
                cols = slice(lane * 128, (lane + 1) * 128)
                carried[lane, there, :] = state_grad[:, cols]
                decays[lane, there, :] = kept_decay[:, cols]
            return total + jnp.sum(
                gelu_grad.astype(jnp.float32).reshape(CHUNK // 8, 8, width), axis=0
            )

        gelu_sum = lax.fori_loop(0, piece // CHUNK, enter_chunk, gelu_sum)

    zero = jnp.zeros((PARTS, 128), jnp.float32)
    one = jnp.ones((PARTS, 128), jnp.float32)

    def scan_step(count, carry):
        step = piece - 1 - count
        result = []
        for lane in range(lanes):
            value, product = carry[lane]
            factor = decays[lane, pl.ds(step + 1, PARTS, stride=piece), :]
            value = factor * value + carried[lane, pl.ds(step, PARTS, stride=piece), :]
            product = factor * product
            carried[lane, pl.ds(step, PARTS, stride=piece), :] = value
            products[lane, pl.ds(step, PARTS, stride=piece), :] = product
            result.append((value, product))
        return tuple(result)

    last = lax.fori_loop(0, piece, scan_step, ((zero, one),) * lanes, unroll=8)
    for lane in range(lanes):
        value, product = last[lane]
        entering = jnp.zeros((1, 128), jnp.float32)
        for part in range(PARTS - 1, -1, -1):
            ends[part, 0:1, lane * 128 : (lane + 1) * 128] = entering
            entering = value[part : part + 1, :] + product[part : part + 1, :] * entering

    def gate_chunk(index, totals):
        rate_sum, inflow_sum, decay_sum = totals
        base = pl.multiple_of(index * CHUNK, CHUNK)
        here = pl.ds(base, CHUNK)
        segment = base // piece
        kept = keep[here, 0:1]
        grad = jnp.concatenate(
            [
                carried[lane, here, :]
                + products[lane, here, :]
                * ends[segment, 0:1, lane * 128 : (lane + 1) * 128]
                for lane in range(lanes)
            ],
            axis=1,
        )
        earlier = before[pl.ds(base, CHUNK + 8), :][7 : 7 + CHUNK, :]
        plain = decay[here, :]
        hole = root[here, :]
        rate_sig = rate[here, :]
        inflow_sig = inflow[here, :]
        conv_vals = conv[here, :].astype(jnp.float32)
        factor = hole * kept + (1.0 - kept)
        scaled = grad * inflow_sig
        log_grad = (
            (grad * earlier * plain - scaled * conv_vals * (plain * plain) / hole) * kept
        )
        rate_low = (
            log_grad * params[9:10, :] * rate_sig * (1.0 - rate_sig)
        ).astype(jnp.bfloat16)
        elem = scaled * factor
        inflow_low = (elem * conv_vals * (1.0 - inflow_sig)).astype(jnp.bfloat16)
        logit_grad[here, :width] = rate_low
        logit_grad[here, width:] = inflow_low
        conv_grad[here, :] = elem

        def fold(values):
            return jnp.sum(values.reshape(CHUNK // 8, 8, width), axis=0)

        return (
            rate_sum + fold(rate_low.astype(jnp.float32)),
            inflow_sum + fold(inflow_low.astype(jnp.float32)),
            decay_sum + fold(log_grad * rate_sig),
        )

    rate_sum, inflow_sum, decay_sum = lax.fori_loop(
        0, rows // CHUNK, gate_chunk, (zero_rows, zero_rows, zero_rows)
    )

    conv_grad[...] += lax.dot_general(
        logit_grad[...],
        gate_weight[...],
        (((1,), (1,)), ((), ())),
        preferred_element_type=jnp.float32,
    )
    gate_grad[...] = lax.dot_general(
        conv[...],
        logit_grad[...],
        (((0,), (0,)), ((), ())),
        preferred_element_type=jnp.float32,
    )

    def tap_chunk(index, totals):
        base = pl.multiple_of(index * CHUNK, CHUNK)
        here = pl.ds(base, CHUNK)
        grad = conv_grad[here, :]
        keeps = keep[here, :]
        window = padded[pl.ds(base, CHUNK + 8), :]

        def fold(values):
            return jnp.sum(values.reshape(CHUNK // 8, 8, width), axis=0)

        result = [totals[0] + fold(grad), totals[1] + fold(grad * window[8:, :])]
        for steps in (1, 2, 3):
            kept_grad = grad * keeps[:, steps - 1 : steps]
            shifted_grad[steps - 1, here, :] = kept_grad
            result.append(
                totals[1 + steps] + fold(kept_grad * window[8 - steps : 8 - steps + CHUNK, :])
            )
        return tuple(result)

    taps = lax.fori_loop(0, rows // CHUNK, tap_chunk, (zero_rows,) * 5)

    def leave_part(part, total):
        start = pl.multiple_of(offsets[part], piece)
        for half in range(piece // CHUNK):
            base = pl.multiple_of(start + half * CHUNK, CHUNK)
            local = pl.ds(pl.multiple_of(part * piece + half * CHUNK, CHUNK), CHUNK)
            grad = params[3:4, :] * conv_grad[pl.ds(base, CHUNK), :]
            for steps in (1, 2, 3):
                window = shifted_grad[steps - 1, pl.ds(base, CHUNK + 8), :]
                grad = grad + params[3 + steps : 4 + steps, :] * window[steps : steps + CHUNK, :]
            low = grad.astype(jnp.bfloat16)
            branch_grad[local, width:] = low
            total = total + jnp.sum(low.astype(jnp.float32).reshape(CHUNK // 8, 8, width), axis=0)
        return total

    input_sum = lax.fori_loop(0, PARTS, leave_part, zero_rows)

    all_sums = (
        gelu_sum, input_sum, taps[1], taps[2], taps[3], taps[4], taps[0], rate_sum, inflow_sum,
    )
    for row, total in enumerate(all_sums):
        sums[row : row + 1, :] = jnp.sum(total, axis=0, keepdims=True)
    sums[9:10, :] = jnp.sum(decay_sum, axis=0, keepdims=True) * params[10:11, :]
    sums[10:16, :] = jnp.zeros((6, width), jnp.float32)


def dot_rows(left, right):
    return lax.dot_general(
        left, right, (((0,), (0,)), ((), ())), preferred_element_type=jnp.float32
    )


def join_columns(pairs, joined):
    size = pairs[0].shape[0]
    for index, pair in enumerate(pairs):
        joined[index * size : (index + 1) * size, :] = pair[...]


def split_cores(total, out):
    size = out.shape[3]
    for core in range(2):
        out[0, core, 0, :, :] = total[core * size : (core + 1) * size, :].astype(out.dtype)


def column_grads(side, *refs):
    left, right = refs[:4], refs[4:8]
    out, left_rows, right_rows = refs[-3:]

    @pl.when(pl.program_id(0) == 0)
    def _():
        join_columns(right, right_rows)

    join_columns(left, left_rows)
    split_cores(dot_rows(left_rows[...], right_rows[...]), out)


def branch_grads(side, *refs):
    normed, mixer, refs = refs[:4], refs[4:8], refs[8:]
    branch_grad, gated, weight, out, gain, normed_rows, mixer_rows = refs
    wide = gated.shape[1]
    width = out.shape[4] // 3
    join_columns(normed, normed_rows)
    join_columns(mixer, mixer_rows)
    branch = dot_rows(normed_rows[...], branch_grad[...])
    mix = dot_rows(mixer_rows[...], gated[...])
    weighted = jnp.sum(branch * weight[...].astype(jnp.float32), axis=1, keepdims=True)
    gain[...] = jnp.broadcast_to(weighted, gain.shape)
    total = jnp.concatenate(
        [branch[:, :width], branch[:, wide : wide + width], mix[:, :width]], axis=1
    )
    split_cores(total, out)


VMEM_SPEC = pl.BlockSpec(memory_space=pltpu.VMEM)
SMEM_SPEC = pl.BlockSpec(memory_space=pltpu.SMEM)


MEGA = 1024 * 1024
TILE = 256


def run_forward(offsets, pre, keep, params, gate_weight):
    rows, width = 4 * pre[0].shape[0], pre[0].shape[1] // 2
    lanes = width // 128
    f32, low = jnp.float32, jnp.bfloat16
    full = jax.ShapeDtypeStruct((rows, width), f32)
    half = jax.ShapeDtypeStruct((rows, width), low)
    return pl.pallas_call(
        recurrent_forward,
        out_shape=(half, half, full, full, full, full, full),
        in_specs=[SMEM_SPEC] + [VMEM_SPEC] * 7,
        out_specs=(VMEM_SPEC,) * 7,
        scratch_shapes=[
            pltpu.VMEM((rows + 8, width), f32),
            pltpu.VMEM((rows, 2 * width), f32),
            pltpu.VMEM((lanes, rows, 128), f32),
            pltpu.VMEM((lanes, rows, 128), f32),
            pltpu.VMEM((lanes, rows, 128), f32),
            pltpu.VMEM((PARTS, 8, width), f32),
        ],
        compiler_params=pltpu.CompilerParams(vmem_limit_bytes=40 * MEGA),
    )(offsets, *pre, keep, params, gate_weight)


def run_backward(offsets, gated_grad, pre, keep, params, gate_weight, kept):
    rows, width = 4 * pre[0].shape[0], pre[0].shape[1] // 2
    lanes = width // 128
    f32, low = jnp.float32, jnp.bfloat16
    return pl.pallas_call(
        recurrent_backward,
        out_shape=(
            jax.ShapeDtypeStruct((rows, 2 * width), low),
            jax.ShapeDtypeStruct((width, 2 * width), f32),
            jax.ShapeDtypeStruct((16, width), f32),
        ),
        in_specs=[SMEM_SPEC] + [VMEM_SPEC] * 17,
        out_specs=(VMEM_SPEC,) * 3,
        scratch_shapes=[
            pltpu.VMEM((rows + 8, width), f32),
            pltpu.VMEM((lanes, rows, 128), f32),
            pltpu.VMEM((lanes, rows + 8, 128), f32),
            pltpu.VMEM((lanes, rows, 128), f32),
            pltpu.VMEM((PARTS, 8, width), f32),
            pltpu.VMEM((rows + 8, width), f32),
            pltpu.VMEM((rows, 2 * width), low),
            pltpu.VMEM((rows, width), f32),
            pltpu.VMEM((3, rows + 8, width), f32),
        ],
        compiler_params=pltpu.CompilerParams(vmem_limit_bytes=48 * MEGA),
    )(offsets, *gated_grad, *pre, keep, params, gate_weight, *kept)


def column_spec(rows):
    return pl.BlockSpec((rows, TILE), lambda step, side: (0, step))


def placed_spec(columns, column):
    return pl.BlockSpec(
        (1, 2, 1, TILE // 2, columns),
        lambda step, side: (step % 4, 0, (step // 4 + side[0]) % 2, 0, column),
    )


def placed_shape(model, columns):
    return jax.ShapeDtypeStruct((model // TILE // 2, 2, 2, TILE // 2, columns), jnp.bfloat16)


def whole_spec(array):
    return pl.BlockSpec(array.shape, lambda step, side: (0, 0))


def run_column_grads(side, left, right, columns, column, earlier=()):
    size, model = left[0].shape
    width = right[0].shape[1]
    return pl.pallas_call(
        column_grads,
        grid_spec=pltpu.PrefetchScalarGridSpec(
            num_scalar_prefetch=1,
            grid=(model // TILE,),
            in_specs=[column_spec(size)] * 4
            + [whole_spec(pair) for pair in right]
            + [pl.BlockSpec(memory_space=pl.ANY)] * len(earlier),
            out_specs=placed_spec(width, column),
            scratch_shapes=[
                pltpu.VMEM((4 * size, TILE), jnp.bfloat16),
                pltpu.VMEM((4 * size, width), jnp.bfloat16),
            ],
        ),
        out_shape=placed_shape(model, columns),
        input_output_aliases={9: 0} if earlier else {},
        compiler_params=pltpu.CompilerParams(vmem_limit_bytes=28 * MEGA),
    )(side, *left, *right, *earlier)


def run_branch_grads(side, normed, mixer, branch_grad, gated, weight, width):
    size, model = normed[0].shape
    return pl.pallas_call(
        branch_grads,
        grid_spec=pltpu.PrefetchScalarGridSpec(
            num_scalar_prefetch=1,
            grid=(model // TILE,),
            in_specs=[column_spec(size)] * 8
            + [whole_spec(branch_grad), whole_spec(gated)]
            + [pl.BlockSpec((TILE, weight.shape[1]), lambda step, side: (step, 0))],
            out_specs=(
                placed_spec(3 * width, 0),
                pl.BlockSpec((TILE, 128), lambda step, side: (step, 0)),
            ),
            scratch_shapes=[pltpu.VMEM((4 * size, TILE), jnp.bfloat16)] * 2,
        ),
        out_shape=(
            placed_shape(model, 3 * width),
            jax.ShapeDtypeStruct((model, 128), jnp.float32),
        ),
        compiler_params=pltpu.CompilerParams(vmem_limit_bytes=28 * MEGA),
    )(side, *normed, *mixer, branch_grad, gated, weight)


RING = 4
PIECES = ((0, 0), (0, 1), (-1, 0), (-1, 1), (1, 0), (1, 1), (2, 0), (2, 1))


def mp_shift(values, along, across):
    pairs = [
        (ring * 2 + side, ((ring + along) % RING) * 2 + (side + across) % 2)
        for ring in range(RING)
        for side in range(2)
    ]
    return lax.ppermute(values, "mp", pairs)


def dp_shift(values, across, along, core):
    pairs = [
        (
            (side * RING + ring) * 2 + own,
            (((side + across) % 2) * RING + (ring + along) % RING) * 2 + (own + core) % 2,
        )
        for side in range(2)
        for ring in range(RING)
        for own in range(2)
    ]
    return lax.ppermute(values, "dp", pairs)


def half_dp_scatter(values):
    groups = [list(range(side * 2 * RING, (side + 1) * 2 * RING)) for side in range(2)]
    return lax.psum_scatter(
        values.reshape(-1, values.shape[-1]),
        "dp",
        scatter_dimension=0,
        tiled=True,
        axis_index_groups=groups,
    )


def sides_sum(values):
    mine, other = halves(values)
    return mine.astype(jnp.float32) + dp_shift(other, 1, 0, 0).astype(jnp.float32)


def swap_sum(values, axis, size, steps, low):
    for step in steps:
        if low:
            values = values.astype(jnp.bfloat16)
        other = lax.ppermute(values, axis, [(place, place ^ step) for place in range(size)])
        values = values.astype(jnp.float32) + other.astype(jnp.float32)
    return values


def join(values):
    return [jnp.concatenate(values[at : at + 2], 0) for at in range(0, len(values), 2)]


def gather_pieces(mine):
    across = mp_shift(mine, 0, 1)
    below = mp_shift(mine, 1, 0)
    above = mp_shift(mine, -1, 0)
    across, below, above = lax.optimization_barrier((across, below, above))
    below_across = mp_shift(across, 1, 0)
    above_across = mp_shift(across, -1, 0)
    far = mp_shift(below, 1, 0)
    far_across = mp_shift(above_across, -1, 0)
    return [mine, across, below, below_across, above, above_across, far, far_across]


def halves(pair):
    rows = pair.shape[0] // 2
    return pair[:rows], pair[rows:]


def low_sum(*terms):
    total = terms[0].astype(jnp.float32)
    for term in terms[1:]:
        total = total + term.astype(jnp.float32)
    return total.astype(jnp.bfloat16)


def send_far(far):
    one, two = halves(far.astype(jnp.bfloat16))
    return mp_shift(one, 1, 0), mp_shift(two, -1, 0)


def send_middle(below, above, far_one, far_two, extra=None):
    below, above, far_one, far_two = lax.optimization_barrier((below, above, far_one, far_two))
    side_down, joined_down = halves(below)
    joined_up, side_up = halves(above)
    side_up = mp_shift(low_sum(side_up), 1, 0)
    joined_down = mp_shift(low_sum(joined_down, far_two), -1, 0)
    joined_up, side_down = low_sum(joined_up, far_one), low_sum(side_down)
    if extra is not None:
        extra = extra()
    side_up, joined_down, joined_up, side_down, extra = lax.optimization_barrier(
        (side_up, joined_down, joined_up, side_down, extra)
    )
    moved = side_up, mp_shift(side_down, -1, 0), joined_down, mp_shift(joined_up, 1, 0)
    return moved if extra is None else (moved, extra)


def send_near(near, side_up, side_down, joined_down, joined_up):
    f32 = jnp.float32
    mine, other = halves(near)
    other = mp_shift(low_sum(other, joined_down, side_up), 0, 1)
    return (
        mine.astype(f32)
        + joined_up.astype(f32)
        + side_down.astype(f32)
        + other.astype(f32)
    )


def rms_forward(values, gain):
    scale = lax.rsqrt(jnp.mean(values * values, axis=-1, keepdims=True) + EPSILON)
    return (values * scale * gain, scale)


def rms_backward(values, scale, gain, grad):
    scaled_grad = grad * gain
    inner = jnp.mean(scaled_grad * values, axis=-1, keepdims=True)
    return scale * scaled_grad - values * scale * scale * scale * inner


def gelu_tanh(values):
    return jax.nn.gelu(values, approximate=True)


def tie(values, anchor):
    return lax.optimization_barrier((values, anchor))[0]


def block_diagonal(weight, width):
    size = weight.shape[1]
    return jnp.concatenate(
        [
            jnp.pad(weight[0], ((0, 0), (0, width - size))),
            jnp.pad(weight[1], ((0, 0), (size, width - 2 * size))),
            jnp.zeros((width - 2 * size, width), weight.dtype),
        ],
        0,
    )


def on_device(
    tokens,
    seg_ids,
    first_gain,
    gelu_weight,
    gelu_bias,
    input_weight,
    input_bias,
    conv_weight,
    conv_bias,
    rate_weight,
    rate_bias,
    inflow_weight,
    inflow_bias,
    decay_param,
    mix_weight,
    second_gain,
    gate_weight,
    up_weight,
    down_weight,
    cotangent,
):
    f32, low = jnp.float32, jnp.bfloat16
    seg_row = seg_ids[0]
    rows = tokens.shape[0]
    model = tokens.shape[1]
    width = gelu_weight.shape[1]
    hidden_width = gate_weight.shape[1]
    size = rate_weight.shape[1]
    wide = -(-width // 128) * 128
    place = lax.axis_index("mp")
    ring, side = place // 2, place % 2
    offsets = jnp.stack(
        [
            (((ring + along + RING) % RING) * 2 + (side + across) % 2) * rows
            for along, across in PIECES
        ]
    ).astype(jnp.int32)

    def dot(left, right):
        return jnp.dot(left, right, preferred_element_type=f32)

    def dot_back(left, right):
        return lax.dot_general(left, right, (((1,), (1,)), ((), ())), preferred_element_type=f32)

    dp_side = (lax.axis_index("dp") // (2 * RING)).astype(jnp.int32).reshape(1)

    rows_in = tokens.astype(f32)
    first_scale_gain = first_gain.astype(f32)
    second_scale_gain = second_gain.astype(f32)
    cot_rows = cotangent.astype(f32)
    first_normed, first_scale = rms_forward(rows_in, first_scale_gain)
    normed_pieces = gather_pieces(first_normed.astype(low))

    keep_list = []
    for steps in (1, 2, 3):
        before = jnp.concatenate([jnp.full((steps,), -1, jnp.int32), seg_row[:-steps]])
        keep_list.append((before == seg_row).astype(f32))
    keep = jnp.stack(keep_list + [jnp.zeros_like(keep_list[0])] * 5, axis=1)
    decay_vals = jnp.pad(decay_param.astype(f32), (0, wide - width), constant_values=1.0)

    def row(values):
        return jnp.pad(values.astype(f32), (0, wide - width))

    params = jnp.stack(
        [row(gelu_bias), row(input_bias), row(conv_bias)]
        + [row(conv_weight[tap]) for tap in range(4)]
        + [
            row(rate_bias),
            row(inflow_bias),
            -DECAY_SCALE * jax.nn.softplus(-decay_vals),
            DECAY_SCALE * jax.nn.sigmoid(-decay_vals),
        ]
        + [jnp.zeros((wide,), f32)] * 5
    )
    lane_pad = ((0, 0), (0, wide - width))
    branch_weight = jnp.concatenate(
        [jnp.pad(gelu_weight, lane_pad), jnp.pad(input_weight, lane_pad)], 1
    )
    mix_wide = jnp.pad(mix_weight, ((0, wide - width), (0, 0)))
    gates_weight = jnp.concatenate(
        [block_diagonal(rate_weight, wide), block_diagonal(inflow_weight, wide)], 1
    )

    normed = join(normed_pieces)
    cot_across = mp_shift(tie(cotangent, normed_pieces[1]), 0, 1)
    cot_mine, cot_across = tie((cotangent, cot_across), normed_pieces[6:])
    cot_below = mp_shift(cot_mine, 1, 0)
    cot_above = mp_shift(cot_mine, -1, 0)
    cot_below_across = mp_shift(cot_across, 1, 0)
    cot_above_across = mp_shift(cot_across, -1, 0)

    pre = [dot(pair, branch_weight) for pair in normed]
    gated, *kept = run_forward(offsets, pre, keep, params, gates_weight)
    cots = [cot_mine, cot_across, cot_below, cot_below_across, cot_above, cot_above_across]
    gated, cots = lax.optimization_barrier((gated, cots))

    def pair_rows(values, pair):
        return values[2 * pair * rows : 2 * (pair + 1) * rows]

    mixed = [dot(pair_rows(gated, pair), mix_wide) for pair in range(4)]
    mixed = send_near(mixed[0], *send_middle(mixed[1], mixed[2], *send_far(mixed[3])))
    middle = rows_in + mixed
    second_normed, second_scale = rms_forward(middle, second_scale_gain)
    second_pieces = gather_pieces(second_normed.astype(low))
    second = join(second_pieces)
    cot_far, cot_far_across = tie((cots[2], cots[5]), second_pieces[6:])
    cots = join(cots + [mp_shift(cot_far, 1, 0), mp_shift(cot_far_across, -1, 0)])

    hiddens, both_grads, second_grads = [], [], []
    for pair in range(4):
        gate_pre = dot(second[pair], gate_weight)
        up_pre = dot(second[pair], up_weight)
        gate_act, gate_back = jax.vjp(gelu_tanh, gate_pre)
        hiddens.append((gate_act * up_pre).astype(low))
        hidden_grad = dot_back(cots[pair], down_weight)
        gate_grad = gate_back(hidden_grad * up_pre)[0].astype(low)
        up_grad = (hidden_grad * gate_act).astype(low)
        both_grads.append(jnp.concatenate([gate_grad, up_grad], 1))
        second_grads.append(dot_back(gate_grad, gate_weight) + dot_back(up_grad, up_weight))

    both_grads, second_grads = lax.optimization_barrier((both_grads, second_grads))
    second_far = send_far(second_grads[3])
    columns = 3 * hidden_width
    feed_sum = run_column_grads(dp_side, second, both_grads, columns, 0)
    feed_sum = run_column_grads(dp_side, cots, hiddens, columns, 2, [feed_sum])
    second_grads, feed_sum = lax.optimization_barrier((second_grads, feed_sum))
    second_grad = send_near(
        second_grads[0], *send_middle(second_grads[1], second_grads[2], *second_far)
    )
    feed_sum = half_dp_scatter(feed_sum)
    middle_grad = cot_rows + rms_backward(middle, second_scale, second_scale_gain, second_grad)
    second_gain_local = jnp.sum(second_grad * middle * second_scale, axis=0)
    mixer_pieces = gather_pieces(middle_grad.astype(low))
    mixer = join(mixer_pieces)
    downs = [dot(hidden, down_weight).astype(low) for hidden in hiddens]
    downs = tie(downs, mixer_pieces[6:])
    down_far = send_far(downs[3])
    down_up = mp_shift(halves(downs[2])[1], 1, 0)
    down_down = mp_shift(halves(downs[1])[0], -1, 0)

    mixer, feed_sum = lax.optimization_barrier((mixer, feed_sum))
    gated_grad = [dot_back(pair, mix_wide) for pair in mixer]
    branch_grad, gates_grad, sums = run_backward(
        offsets, gated_grad, pre, keep, params, gates_weight, kept
    )
    branch_grad, down_far, down_up, down_down = lax.optimization_barrier(
        (branch_grad, down_far, down_up, down_down)
    )
    joined_down = mp_shift(low_sum(halves(downs[1])[1], down_far[1]), -1, 0)
    joined_up = mp_shift(low_sum(halves(downs[2])[0], down_far[0]), 1, 0)
    result = (
        middle + send_near(downs[0], down_up, down_down, joined_down, joined_up)
    ).astype(low)

    first_grads = [dot_back(pair_rows(branch_grad, pair), branch_weight) for pair in range(4)]
    branch_grad, first_grads = lax.optimization_barrier((branch_grad, first_grads))
    branch_sum, gain_rows = run_branch_grads(
        dp_side, normed, mixer, branch_grad, gated, branch_weight, width
    )
    first_far = send_far(first_grads[3])
    first_grads, branch_sum, gain_rows = lax.optimization_barrier(
        (first_grads, branch_sum, gain_rows)
    )
    branch_sum = half_dp_scatter(branch_sum)
    first_moved = send_middle(first_grads[1], first_grads[2], *first_far)
    first_grad = send_near(first_grads[0], *first_moved)
    tokens_grad = middle_grad + rms_backward(rows_in, first_scale, first_scale_gain, first_grad)

    branch_sum = sides_sum(branch_sum)
    feed_sum = sides_sum(tie(feed_sum, branch_grad))

    gates_grad, sums, gain_rows = tie((gates_grad, sums, gain_rows), first_moved[2])
    gate_blocks = jnp.concatenate(
        [
            gates_grad[:size, :size],
            gates_grad[size : 2 * size, size : 2 * size],
            gates_grad[:size, wide : wide + size],
            gates_grad[size : 2 * size, wide + size : wide + 2 * size],
        ],
        1,
    )
    gains = jnp.stack([gain_rows[:, 0], second_gain_local]).reshape(8, model // 4)
    small = jnp.concatenate(
        [
            gate_blocks,
            jnp.pad(sums[:, :width], ((0, 0), (0, 4 * size - width))),
            jnp.pad(gains, ((0, 0), (0, 4 * size - model // 4))),
        ],
        0,
    )
    small = swap_sum(small, "dp", 16, (1, 2, 4, 8), True)
    gains = swap_sum(small[size + 16 :], "mp", 8, (1, 2, 4), False)
    gains = gains[:, : model // 4].reshape(2, model)
    sums = small[size : size + 16, :width]
    return (
        result,
        tokens_grad,
        gains[0] / first_scale_gain,
        branch_sum[:, :width],
        sums[0],
        branch_sum[:, width : 2 * width],
        sums[1],
        sums[2:6],
        sums[6],
        jnp.stack([small[:size, :size], small[:size, size : 2 * size]]),
        sums[7],
        jnp.stack([small[:size, 2 * size : 3 * size], small[:size, 3 * size : 4 * size]]),
        sums[8],
        sums[9],
        branch_sum[:, 2 * width :].T,
        gains[1],
        feed_sum[:, :hidden_width],
        feed_sum[:, hidden_width : 2 * hidden_width],
        feed_sum[:, 2 * hidden_width :].T,
    )


def solution(mesh):
    return jax.shard_map(
        on_device,
        mesh=mesh,
        in_specs=(
            P(("dp", "mp"), None),
            P("dp", None),
            P(),
            P(None, "mp"),
            P("mp"),
            P(None, "mp"),
            P("mp"),
            P(None, "mp"),
            P("mp"),
            P("mp", None, None),
            P("mp"),
            P("mp", None, None),
            P("mp"),
            P("mp"),
            P("mp", None),
            P(),
            P(None, "mp"),
            P(None, "mp"),
            P("mp", None),
            P(("dp", "mp"), None),
        ),
        out_specs=(
            P(("dp", "mp"), None),
            P(("dp", "mp"), None),
            P(),
            P("dp", "mp"),
            P("mp"),
            P("dp", "mp"),
            P("mp"),
            P(None, "mp"),
            P("mp"),
            P("mp", None, None),
            P("mp"),
            P("mp", None, None),
            P("mp"),
            P("mp"),
            P("mp", "dp"),
            P(),
            P("dp", "mp"),
            P("dp", "mp"),
            P("mp", "dp"),
        ),
        check_vma=False,
    )
```

```python
import jax
import jax.numpy as jnp
from jax import lax
from jax.experimental import pallas as pl
from jax.experimental.layout import Layout, with_layout_constraint
from jax.experimental.pallas import tpu as pltpu
from jax.sharding import PartitionSpec as P

EPSILON = 1e-06
DECAY_SCALE = 8.0
GELU_SCALE = 0.7978845608028654
GELU_CUBE = 0.044715
CHUNK = 64
PARTS = 8


def one_minus_exp(double_rate, exp_square):
    y = -double_rate
    series = 1.0 - y * (1.0 / 7.0)
    for order in (6.0, 5.0, 4.0, 3.0, 2.0):
        series = 1.0 - y * (1.0 / order) * series
    return jnp.where(y < 0.5, y * series, 1.0 - exp_square)


def gelu_parts(values):
    square = values * values
    slope = GELU_SCALE + (GELU_SCALE * GELU_CUBE) * square
    bend = jnp.tanh(values * slope)
    half = 0.5 + 0.5 * bend
    return half, bend, square


def recurrent_forward(
    offsets, pre_one, pre_two, pre_three, pre_four, keep, params, gate_weight,
    gated, conv, rate, inflow, decay, root, state,
    padded, logits, decays, injects, products, ends,
):
    rows, width = conv.shape
    piece = rows // PARTS
    pairs = (pre_one, pre_two, pre_three, pre_four)

    padded[0:8, :] = jnp.zeros((8, width), jnp.float32)
    for part in range(PARTS):
        place = pl.multiple_of(offsets[part] + 8, 8)
        half = slice(part % 2 * piece, (part % 2 + 1) * piece)
        padded[pl.ds(place, piece), :] = pairs[part // 2][half, width:] + params[1:2, :]

    def conv_chunk(index, carry):
        base = pl.multiple_of(index * CHUNK, CHUNK)
        window = padded[pl.ds(base, CHUNK + 8), :]
        keeps = keep[pl.ds(base, CHUNK), :]
        total = params[2:3, :] + params[3:4, :] * window[8:, :]
        for steps in (1, 2, 3):
            shifted = window[8 - steps : 8 - steps + CHUNK, :]
            total = total + params[3 + steps : 4 + steps, :] * shifted * keeps[:, steps - 1 : steps]
        conv[pl.ds(base, CHUNK), :] = total.astype(jnp.bfloat16)
        return carry

    lax.fori_loop(0, rows // CHUNK, conv_chunk, 0)

    logits[...] = jnp.dot(conv[...], gate_weight[...], preferred_element_type=jnp.float32)

    def gate_chunk(index, carry):
        base = pl.multiple_of(index * CHUNK, CHUNK)
        here = pl.ds(base, CHUNK)
        kept = keep[here, 0:1]
        rate_sig = jax.nn.sigmoid(logits[here, :width] + params[7:8, :])
        inflow_sig = jax.nn.sigmoid(logits[here, width:] + params[8:9, :])
        log_rate = rate_sig * params[9:10, :]
        plain = jnp.exp(log_rate)
        hole = jnp.sqrt(one_minus_exp(2.0 * log_rate, plain * plain))
        factor = hole * kept + (1.0 - kept)
        rate[here, :] = rate_sig
        inflow[here, :] = inflow_sig
        decay[here, :] = plain
        root[here, :] = hole
        kept_decay = plain * kept
        inject = factor * inflow_sig * conv[here, :].astype(jnp.float32)
        for lane in range(width // 128):
            decays[lane, here, :] = kept_decay[:, lane * 128 : (lane + 1) * 128]
            injects[lane, here, :] = inject[:, lane * 128 : (lane + 1) * 128]
        return carry

    lax.fori_loop(0, rows // CHUNK, gate_chunk, 0)

    lanes = width // 128
    zero = jnp.zeros((PARTS, 128), jnp.float32)
    one = jnp.ones((PARTS, 128), jnp.float32)

    def scan_step(step, carry):
        result = []
        for lane in range(lanes):
            value, product = carry[lane]
            factor = decays[lane, pl.ds(step, PARTS, stride=piece), :]
            value = factor * value + injects[lane, pl.ds(step, PARTS, stride=piece), :]
            product = factor * product
            injects[lane, pl.ds(step, PARTS, stride=piece), :] = value
            products[lane, pl.ds(step, PARTS, stride=piece), :] = product
            result.append((value, product))
        return tuple(result)

    last = lax.fori_loop(0, piece, scan_step, ((zero, one),) * lanes, unroll=8)
    for lane in range(lanes):
        value, product = last[lane]
        entering = jnp.zeros((1, 128), jnp.float32)
        for part in range(PARTS):
            ends[part, 0:1, lane * 128 : (lane + 1) * 128] = entering
            entering = value[part : part + 1, :] + product[part : part + 1, :] * entering

    for part in range(PARTS):
        start = pl.multiple_of(offsets[part], piece)
        segment = offsets[part] // piece
        pre = pairs[part // 2]

        def finish_chunk(index, carry, part=part, start=start, segment=segment, pre=pre):
            there = pl.ds(pl.multiple_of(start + index * CHUNK, CHUNK), CHUNK)
            near = pl.ds(pl.multiple_of(part % 2 * piece + index * CHUNK, CHUNK), CHUNK)
            local = pl.ds(pl.multiple_of(part * piece + index * CHUNK, CHUNK), CHUNK)
            for lane in range(lanes):
                cols = slice(lane * 128, (lane + 1) * 128)
                whole = (
                    injects[lane, there, :]
                    + products[lane, there, :] * ends[segment, 0:1, cols]
                )
                state[there, cols] = whole
                values = pre[near, cols] + params[0:1, cols]
                act = values * gelu_parts(values)[0]
                gated[local, cols] = (act * whole).astype(jnp.bfloat16)
            return carry

        lax.fori_loop(0, piece // CHUNK, finish_chunk, 0)


def recurrent_backward(
    offsets, grad_one, grad_two, grad_three, grad_four, pre_one, pre_two, pre_three, pre_four,
    keep, params, gate_weight, conv, rate, inflow, decay, root, state,
    branch_grad, gate_grad, sums,
    padded, carried, decays, products, ends, before, logit_grad, conv_grad, shifted_grad,
):
    rows, width = conv.shape
    piece = rows // PARTS
    lanes = width // 128
    grad_pairs = (grad_one, grad_two, grad_three, grad_four)
    pre_pairs = (pre_one, pre_two, pre_three, pre_four)
    zero_rows = jnp.zeros((8, width), jnp.float32)

    padded[0:8, :] = zero_rows
    before[0:8, :] = zero_rows
    for lane in range(lanes):
        decays[lane, rows : rows + 8, :] = jnp.zeros((8, 128), jnp.float32)
    shifted_grad[:, rows : rows + 8, :] = jnp.zeros((3, 8, width), jnp.float32)

    gelu_sum = zero_rows
    for part in range(PARTS):
        start = pl.multiple_of(offsets[part], piece)
        pre, gated_grad = pre_pairs[part // 2], grad_pairs[part // 2]

        def enter_chunk(index, total, part=part, start=start, pre=pre, gated_grad=gated_grad):
            there = pl.ds(pl.multiple_of(start + index * CHUNK, CHUNK), CHUNK)
            ahead = pl.ds(pl.multiple_of(start + index * CHUNK + 8, 8), CHUNK)
            near = pl.ds(pl.multiple_of(part % 2 * piece + index * CHUNK, CHUNK), CHUNK)
            local = pl.ds(pl.multiple_of(part * piece + index * CHUNK, CHUNK), CHUNK)
            kept = keep[there, 0:1]
            padded[ahead, :] = pre[near, width:] + params[1:2, :]
            values = pre[near, :width] + params[0:1, :]
            upper, bend, square = gelu_parts(values)
            slope = upper + 0.5 * values * (1.0 - bend * bend) * (
                GELU_SCALE + (3.0 * GELU_SCALE * GELU_CUBE) * square
            )
            grad = gated_grad[near, :]
            here_state = state[there, :]
            before[ahead, :] = here_state
            gelu_grad = (grad * here_state * slope).astype(jnp.bfloat16)
            branch_grad[local, :width] = gelu_grad
            state_grad = grad * values * upper
            kept_decay = decay[there, :] * kept
            for lane in range(lanes):
                cols = slice(lane * 128, (lane + 1) * 128)
                carried[lane, there, :] = state_grad[:, cols]
                decays[lane, there, :] = kept_decay[:, cols]
            return total + jnp.sum(
                gelu_grad.astype(jnp.float32).reshape(CHUNK // 8, 8, width), axis=0
            )

        gelu_sum = lax.fori_loop(0, piece // CHUNK, enter_chunk, gelu_sum)

    zero = jnp.zeros((PARTS, 128), jnp.float32)
    one = jnp.ones((PARTS, 128), jnp.float32)

    def scan_step(count, carry):
        step = piece - 1 - count
        result = []
        for lane in range(lanes):
            value, product = carry[lane]
            factor = decays[lane, pl.ds(step + 1, PARTS, stride=piece), :]
            value = factor * value + carried[lane, pl.ds(step, PARTS, stride=piece), :]
            product = factor * product
            carried[lane, pl.ds(step, PARTS, stride=piece), :] = value
            products[lane, pl.ds(step, PARTS, stride=piece), :] = product
            result.append((value, product))
        return tuple(result)

    last = lax.fori_loop(0, piece, scan_step, ((zero, one),) * lanes, unroll=8)
    for lane in range(lanes):
        value, product = last[lane]
        entering = jnp.zeros((1, 128), jnp.float32)
        for part in range(PARTS - 1, -1, -1):
            ends[part, 0:1, lane * 128 : (lane + 1) * 128] = entering
            entering = value[part : part + 1, :] + product[part : part + 1, :] * entering

    def gate_chunk(index, totals):
        rate_sum, inflow_sum, decay_sum = totals
        base = pl.multiple_of(index * CHUNK, CHUNK)
        here = pl.ds(base, CHUNK)
        segment = base // piece
        kept = keep[here, 0:1]
        grad = jnp.concatenate(
            [
                carried[lane, here, :]
                + products[lane, here, :]
                * ends[segment, 0:1, lane * 128 : (lane + 1) * 128]
                for lane in range(lanes)
            ],
            axis=1,
        )
        earlier = before[pl.ds(base, CHUNK + 8), :][7 : 7 + CHUNK, :]
        plain = decay[here, :]
        hole = root[here, :]
        rate_sig = rate[here, :]
        inflow_sig = inflow[here, :]
        conv_vals = conv[here, :].astype(jnp.float32)
        factor = hole * kept + (1.0 - kept)
        scaled = grad * inflow_sig
        log_grad = (
            (grad * earlier * plain - scaled * conv_vals * (plain * plain) / hole) * kept
        )
        rate_low = (
            log_grad * params[9:10, :] * rate_sig * (1.0 - rate_sig)
        ).astype(jnp.bfloat16)
        elem = scaled * factor
        inflow_low = (elem * conv_vals * (1.0 - inflow_sig)).astype(jnp.bfloat16)
        logit_grad[here, :width] = rate_low
        logit_grad[here, width:] = inflow_low
        conv_grad[here, :] = elem

        def fold(values):
            return jnp.sum(values.reshape(CHUNK // 8, 8, width), axis=0)

        return (
            rate_sum + fold(rate_low.astype(jnp.float32)),
            inflow_sum + fold(inflow_low.astype(jnp.float32)),
            decay_sum + fold(log_grad * rate_sig),
        )

    rate_sum, inflow_sum, decay_sum = lax.fori_loop(
        0, rows // CHUNK, gate_chunk, (zero_rows, zero_rows, zero_rows)
    )

    conv_grad[...] += lax.dot_general(
        logit_grad[...],
        gate_weight[...],
        (((1,), (1,)), ((), ())),
        preferred_element_type=jnp.float32,
    )
    gate_grad[...] = lax.dot_general(
        conv[...],
        logit_grad[...],
        (((0,), (0,)), ((), ())),
        preferred_element_type=jnp.float32,
    )

    def tap_chunk(index, totals):
        base = pl.multiple_of(index * CHUNK, CHUNK)
        here = pl.ds(base, CHUNK)
        grad = conv_grad[here, :]
        keeps = keep[here, :]
        window = padded[pl.ds(base, CHUNK + 8), :]

        def fold(values):
            return jnp.sum(values.reshape(CHUNK // 8, 8, width), axis=0)

        result = [totals[0] + fold(grad), totals[1] + fold(grad * window[8:, :])]
        for steps in (1, 2, 3):
            kept_grad = grad * keeps[:, steps - 1 : steps]
            shifted_grad[steps - 1, here, :] = kept_grad
            result.append(
                totals[1 + steps] + fold(kept_grad * window[8 - steps : 8 - steps + CHUNK, :])
            )
        return tuple(result)

    taps = lax.fori_loop(0, rows // CHUNK, tap_chunk, (zero_rows,) * 5)

    def leave_part(part, total):
        start = pl.multiple_of(offsets[part], piece)
        for half in range(piece // CHUNK):
            base = pl.multiple_of(start + half * CHUNK, CHUNK)
            local = pl.ds(pl.multiple_of(part * piece + half * CHUNK, CHUNK), CHUNK)
            grad = params[3:4, :] * conv_grad[pl.ds(base, CHUNK), :]
            for steps in (1, 2, 3):
                window = shifted_grad[steps - 1, pl.ds(base, CHUNK + 8), :]
                grad = grad + params[3 + steps : 4 + steps, :] * window[steps : steps + CHUNK, :]
            low = grad.astype(jnp.bfloat16)
            branch_grad[local, width:] = low
            total = total + jnp.sum(low.astype(jnp.float32).reshape(CHUNK // 8, 8, width), axis=0)
        return total

    input_sum = lax.fori_loop(0, PARTS, leave_part, zero_rows)

    all_sums = (
        gelu_sum, input_sum, taps[1], taps[2], taps[3], taps[4], taps[0], rate_sum, inflow_sum,
    )
    for row, total in enumerate(all_sums):
        sums[row : row + 1, :] = jnp.sum(total, axis=0, keepdims=True)
    sums[9:10, :] = jnp.sum(decay_sum, axis=0, keepdims=True) * params[10:11, :]
    sums[10:16, :] = jnp.zeros((6, width), jnp.float32)


def dot_rows(left, right):
    return lax.dot_general(
        left, right, (((0,), (0,)), ((), ())), preferred_element_type=jnp.float32
    )


def dot_back(left, right):
    return lax.dot_general(
        left, right, (((1,), (1,)), ((), ())), preferred_element_type=jnp.float32
    )


def dot_plain(left, right):
    return jnp.dot(left, right, preferred_element_type=jnp.float32)


def feed_pair(
    second, cots, gate_weight, up_weight, down_weight, hidden, gate_grad, up_grad, back, down,
    back_total, down_total,
):
    step = pl.program_id(0)
    gate = dot_plain(second[...], gate_weight[...])
    up = dot_plain(second[...], up_weight[...])
    upper, bend, square = gelu_parts(gate)
    act = gate * upper
    low = (act * up).astype(jnp.bfloat16)
    hidden[...] = low
    grad = dot_back(cots[...], down_weight[...])
    slope = upper + 0.5 * gate * (1.0 - bend * bend) * (
        GELU_SCALE + (3.0 * GELU_SCALE * GELU_CUBE) * square
    )
    gate_low = (grad * up * slope).astype(jnp.bfloat16)
    up_low = (grad * act).astype(jnp.bfloat16)
    gate_grad[...] = gate_low
    up_grad[...] = up_low
    back_part = dot_back(gate_low, gate_weight[...]) + dot_back(up_low, up_weight[...])
    down_part = dot_plain(low, down_weight[...])

    @pl.when(step == 0)
    def _():
        back_total[...] = back_part
        down_total[...] = down_part

    @pl.when(step > 0)
    def _():
        back_total[...] += back_part
        down_total[...] += down_part

    @pl.when(step == pl.num_programs(0) - 1)
    def _():
        back[...] = back_total[...].astype(jnp.bfloat16)
        down[...] = down_total[...].astype(jnp.bfloat16)


def join_columns(pairs, joined, column=0):
    size, width = pairs[0].shape
    for index, pair in enumerate(pairs):
        joined[index * size : (index + 1) * size, column : column + width] = pair[...]


def split_cores(total, out):
    size = out.shape[3]
    for core in range(2):
        out[0, core, 0, :, :] = total[core * size : (core + 1) * size, :].astype(out.dtype)


def column_grads(side, *refs):
    left, right = refs[:4], refs[4:-3]
    out, left_rows, right_rows = refs[-3:]
    width = right[0].shape[1]

    @pl.when(pl.program_id(0) == 0)
    def _():
        for group in range(right_rows.shape[1] // width):
            join_columns(right[4 * group : 4 * group + 4], right_rows, group * width)

    join_columns(left, left_rows)
    split_cores(dot_rows(left_rows[...], right_rows[...]), out)


def branch_grads(side, *refs):
    normed, mixer, refs = refs[:4], refs[4:8], refs[8:]
    branch_grad, gated, weight, out, gain, back, normed_rows, mixer_rows = refs
    wide = gated.shape[1]
    width = out.shape[4] // 3
    join_columns(normed, normed_rows)
    join_columns(mixer, mixer_rows)
    back[...] = dot_back(branch_grad[: back.shape[0], :], weight[...]).astype(back.dtype)
    branch = dot_rows(normed_rows[...], branch_grad[...])
    mix = dot_rows(mixer_rows[...], gated[...])
    weighted = jnp.sum(branch * weight[...].astype(jnp.float32), axis=1, keepdims=True)
    gain[...] = jnp.broadcast_to(weighted, gain.shape)
    total = jnp.concatenate(
        [branch[:, :width], branch[:, wide : wide + width], mix[:, :width]], axis=1
    )
    split_cores(total, out)


VMEM_SPEC = pl.BlockSpec(memory_space=pltpu.VMEM)
SMEM_SPEC = pl.BlockSpec(memory_space=pltpu.SMEM)


MEGA = 1024 * 1024
TILE = 256


def run_forward(offsets, pre, keep, params, gate_weight):
    rows, width = 4 * pre[0].shape[0], pre[0].shape[1] // 2
    lanes = width // 128
    f32, low = jnp.float32, jnp.bfloat16
    full = jax.ShapeDtypeStruct((rows, width), f32)
    half = jax.ShapeDtypeStruct((rows, width), low)
    return pl.pallas_call(
        recurrent_forward,
        out_shape=(half, half, full, full, full, full, full),
        in_specs=[SMEM_SPEC] + [VMEM_SPEC] * 7,
        out_specs=(VMEM_SPEC,) * 7,
        scratch_shapes=[
            pltpu.VMEM((rows + 8, width), f32),
            pltpu.VMEM((rows, 2 * width), f32),
            pltpu.VMEM((lanes, rows, 128), f32),
            pltpu.VMEM((lanes, rows, 128), f32),
            pltpu.VMEM((lanes, rows, 128), f32),
            pltpu.VMEM((PARTS, 8, width), f32),
        ],
        compiler_params=pltpu.CompilerParams(vmem_limit_bytes=40 * MEGA),
    )(offsets, *pre, keep, params, gate_weight)


def run_backward(offsets, gated_grad, pre, keep, params, gate_weight, kept):
    rows, width = 4 * pre[0].shape[0], pre[0].shape[1] // 2
    lanes = width // 128
    f32, low = jnp.float32, jnp.bfloat16
    return pl.pallas_call(
        recurrent_backward,
        out_shape=(
            jax.ShapeDtypeStruct((rows, 2 * width), low),
            jax.ShapeDtypeStruct((width, 2 * width), f32),
            jax.ShapeDtypeStruct((16, width), f32),
        ),
        in_specs=[SMEM_SPEC] + [VMEM_SPEC] * 17,
        out_specs=(VMEM_SPEC,) * 3,
        scratch_shapes=[
            pltpu.VMEM((rows + 8, width), f32),
            pltpu.VMEM((lanes, rows, 128), f32),
            pltpu.VMEM((lanes, rows + 8, 128), f32),
            pltpu.VMEM((lanes, rows, 128), f32),
            pltpu.VMEM((PARTS, 8, width), f32),
            pltpu.VMEM((rows + 8, width), f32),
            pltpu.VMEM((rows, 2 * width), low),
            pltpu.VMEM((rows, width), f32),
            pltpu.VMEM((3, rows + 8, width), f32),
        ],
        compiler_params=pltpu.CompilerParams(vmem_limit_bytes=48 * MEGA),
    )(offsets, *gated_grad, *pre, keep, params, gate_weight, *kept)


def column_spec(rows):
    return pl.BlockSpec((rows, TILE), lambda step, side: (0, step))


def placed_spec(columns, column):
    return pl.BlockSpec(
        (1, 2, 1, TILE // 2, columns),
        lambda step, side: (step % 4, 0, (step // 4 + side[0]) % 2, 0, column),
    )


def placed_shape(model, columns):
    return pltpu.HBM((model // TILE // 2, 2, 2, TILE // 2, columns), jnp.bfloat16)


def whole_spec(array):
    return pl.BlockSpec(array.shape, lambda step, side: (0, 0))


def run_feed_pair(second, cots, gate_weight, up_weight, down_weight):
    size, model = second.shape
    width = gate_weight.shape[1]
    whole = pl.BlockSpec((size, model), lambda step: (0, 0))
    across = pl.BlockSpec((model, TILE), lambda step: (0, step))
    slim = pl.BlockSpec((size, TILE), lambda step: (0, step))
    narrow = jax.ShapeDtypeStruct((size, width), jnp.bfloat16)
    long = jax.ShapeDtypeStruct((size, model), jnp.bfloat16)
    return pl.pallas_call(
        feed_pair,
        grid=(width // TILE,),
        in_specs=[
            whole, whole, across, across, pl.BlockSpec((TILE, model), lambda step: (step, 0))
        ],
        out_specs=(slim, slim, slim, whole, whole),
        out_shape=(narrow, narrow, narrow, long, long),
        scratch_shapes=[pltpu.VMEM((size, model), jnp.float32)] * 2,
        compiler_params=pltpu.CompilerParams(vmem_limit_bytes=28 * MEGA),
    )(second, cots, gate_weight, up_weight, down_weight)


def run_column_grads(side, left, right, columns, column, earlier=()):
    size, model = left[0].shape
    width = len(right) // 4 * right[0].shape[1]
    return pl.pallas_call(
        column_grads,
        grid_spec=pltpu.PrefetchScalarGridSpec(
            num_scalar_prefetch=1,
            grid=(model // TILE,),
            in_specs=[column_spec(size)] * 4
            + [whole_spec(pair) for pair in right]
            + [pl.BlockSpec(memory_space=pl.ANY)] * len(earlier),
            out_specs=placed_spec(width, column),
            scratch_shapes=[
                pltpu.VMEM((4 * size, TILE), jnp.bfloat16),
                pltpu.VMEM((4 * size, width), jnp.bfloat16),
            ],
        ),
        out_shape=placed_shape(model, columns),
        input_output_aliases={5 + len(right): 0} if earlier else {},
        compiler_params=pltpu.CompilerParams(vmem_limit_bytes=28 * MEGA),
    )(side, *left, *right, *earlier)


def run_branch_grads(side, normed, mixer, branch_grad, gated, weight, width):
    size, model = normed[0].shape
    return pl.pallas_call(
        branch_grads,
        grid_spec=pltpu.PrefetchScalarGridSpec(
            num_scalar_prefetch=1,
            grid=(model // TILE,),
            in_specs=[column_spec(size)] * 8
            + [whole_spec(branch_grad), whole_spec(gated)]
            + [pl.BlockSpec((TILE, weight.shape[1]), lambda step, side: (step, 0))],
            out_specs=(
                placed_spec(3 * width, 0),
                pl.BlockSpec((TILE, 128), lambda step, side: (step, 0)),
                column_spec(3 * size),
            ),
            scratch_shapes=[pltpu.VMEM((4 * size, TILE), jnp.bfloat16)] * 2,
        ),
        out_shape=(
            placed_shape(model, 3 * width),
            pltpu.HBM((model, 128), jnp.float32),
            jax.ShapeDtypeStruct((3 * size, model), jnp.bfloat16),
        ),
        compiler_params=pltpu.CompilerParams(vmem_limit_bytes=28 * MEGA),
    )(side, *normed, *mixer, branch_grad, gated, weight)


RING = 4
PIECES = ((0, 0), (0, 1), (-1, 0), (-1, 1), (1, 0), (1, 1), (2, 0), (2, 1))


def mp_shift(values, along, across):
    pairs = [
        (ring * 2 + side, ((ring + along) % RING) * 2 + (side + across) % 2)
        for ring in range(RING)
        for side in range(2)
    ]
    return lax.ppermute(values, "mp", pairs)


def dp_shift(values, across, along, core):
    pairs = [
        (
            (side * RING + ring) * 2 + own,
            (((side + across) % 2) * RING + (ring + along) % RING) * 2 + (own + core) % 2,
        )
        for side in range(2)
        for ring in range(RING)
        for own in range(2)
    ]
    return lax.ppermute(values, "dp", pairs)


def half_dp_scatter(values):
    groups = [list(range(side * 2 * RING, (side + 1) * 2 * RING)) for side in range(2)]
    values = with_layout_constraint(values.reshape(-1, values.shape[-1]), Layout((0, 1)))
    total = lax.psum_scatter(
        values, "dp", scatter_dimension=0, tiled=True, axis_index_groups=groups
    )
    return with_layout_constraint(total, Layout((0, 1)))


def sides_sum(values):
    mine, other = halves(values)
    return mine.astype(jnp.float32) + dp_shift(other, 1, 0, 0).astype(jnp.float32)


def pair_sum(values, shift, low):
    values = values.astype(jnp.bfloat16) if low else values
    return values.astype(jnp.float32) + shift(values).astype(jnp.float32)


def ring_sum(values, shift, low):
    values = values.astype(jnp.bfloat16) if low else values
    one, two, three = [shift(values, along).astype(jnp.float32) for along in (1, 2, 3)]
    return (values.astype(jnp.float32) + two) + (one + three)


def core_sum(values, low):
    return pair_sum(values, lambda part: dp_shift(part, 0, 0, 1), low)


def row_sum(values, low, step):
    def swap(part):
        return lax.ppermute(part, "dp", [(place, place ^ step) for place in range(4 * RING)])

    return pair_sum(values, swap, low)


def side_sum(values, low):
    return pair_sum(values, lambda part: dp_shift(part, 1, 0, 0), low)


def join(values):
    return [jnp.concatenate(values[at : at + 2], 0) for at in range(0, len(values), 2)]


def gather_pieces(mine, second_work=None, third_work=None):
    across = mp_shift(mine, 0, 1)
    below = mp_shift(mine, 1, 0)
    above = mp_shift(mine, -1, 0)
    across, below, above = lax.optimization_barrier((across, below, above))
    below_across = mp_shift(across, 1, 0)
    above_across = mp_shift(across, -1, 0)
    done = second_work([mine, across]) if second_work else ()
    below_across, above_across, near_below, second_done = lax.optimization_barrier(
        (below_across, above_across, below, done)
    )
    far = mp_shift(near_below, 1, 0)
    far_across = mp_shift(above_across, -1, 0)
    done = third_work([below, below_across]) if third_work else ()
    far, far_across, third_done = lax.optimization_barrier((far, far_across, done))
    pieces = [mine, across, below, below_across, above, above_across, far, far_across]
    if second_work or third_work:
        return pieces, second_done, third_done
    return pieces


def halves(pair):
    rows = pair.shape[0] // 2
    return pair[:rows], pair[rows:]


def low_sum(*terms):
    total = terms[0].astype(jnp.float32)
    for term in terms[1:]:
        total = total + term.astype(jnp.float32)
    return total.astype(jnp.bfloat16)


def send_far(far):
    one, two = halves(far.astype(jnp.bfloat16))
    return mp_shift(one, 1, 0), mp_shift(two, -1, 0)


def send_middle(below, above, far_one, far_two, work=None):
    below, above, far_one, far_two = lax.optimization_barrier((below, above, far_one, far_two))
    side_down, joined_down = halves(below)
    joined_up, side_up = halves(above)
    side_up = mp_shift(low_sum(side_up), 1, 0)
    joined_down = mp_shift(low_sum(joined_down, far_two), -1, 0)
    joined_up, side_down = low_sum(joined_up, far_one), low_sum(side_down)
    done = work(joined_up) if work else ()
    side_up, joined_down, joined_up, side_down, done = lax.optimization_barrier(
        (side_up, joined_down, joined_up, side_down, done)
    )
    moved = side_up, mp_shift(side_down, -1, 0), joined_down, mp_shift(joined_up, 1, 0)
    return (moved, done) if work else moved


def send_near(near, side_up, side_down, joined_down, joined_up, work=None):
    f32 = jnp.float32
    mine, other = halves(near)
    other = mp_shift(low_sum(other, joined_down, side_up), 0, 1)
    done = work() if work else ()
    other, side_down, joined_up, done = lax.optimization_barrier(
        (other, side_down, joined_up, done)
    )
    total = (
        mine.astype(f32)
        + joined_up.astype(f32)
        + side_down.astype(f32)
        + other.astype(f32)
    )
    return (total, done) if work else total


def rms_forward(values, gain):
    scale = lax.rsqrt(jnp.mean(values * values, axis=-1, keepdims=True) + EPSILON)
    return (values * scale * gain, scale)


def rms_backward(values, scale, gain, grad):
    scaled_grad = grad * gain
    inner = jnp.mean(scaled_grad * values, axis=-1, keepdims=True)
    return scale * scaled_grad - values * scale * scale * scale * inner


def gelu_tanh(values):
    return jax.nn.gelu(values, approximate=True)


def tie(values, anchor):
    return lax.optimization_barrier((values, anchor))[0]


def block_diagonal(weight, width):
    size = weight.shape[1]
    return jnp.concatenate(
        [
            jnp.pad(weight[0], ((0, 0), (0, width - size))),
            jnp.pad(weight[1], ((0, 0), (size, width - 2 * size))),
            jnp.zeros((width - 2 * size, width), weight.dtype),
        ],
        0,
    )


def on_device(
    tokens,
    seg_ids,
    first_gain,
    gelu_weight,
    gelu_bias,
    input_weight,
    input_bias,
    conv_weight,
    conv_bias,
    rate_weight,
    rate_bias,
    inflow_weight,
    inflow_bias,
    decay_param,
    mix_weight,
    second_gain,
    gate_weight,
    up_weight,
    down_weight,
    cotangent,
):
    f32, low = jnp.float32, jnp.bfloat16
    seg_row = seg_ids[0]
    rows = tokens.shape[0]
    model = tokens.shape[1]
    width = gelu_weight.shape[1]
    hidden_width = gate_weight.shape[1]
    size = rate_weight.shape[1]
    wide = -(-width // 128) * 128
    place = lax.axis_index("mp")
    ring, side = place // 2, place % 2
    offsets = jnp.stack(
        [
            (((ring + along + RING) % RING) * 2 + (side + across) % 2) * rows
            for along, across in PIECES
        ]
    ).astype(jnp.int32)

    def dot(left, right):
        return jnp.dot(left, right, preferred_element_type=f32)

    def dot_back(left, right):
        return lax.dot_general(left, right, (((1,), (1,)), ((), ())), preferred_element_type=f32)

    dp_side = (lax.axis_index("dp") // (2 * RING)).astype(jnp.int32).reshape(1)

    rows_in = tokens.astype(f32)
    first_scale_gain = first_gain.astype(f32)
    second_scale_gain = second_gain.astype(f32)
    cot_rows = cotangent.astype(f32)
    first_normed, first_scale = rms_forward(rows_in, first_scale_gain)
    normed_pieces = gather_pieces(first_normed.astype(low))

    keep_list = []
    for steps in (1, 2, 3):
        before = jnp.concatenate([jnp.full((steps,), -1, jnp.int32), seg_row[:-steps]])
        keep_list.append((before == seg_row).astype(f32))
    keep = jnp.stack(keep_list + [jnp.zeros_like(keep_list[0])] * 5, axis=1)
    decay_vals = jnp.pad(decay_param.astype(f32), (0, wide - width), constant_values=1.0)

    def row(values):
        return jnp.pad(values.astype(f32), (0, wide - width))

    params = jnp.stack(
        [row(gelu_bias), row(input_bias), row(conv_bias)]
        + [row(conv_weight[tap]) for tap in range(4)]
        + [
            row(rate_bias),
            row(inflow_bias),
            -DECAY_SCALE * jax.nn.softplus(-decay_vals),
            DECAY_SCALE * jax.nn.sigmoid(-decay_vals),
        ]
        + [jnp.zeros((wide,), f32)] * 5
    )
    lane_pad = ((0, 0), (0, wide - width))
    branch_weight = jnp.concatenate(
        [jnp.pad(gelu_weight, lane_pad), jnp.pad(input_weight, lane_pad)], 1
    )
    mix_wide = jnp.pad(mix_weight, ((0, wide - width), (0, 0)))
    gates_weight = jnp.concatenate(
        [block_diagonal(rate_weight, wide), block_diagonal(inflow_weight, wide)], 1
    )

    normed = join(normed_pieces)
    cot_across = mp_shift(tie(cotangent, normed_pieces[1]), 0, 1)
    cot_mine, cot_across = tie((cotangent, cot_across), normed_pieces[6:])
    cots = [
        cot_mine,
        cot_across,
        mp_shift(cot_mine, 1, 0),
        mp_shift(cot_across, 1, 0),
        mp_shift(cot_mine, -1, 0),
        mp_shift(cot_across, -1, 0),
    ]

    pre = [dot(pair, branch_weight) for pair in normed]
    gated, *kept = run_forward(offsets, pre, keep, params, gates_weight)
    gated, cots = lax.optimization_barrier((gated, cots))

    def pair_rows(values, pair):
        return values[2 * pair * rows : 2 * (pair + 1) * rows]

    mixed = [dot(pair_rows(gated, pair), mix_wide) for pair in range(4)]
    mixed_far = send_far(mixed[3])
    cot_far, cot_far_across = tie((cots[2], cots[5]), mixed_far)
    cot_far = [mp_shift(cot_far, 1, 0), mp_shift(cot_far_across, -1, 0)]
    mixed = send_near(mixed[0], *send_middle(mixed[1], mixed[2], *mixed_far))
    middle = rows_in + mixed
    second_normed, second_scale = rms_forward(middle, second_scale_gain)
    second_low, cot_far = lax.optimization_barrier((second_normed.astype(low), cot_far))
    cots = join(cots + cot_far)

    def feed(pair, pieces):
        return run_feed_pair(
            jnp.concatenate(pieces, 0), cots[pair], gate_weight, up_weight, down_weight
        )

    second_pieces, feed_zero, feed_one = gather_pieces(
        second_low, lambda pieces: feed(0, pieces), lambda pieces: feed(1, pieces)
    )
    feed_three = feed(3, second_pieces[6:])
    second_above, second_last = lax.optimization_barrier((second_pieces[4:6], feed_three[3]))
    second_far = send_far(second_last)
    feed_two = feed(2, second_above)
    feed_two, second_far = lax.optimization_barrier((feed_two, second_far))
    feeds = zip(feed_zero, feed_one, feed_two, feed_three)
    hiddens, gate_grads, up_grads, second_grads, downs = [list(values) for values in feeds]
    second = join(second_pieces)
    columns = 3 * hidden_width
    second_moved, feed_sum = send_middle(
        second_grads[1],
        second_grads[2],
        *second_far,
        lambda _: run_column_grads(dp_side, second, gate_grads + up_grads, columns, 0),
    )
    second_grad, feed_sum = send_near(
        second_grads[0],
        *second_moved,
        lambda: run_column_grads(dp_side, cots, hiddens, columns, 2, [feed_sum]),
    )
    feed_sum = half_dp_scatter(feed_sum)
    middle_grad = cot_rows + rms_backward(middle, second_scale, second_scale_gain, second_grad)
    second_gain_local = jnp.sum(second_grad * middle * second_scale, axis=0)
    mixer_pieces = gather_pieces(middle_grad.astype(low))
    mixer = join(mixer_pieces)
    downs = tie(downs, mixer_pieces[6:])
    down_up = mp_shift(jnp.concatenate([halves(downs[3])[0], halves(downs[2])[1]], 0), 1, 0)
    down_down = mp_shift(jnp.concatenate([halves(downs[3])[1], halves(downs[1])[0]], 0), -1, 0)

    gated_grad = [dot_back(pair, mix_wide) for pair in mixer]
    branch_grad, gates_grad, sums = run_backward(
        offsets, gated_grad, pre, keep, params, gates_weight, kept
    )
    branch_grad, down_up, down_down, feed_sum = lax.optimization_barrier(
        (branch_grad, down_up, down_down, feed_sum)
    )
    far_one, down_up = halves(down_up)
    far_two, down_down = halves(down_down)
    gate_blocks = jnp.concatenate(
        [
            gates_grad[:size, :size],
            gates_grad[size : 2 * size, size : 2 * size],
            gates_grad[:size, wide : wide + size],
            gates_grad[size : 2 * size, wide + size : wide + 2 * size],
        ],
        1,
    )
    small = jnp.concatenate(
        [gate_blocks, jnp.pad(sums[:, :width], ((0, 0), (0, 4 * size - width)))], 0
    )

    branch_grad, first_far, far_one, far_two = lax.optimization_barrier(
        (branch_grad, dot_back(pair_rows(branch_grad, 3), branch_weight), far_one, far_two)
    )
    first_far = send_far(first_far)
    joined = (
        mp_shift(low_sum(halves(downs[1])[1], far_two), -1, 0),
        mp_shift(low_sum(halves(downs[2])[0], far_one), 1, 0),
    )
    branch_parts = run_branch_grads(
        dp_side, normed, mixer, branch_grad, gated, branch_weight, width
    )
    feed_sum = sides_sum(tie(feed_sum, branch_grad))
    branch_parts, first_far, joined, feed_sum = lax.optimization_barrier(
        (branch_parts, first_far, joined, feed_sum)
    )
    branch_sum, gain_rows, first_grads = branch_parts
    branch_sum = half_dp_scatter(branch_sum)
    gains = jnp.stack([gain_rows[:, 0], second_gain_local])
    first_moved, (small, gains) = send_middle(
        pair_rows(first_grads, 1),
        pair_rows(first_grads, 2),
        *first_far,
        lambda ready: (core_sum(tie(small, ready), True), core_sum(tie(gains, ready), False)),
    )
    first_grad, (small, gains) = send_near(
        pair_rows(first_grads, 0),
        *first_moved,
        lambda: (row_sum(small, True, 2), row_sum(gains, False, 2)),
    )
    tokens_grad = middle_grad + rms_backward(rows_in, first_scale, first_scale_gain, first_grad)
    small = side_sum(row_sum(small, True, 4), True)
    gains = side_sum(row_sum(gains, False, 4), False)
    gains = pair_sum(gains, lambda part: mp_shift(part, 0, 1), False)
    gains, branch_sum = lax.optimization_barrier((gains, branch_sum))
    gains = ring_sum(gains, lambda part, along: mp_shift(part, along, 0), False)
    joined = tie(joined, first_moved[0])
    result = (middle + send_near(downs[0], down_up, down_down, *joined)).astype(low)

    branch_sum = sides_sum(branch_sum)

    sums = small[size : size + 16, :width]
    return (
        result,
        tokens_grad,
        gains[0] / first_scale_gain,
        branch_sum[:, :width],
        sums[0],
        branch_sum[:, width : 2 * width],
        sums[1],
        sums[2:6],
        sums[6],
        jnp.stack([small[:size, :size], small[:size, size : 2 * size]]),
        sums[7],
        jnp.stack([small[:size, 2 * size : 3 * size], small[:size, 3 * size : 4 * size]]),
        sums[8],
        sums[9],
        branch_sum[:, 2 * width :].T,
        gains[1],
        feed_sum[:, :hidden_width],
        feed_sum[:, hidden_width : 2 * hidden_width],
        feed_sum[:, 2 * hidden_width :].T,
    )


def solution(mesh):
    return jax.shard_map(
        on_device,
        mesh=mesh,
        in_specs=(
            P(("dp", "mp"), None),
            P("dp", None),
            P(),
            P(None, "mp"),
            P("mp"),
            P(None, "mp"),
            P("mp"),
            P(None, "mp"),
            P("mp"),
            P("mp", None, None),
            P("mp"),
            P("mp", None, None),
            P("mp"),
            P("mp"),
            P("mp", None),
            P(),
            P(None, "mp"),
            P(None, "mp"),
            P("mp", None),
            P(("dp", "mp"), None),
        ),
        out_specs=(
            P(("dp", "mp"), None),
            P(("dp", "mp"), None),
            P(),
            P("dp", "mp"),
            P("mp"),
            P("dp", "mp"),
            P("mp"),
            P(None, "mp"),
            P("mp"),
            P("mp", None, None),
            P("mp"),
            P("mp", None, None),
            P("mp"),
            P("mp"),
            P("mp", "dp"),
            P(),
            P("dp", "mp"),
            P("dp", "mp"),
            P("mp", "dp"),
        ),
        check_vma=False,
    )
```

```python
import jax
import jax.numpy as jnp
from jax import lax
from jax.experimental import pallas as pl
from jax.experimental.layout import Layout, with_layout_constraint
from jax.experimental.pallas import tpu as pltpu
from jax.sharding import PartitionSpec as P

EPSILON = 1e-06
DECAY_SCALE = 8.0
GELU_SCALE = 0.7978845608028654
GELU_CUBE = 0.044715
CHUNK = 64
PARTS = 8


def one_minus_exp(double_rate, exp_square):
    y = -double_rate
    series = 1.0 - y * (1.0 / 7.0)
    for order in (6.0, 5.0, 4.0, 3.0, 2.0):
        series = 1.0 - y * (1.0 / order) * series
    return jnp.where(y < 0.5, y * series, 1.0 - exp_square)


def gelu_parts(values):
    square = values * values
    slope = GELU_SCALE + (GELU_SCALE * GELU_CUBE) * square
    bend = jnp.tanh(values * slope)
    half = 0.5 + 0.5 * bend
    return half, bend, square


def recurrent_forward(
    offsets, pre_one, pre_two, pre_three, pre_four, keep, params, gate_weight,
    gated, conv, rate, inflow, decay, root, state,
    padded, logits, decays, injects, products, ends,
):
    rows, width = conv.shape
    piece = rows // PARTS
    pairs = (pre_one, pre_two, pre_three, pre_four)

    padded[0:8, :] = jnp.zeros((8, width), jnp.float32)
    for part in range(PARTS):
        place = pl.multiple_of(offsets[part] + 8, 8)
        half = slice(part % 2 * piece, (part % 2 + 1) * piece)
        padded[pl.ds(place, piece), :] = pairs[part // 2][half, width:] + params[1:2, :]

    def conv_chunk(index, carry):
        base = pl.multiple_of(index * CHUNK, CHUNK)
        window = padded[pl.ds(base, CHUNK + 8), :]
        keeps = keep[pl.ds(base, CHUNK), :]
        total = params[2:3, :] + params[3:4, :] * window[8:, :]
        for steps in (1, 2, 3):
            shifted = window[8 - steps : 8 - steps + CHUNK, :]
            total = total + params[3 + steps : 4 + steps, :] * shifted * keeps[:, steps - 1 : steps]
        conv[pl.ds(base, CHUNK), :] = total.astype(jnp.bfloat16)
        return carry

    lax.fori_loop(0, rows // CHUNK, conv_chunk, 0)

    logits[...] = jnp.dot(conv[...], gate_weight[...], preferred_element_type=jnp.float32)

    def gate_chunk(index, carry):
        base = pl.multiple_of(index * CHUNK, CHUNK)
        here = pl.ds(base, CHUNK)
        kept = keep[here, 0:1]
        rate_sig = jax.nn.sigmoid(logits[here, :width] + params[7:8, :])
        inflow_sig = jax.nn.sigmoid(logits[here, width:] + params[8:9, :])
        log_rate = rate_sig * params[9:10, :]
        plain = jnp.exp(log_rate)
        hole = jnp.sqrt(one_minus_exp(2.0 * log_rate, plain * plain))
        factor = hole * kept + (1.0 - kept)
        rate[here, :] = rate_sig
        inflow[here, :] = inflow_sig
        decay[here, :] = plain
        root[here, :] = hole
        kept_decay = plain * kept
        inject = factor * inflow_sig * conv[here, :].astype(jnp.float32)
        for lane in range(width // 128):
            decays[lane, here, :] = kept_decay[:, lane * 128 : (lane + 1) * 128]
            injects[lane, here, :] = inject[:, lane * 128 : (lane + 1) * 128]
        return carry

    lax.fori_loop(0, rows // CHUNK, gate_chunk, 0)

    lanes = width // 128
    zero = jnp.zeros((PARTS, 128), jnp.float32)
    one = jnp.ones((PARTS, 128), jnp.float32)

    def scan_step(step, carry):
        result = []
        for lane in range(lanes):
            value, product = carry[lane]
            factor = decays[lane, pl.ds(step, PARTS, stride=piece), :]
            value = factor * value + injects[lane, pl.ds(step, PARTS, stride=piece), :]
            product = factor * product
            injects[lane, pl.ds(step, PARTS, stride=piece), :] = value
            products[lane, pl.ds(step, PARTS, stride=piece), :] = product
            result.append((value, product))
        return tuple(result)

    last = lax.fori_loop(0, piece, scan_step, ((zero, one),) * lanes, unroll=8)
    for lane in range(lanes):
        value, product = last[lane]
        entering = jnp.zeros((1, 128), jnp.float32)
        for part in range(PARTS):
            ends[part, 0:1, lane * 128 : (lane + 1) * 128] = entering
            entering = value[part : part + 1, :] + product[part : part + 1, :] * entering

    for part in range(PARTS):
        start = pl.multiple_of(offsets[part], piece)
        segment = offsets[part] // piece
        pre = pairs[part // 2]

        def finish_chunk(index, carry, part=part, start=start, segment=segment, pre=pre):
            there = pl.ds(pl.multiple_of(start + index * CHUNK, CHUNK), CHUNK)
            near = pl.ds(pl.multiple_of(part % 2 * piece + index * CHUNK, CHUNK), CHUNK)
            local = pl.ds(pl.multiple_of(part * piece + index * CHUNK, CHUNK), CHUNK)
            for lane in range(lanes):
                cols = slice(lane * 128, (lane + 1) * 128)
                whole = (
                    injects[lane, there, :]
                    + products[lane, there, :] * ends[segment, 0:1, cols]
                )
                state[there, cols] = whole
                values = pre[near, cols] + params[0:1, cols]
                act = values * gelu_parts(values)[0]
                gated[local, cols] = (act * whole).astype(jnp.bfloat16)
            return carry

        lax.fori_loop(0, piece // CHUNK, finish_chunk, 0)


def recurrent_backward(
    offsets, grad_one, grad_two, grad_three, grad_four, pre_one, pre_two, pre_three, pre_four,
    keep, params, gate_weight, conv, rate, inflow, decay, root, state,
    branch_grad, gate_grad, sums,
    padded, carried, decays, products, ends, before, logit_grad, conv_grad, shifted_grad,
):
    rows, width = conv.shape
    piece = rows // PARTS
    lanes = width // 128
    grad_pairs = (grad_one, grad_two, grad_three, grad_four)
    pre_pairs = (pre_one, pre_two, pre_three, pre_four)
    zero_rows = jnp.zeros((8, width), jnp.float32)

    padded[0:8, :] = zero_rows
    before[0:8, :] = zero_rows
    for lane in range(lanes):
        decays[lane, rows : rows + 8, :] = jnp.zeros((8, 128), jnp.float32)
    shifted_grad[:, rows : rows + 8, :] = jnp.zeros((3, 8, width), jnp.float32)

    gelu_sum = zero_rows
    for part in range(PARTS):
        start = pl.multiple_of(offsets[part], piece)
        pre, gated_grad = pre_pairs[part // 2], grad_pairs[part // 2]

        def enter_chunk(index, total, part=part, start=start, pre=pre, gated_grad=gated_grad):
            there = pl.ds(pl.multiple_of(start + index * CHUNK, CHUNK), CHUNK)
            ahead = pl.ds(pl.multiple_of(start + index * CHUNK + 8, 8), CHUNK)
            near = pl.ds(pl.multiple_of(part % 2 * piece + index * CHUNK, CHUNK), CHUNK)
            local = pl.ds(pl.multiple_of(part * piece + index * CHUNK, CHUNK), CHUNK)
            kept = keep[there, 0:1]
            padded[ahead, :] = pre[near, width:] + params[1:2, :]
            values = pre[near, :width] + params[0:1, :]
            upper, bend, square = gelu_parts(values)
            slope = upper + 0.5 * values * (1.0 - bend * bend) * (
                GELU_SCALE + (3.0 * GELU_SCALE * GELU_CUBE) * square
            )
            grad = gated_grad[near, :]
            here_state = state[there, :]
            before[ahead, :] = here_state
            gelu_grad = (grad * here_state * slope).astype(jnp.bfloat16)
            branch_grad[local, :width] = gelu_grad
            state_grad = grad * values * upper
            kept_decay = decay[there, :] * kept
            for lane in range(lanes):
                cols = slice(lane * 128, (lane + 1) * 128)
                carried[lane, there, :] = state_grad[:, cols]
                decays[lane, there, :] = kept_decay[:, cols]
            return total + jnp.sum(
                gelu_grad.astype(jnp.float32).reshape(CHUNK // 8, 8, width), axis=0
            )

        gelu_sum = lax.fori_loop(0, piece // CHUNK, enter_chunk, gelu_sum)

    zero = jnp.zeros((PARTS, 128), jnp.float32)
    one = jnp.ones((PARTS, 128), jnp.float32)

    def scan_step(count, carry):
        step = piece - 1 - count
        result = []
        for lane in range(lanes):
            value, product = carry[lane]
            factor = decays[lane, pl.ds(step + 1, PARTS, stride=piece), :]
            value = factor * value + carried[lane, pl.ds(step, PARTS, stride=piece), :]
            product = factor * product
            carried[lane, pl.ds(step, PARTS, stride=piece), :] = value
            products[lane, pl.ds(step, PARTS, stride=piece), :] = product
            result.append((value, product))
        return tuple(result)

    last = lax.fori_loop(0, piece, scan_step, ((zero, one),) * lanes, unroll=8)
    for lane in range(lanes):
        value, product = last[lane]
        entering = jnp.zeros((1, 128), jnp.float32)
        for part in range(PARTS - 1, -1, -1):
            ends[part, 0:1, lane * 128 : (lane + 1) * 128] = entering
            entering = value[part : part + 1, :] + product[part : part + 1, :] * entering

    def gate_chunk(index, totals):
        rate_sum, inflow_sum, decay_sum = totals
        base = pl.multiple_of(index * CHUNK, CHUNK)
        here = pl.ds(base, CHUNK)
        segment = base // piece
        kept = keep[here, 0:1]
        grad = jnp.concatenate(
            [
                carried[lane, here, :]
                + products[lane, here, :]
                * ends[segment, 0:1, lane * 128 : (lane + 1) * 128]
                for lane in range(lanes)
            ],
            axis=1,
        )
        earlier = before[pl.ds(base, CHUNK + 8), :][7 : 7 + CHUNK, :]
        plain = decay[here, :]
        hole = root[here, :]
        rate_sig = rate[here, :]
        inflow_sig = inflow[here, :]
        conv_vals = conv[here, :].astype(jnp.float32)
        factor = hole * kept + (1.0 - kept)
        scaled = grad * inflow_sig
        log_grad = (
            (grad * earlier * plain - scaled * conv_vals * (plain * plain) / hole) * kept
        )
        rate_low = (
            log_grad * params[9:10, :] * rate_sig * (1.0 - rate_sig)
        ).astype(jnp.bfloat16)
        elem = scaled * factor
        inflow_low = (elem * conv_vals * (1.0 - inflow_sig)).astype(jnp.bfloat16)
        logit_grad[here, :width] = rate_low
        logit_grad[here, width:] = inflow_low
        conv_grad[here, :] = elem

        def fold(values):
            return jnp.sum(values.reshape(CHUNK // 8, 8, width), axis=0)

        return (
            rate_sum + fold(rate_low.astype(jnp.float32)),
            inflow_sum + fold(inflow_low.astype(jnp.float32)),
            decay_sum + fold(log_grad * rate_sig),
        )

    rate_sum, inflow_sum, decay_sum = lax.fori_loop(
        0, rows // CHUNK, gate_chunk, (zero_rows, zero_rows, zero_rows)
    )

    conv_grad[...] += lax.dot_general(
        logit_grad[...],
        gate_weight[...],
        (((1,), (1,)), ((), ())),
        preferred_element_type=jnp.float32,
    )
    gate_grad[...] = lax.dot_general(
        conv[...],
        logit_grad[...],
        (((0,), (0,)), ((), ())),
        preferred_element_type=jnp.float32,
    )

    def tap_chunk(index, totals):
        base = pl.multiple_of(index * CHUNK, CHUNK)
        here = pl.ds(base, CHUNK)
        grad = conv_grad[here, :]
        keeps = keep[here, :]
        window = padded[pl.ds(base, CHUNK + 8), :]

        def fold(values):
            return jnp.sum(values.reshape(CHUNK // 8, 8, width), axis=0)

        result = [totals[0] + fold(grad), totals[1] + fold(grad * window[8:, :])]
        for steps in (1, 2, 3):
            kept_grad = grad * keeps[:, steps - 1 : steps]
            shifted_grad[steps - 1, here, :] = kept_grad
            result.append(
                totals[1 + steps] + fold(kept_grad * window[8 - steps : 8 - steps + CHUNK, :])
            )
        return tuple(result)

    taps = lax.fori_loop(0, rows // CHUNK, tap_chunk, (zero_rows,) * 5)

    def leave_part(part, total):
        start = pl.multiple_of(offsets[part], piece)
        for half in range(piece // CHUNK):
            base = pl.multiple_of(start + half * CHUNK, CHUNK)
            local = pl.ds(pl.multiple_of(part * piece + half * CHUNK, CHUNK), CHUNK)
            grad = params[3:4, :] * conv_grad[pl.ds(base, CHUNK), :]
            for steps in (1, 2, 3):
                window = shifted_grad[steps - 1, pl.ds(base, CHUNK + 8), :]
                grad = grad + params[3 + steps : 4 + steps, :] * window[steps : steps + CHUNK, :]
            low = grad.astype(jnp.bfloat16)
            branch_grad[local, width:] = low
            total = total + jnp.sum(low.astype(jnp.float32).reshape(CHUNK // 8, 8, width), axis=0)
        return total

    input_sum = lax.fori_loop(0, PARTS, leave_part, zero_rows)

    all_sums = (
        gelu_sum, input_sum, taps[1], taps[2], taps[3], taps[4], taps[0], rate_sum, inflow_sum,
    )
    for row, total in enumerate(all_sums):
        sums[row : row + 1, :] = jnp.sum(total, axis=0, keepdims=True)
    sums[9:10, :] = jnp.sum(decay_sum, axis=0, keepdims=True) * params[10:11, :]
    sums[10:16, :] = jnp.zeros((6, width), jnp.float32)


def dot_rows(left, right):
    return lax.dot_general(
        left, right, (((0,), (0,)), ((), ())), preferred_element_type=jnp.float32
    )


def dot_back(left, right):
    return lax.dot_general(
        left, right, (((1,), (1,)), ((), ())), preferred_element_type=jnp.float32
    )


def dot_plain(left, right):
    return jnp.dot(left, right, preferred_element_type=jnp.float32)


def feed_pair(
    second, cots, gate_weight, up_weight, down_weight, hidden, gate_grad, up_grad, back, down,
    back_total, down_total,
):
    step = pl.program_id(0)
    gate = dot_plain(second[...], gate_weight[...])
    up = dot_plain(second[...], up_weight[...])
    upper, bend, square = gelu_parts(gate)
    act = gate * upper
    low = (act * up).astype(jnp.bfloat16)
    hidden[...] = low
    grad = dot_back(cots[...], down_weight[...])
    slope = upper + 0.5 * gate * (1.0 - bend * bend) * (
        GELU_SCALE + (3.0 * GELU_SCALE * GELU_CUBE) * square
    )
    gate_low = (grad * up * slope).astype(jnp.bfloat16)
    up_low = (grad * act).astype(jnp.bfloat16)
    gate_grad[...] = gate_low
    up_grad[...] = up_low
    back_part = dot_back(gate_low, gate_weight[...]) + dot_back(up_low, up_weight[...])
    down_part = dot_plain(low, down_weight[...])

    @pl.when(step == 0)
    def _():
        back_total[...] = back_part
        down_total[...] = down_part

    @pl.when(step > 0)
    def _():
        back_total[...] += back_part
        down_total[...] += down_part

    @pl.when(step == pl.num_programs(0) - 1)
    def _():
        back[...] = back_total[...].astype(jnp.bfloat16)
        down[...] = down_total[...].astype(jnp.bfloat16)


def join_columns(pairs, joined, column=0):
    start = 0
    for pair in pairs:
        size, width = pair.shape
        joined[start : start + size, column : column + width] = pair[...]
        start += size


def split_cores(total, out):
    size = out.shape[3]
    for core in range(2):
        out[0, core, 0, :, :] = total[core * size : (core + 1) * size, :].astype(out.dtype)


def column_grads(side, *refs):
    left, right = refs[:4], refs[4:-3]
    out, left_rows, right_rows = refs[-3:]
    width = right[0].shape[1]

    @pl.when(pl.program_id(0) == 0)
    def _():
        for group in range(right_rows.shape[1] // width):
            join_columns(right[4 * group : 4 * group + 4], right_rows, group * width)

    join_columns(left, left_rows)
    split_cores(dot_rows(left_rows[...], right_rows[...]), out)


def branch_grads(side, *refs):
    normed, mixer, refs = refs[:4], refs[4:8], refs[8:]
    branch_grad, gated, weight, out, gain, back, normed_rows, mixer_rows = refs
    wide = gated.shape[1]
    width = out.shape[4] // 3
    join_columns(normed, normed_rows)
    join_columns(mixer, mixer_rows)
    back[...] = dot_back(branch_grad[: back.shape[0], :], weight[...]).astype(back.dtype)
    branch = dot_rows(normed_rows[...], branch_grad[...])
    mix = dot_rows(mixer_rows[...], gated[...])
    weighted = jnp.sum(branch * weight[...].astype(jnp.float32), axis=1, keepdims=True)
    gain[...] = jnp.broadcast_to(weighted, gain.shape)
    total = jnp.concatenate(
        [branch[:, :width], branch[:, wide : wide + width], mix[:, :width]], axis=1
    )
    split_cores(total, out)


VMEM_SPEC = pl.BlockSpec(memory_space=pltpu.VMEM)
SMEM_SPEC = pl.BlockSpec(memory_space=pltpu.SMEM)


MEGA = 1024 * 1024
TILE = 256


def run_forward(offsets, pre, keep, params, gate_weight):
    rows, width = 4 * pre[0].shape[0], pre[0].shape[1] // 2
    lanes = width // 128
    f32, low = jnp.float32, jnp.bfloat16
    full = jax.ShapeDtypeStruct((rows, width), f32)
    half = jax.ShapeDtypeStruct((rows, width), low)
    return pl.pallas_call(
        recurrent_forward,
        out_shape=(half, half, full, full, full, full, full),
        in_specs=[SMEM_SPEC] + [VMEM_SPEC] * 7,
        out_specs=(VMEM_SPEC,) * 7,
        scratch_shapes=[
            pltpu.VMEM((rows + 8, width), f32),
            pltpu.VMEM((rows, 2 * width), f32),
            pltpu.VMEM((lanes, rows, 128), f32),
            pltpu.VMEM((lanes, rows, 128), f32),
            pltpu.VMEM((lanes, rows, 128), f32),
            pltpu.VMEM((PARTS, 8, width), f32),
        ],
        compiler_params=pltpu.CompilerParams(vmem_limit_bytes=40 * MEGA),
    )(offsets, *pre, keep, params, gate_weight)


def run_backward(offsets, gated_grad, pre, keep, params, gate_weight, kept):
    rows, width = 4 * pre[0].shape[0], pre[0].shape[1] // 2
    lanes = width // 128
    f32, low = jnp.float32, jnp.bfloat16
    return pl.pallas_call(
        recurrent_backward,
        out_shape=(
            jax.ShapeDtypeStruct((rows, 2 * width), low),
            jax.ShapeDtypeStruct((width, 2 * width), f32),
            jax.ShapeDtypeStruct((16, width), f32),
        ),
        in_specs=[SMEM_SPEC] + [VMEM_SPEC] * 17,
        out_specs=(VMEM_SPEC,) * 3,
        scratch_shapes=[
            pltpu.VMEM((rows + 8, width), f32),
            pltpu.VMEM((lanes, rows, 128), f32),
            pltpu.VMEM((lanes, rows + 8, 128), f32),
            pltpu.VMEM((lanes, rows, 128), f32),
            pltpu.VMEM((PARTS, 8, width), f32),
            pltpu.VMEM((rows + 8, width), f32),
            pltpu.VMEM((rows, 2 * width), low),
            pltpu.VMEM((rows, width), f32),
            pltpu.VMEM((3, rows + 8, width), f32),
        ],
        compiler_params=pltpu.CompilerParams(vmem_limit_bytes=48 * MEGA),
    )(offsets, *gated_grad, *pre, keep, params, gate_weight, *kept)


def column_spec(rows):
    return pl.BlockSpec((rows, TILE), lambda step, side: (0, step))


def placed_spec(columns, column):
    return pl.BlockSpec(
        (1, 2, 1, TILE // 2, columns),
        lambda step, side: (step % 4, 0, (step // 4 + side[0]) % 2, 0, column),
    )


def placed_shape(model, columns):
    return pltpu.HBM((model // TILE // 2, 2, 2, TILE // 2, columns), jnp.bfloat16)


def whole_spec(array):
    return pl.BlockSpec(array.shape, lambda step, side: (0, 0))


def run_feed_pair(second, cots, gate_weight, up_weight, down_weight):
    size, model = second.shape
    width = gate_weight.shape[1]
    whole = pl.BlockSpec((size, model), lambda step: (0, 0))
    across = pl.BlockSpec((model, TILE), lambda step: (0, step))
    slim = pl.BlockSpec((size, TILE), lambda step: (0, step))
    narrow = jax.ShapeDtypeStruct((size, width), jnp.bfloat16)
    long = jax.ShapeDtypeStruct((size, model), jnp.bfloat16)
    return pl.pallas_call(
        feed_pair,
        grid=(width // TILE,),
        in_specs=[
            whole, whole, across, across, pl.BlockSpec((TILE, model), lambda step: (step, 0))
        ],
        out_specs=(slim, slim, slim, whole, whole),
        out_shape=(narrow, narrow, narrow, long, long),
        scratch_shapes=[pltpu.VMEM((size, model), jnp.float32)] * 2,
        compiler_params=pltpu.CompilerParams(vmem_limit_bytes=28 * MEGA),
    )(second, cots, gate_weight, up_weight, down_weight)


def run_column_grads(side, left, right, columns, column, earlier=()):
    model = left[0].shape[1]
    rows = sum(group.shape[0] for group in left)
    width = len(right) // 4 * right[0].shape[1]
    return pl.pallas_call(
        column_grads,
        grid_spec=pltpu.PrefetchScalarGridSpec(
            num_scalar_prefetch=1,
            grid=(model // TILE,),
            in_specs=[column_spec(group.shape[0]) for group in left]
            + [whole_spec(group) for group in right]
            + [pl.BlockSpec(memory_space=pl.ANY)] * len(earlier),
            out_specs=placed_spec(width, column),
            scratch_shapes=[
                pltpu.VMEM((rows, TILE), jnp.bfloat16),
                pltpu.VMEM((rows, width), jnp.bfloat16),
            ],
        ),
        out_shape=placed_shape(model, columns),
        input_output_aliases={5 + len(right): 0} if earlier else {},
        compiler_params=pltpu.CompilerParams(vmem_limit_bytes=28 * MEGA),
    )(side, *left, *right, *earlier)


def run_branch_grads(side, normed, mixer, branch_grad, gated, weight, width):
    size, model = normed[0].shape
    return pl.pallas_call(
        branch_grads,
        grid_spec=pltpu.PrefetchScalarGridSpec(
            num_scalar_prefetch=1,
            grid=(model // TILE,),
            in_specs=[column_spec(size)] * 8
            + [whole_spec(branch_grad), whole_spec(gated)]
            + [pl.BlockSpec((TILE, weight.shape[1]), lambda step, side: (step, 0))],
            out_specs=(
                placed_spec(3 * width, 0),
                pl.BlockSpec((TILE, 128), lambda step, side: (step, 0)),
                column_spec(5 * size // 2),
            ),
            scratch_shapes=[pltpu.VMEM((4 * size, TILE), jnp.bfloat16)] * 2,
        ),
        out_shape=(
            placed_shape(model, 3 * width),
            pltpu.HBM((model, 128), jnp.float32),
            jax.ShapeDtypeStruct((5 * size // 2, model), jnp.bfloat16),
        ),
        compiler_params=pltpu.CompilerParams(vmem_limit_bytes=28 * MEGA),
    )(side, *normed, *mixer, branch_grad, gated, weight)


RING = 4
PIECES = ((0, 0), (0, 1), (-1, 0), (1, 0), (2, 0), (-1, 1), (1, 1), (2, 1))


def mp_shift(values, along, across):
    pairs = [
        (ring * 2 + side, ((ring + along) % RING) * 2 + (side + across) % 2)
        for ring in range(RING)
        for side in range(2)
    ]
    return lax.ppermute(values, "mp", pairs)


def dp_shift(values, across, along, core):
    pairs = [
        (
            (side * RING + ring) * 2 + own,
            (((side + across) % 2) * RING + (ring + along) % RING) * 2 + (own + core) % 2,
        )
        for side in range(2)
        for ring in range(RING)
        for own in range(2)
    ]
    return lax.ppermute(values, "dp", pairs)


def half_dp_scatter(values):
    groups = [list(range(side * 2 * RING, (side + 1) * 2 * RING)) for side in range(2)]
    values = with_layout_constraint(values.reshape(-1, values.shape[-1]), Layout((0, 1)))
    total = lax.psum_scatter(
        values, "dp", scatter_dimension=0, tiled=True, axis_index_groups=groups
    )
    return with_layout_constraint(total, Layout((0, 1)))


def sides_sum(values):
    mine, other = halves(values)
    return mine.astype(jnp.float32) + dp_shift(other, 1, 0, 0).astype(jnp.float32)


def pair_sum(values, shift, low):
    values = values.astype(jnp.bfloat16) if low else values
    return values.astype(jnp.float32) + shift(values).astype(jnp.float32)


def ring_sum(values, shift, low):
    values = values.astype(jnp.bfloat16) if low else values
    one, two, three = [shift(values, along).astype(jnp.float32) for along in (1, 2, 3)]
    return (values.astype(jnp.float32) + two) + (one + three)


def core_sum(values, low):
    return pair_sum(values, lambda part: dp_shift(part, 0, 0, 1), low)


def row_sum(values, low, step):
    def swap(part):
        return lax.ppermute(part, "dp", [(place, place ^ step) for place in range(4 * RING)])

    return pair_sum(values, swap, low)


def side_sum(values, low):
    return pair_sum(values, lambda part: dp_shift(part, 1, 0, 0), low)


def join(values):
    return [jnp.concatenate(values[at : at + 2], 0) for at in range(0, len(values), 2)]


def gather_pieces(mine, extra=(), second_work=None, third_work=None):
    across = mp_shift(mine, 0, 1)
    below = mp_shift(mine, 1, 0)
    above = mp_shift(mine, -1, 0)
    across, below, above, extra = lax.optimization_barrier((across, below, above, extra))
    far_top = mp_shift(halves(below)[0], 1, 0)
    far_bottom = mp_shift(halves(above)[1], -1, 0)
    done = second_work([mine, across]) if second_work else ()
    far_top, far_bottom, across, second_done = lax.optimization_barrier(
        (far_top, far_bottom, across, done)
    )
    far = jnp.concatenate([far_top, far_bottom], 0)
    below_across = mp_shift(across, 1, 0)
    above_across = mp_shift(across, -1, 0)
    far_across = mp_shift(far, 0, 1)
    done = third_work([below, above]) if third_work else ()
    below_across, above_across, far_across, third_done = lax.optimization_barrier(
        (below_across, above_across, far_across, done)
    )
    pieces = [mine, across, below, above, far, below_across, above_across, far_across]
    return pieces, extra, second_done, third_done


def halves(pair):
    rows = pair.shape[0] // 2
    return pair[:rows], pair[rows:]


def low_sum(*terms):
    total = terms[0].astype(jnp.float32)
    for term in terms[1:]:
        total = total + term.astype(jnp.float32)
    return total.astype(jnp.bfloat16)


def send_across(three, work=None):
    rows = three.shape[0] // 3
    down = mp_shift(three[:rows], -1, 0)
    up = mp_shift(three[rows : 2 * rows], 1, 0)
    far = mp_shift(three[2 * rows :], 0, 1)
    done = work() if work else ()
    return lax.optimization_barrier((down, up, far, done))


def send_far(far, far_in, work=None):
    top, bottom = halves(low_sum(far, far_in))
    done = work((top, bottom)) if work else ()
    top, bottom = mp_shift(top, 1, 0), mp_shift(bottom, -1, 0)
    return lax.optimization_barrier((top, bottom, done))


def send_near(near, beside, side_down, side_up, top, bottom, work=None):
    f32 = jnp.float32
    mine, other = halves(near)
    below, above = halves(beside)
    below_top, below_bottom = halves(below)
    above_top, above_bottom = halves(above)
    up = jnp.concatenate([low_sum(above_top, top), low_sum(above_bottom)], 0)
    down = jnp.concatenate([low_sum(below_top), low_sum(below_bottom, bottom)], 0)
    up, down = mp_shift(up, 1, 0), mp_shift(down, -1, 0)
    other = mp_shift(low_sum(other, side_down, side_up), 0, 1)
    done = work() if work else ()
    other, up, down, done = lax.optimization_barrier((other, up, down, done))
    total = mine.astype(f32) + up.astype(f32) + down.astype(f32) + other.astype(f32)
    return total, done


def rms_forward(values, gain):
    scale = lax.rsqrt(jnp.mean(values * values, axis=-1, keepdims=True) + EPSILON)
    return (values * scale * gain, scale)


def rms_backward(values, scale, gain, grad):
    scaled_grad = grad * gain
    inner = jnp.mean(scaled_grad * values, axis=-1, keepdims=True)
    return scale * scaled_grad - values * scale * scale * scale * inner


def gelu_tanh(values):
    return jax.nn.gelu(values, approximate=True)


def tie(values, anchor):
    return lax.optimization_barrier((values, anchor))[0]


def block_diagonal(weight, width):
    size = weight.shape[1]
    return jnp.concatenate(
        [
            jnp.pad(weight[0], ((0, 0), (0, width - size))),
            jnp.pad(weight[1], ((0, 0), (size, width - 2 * size))),
            jnp.zeros((width - 2 * size, width), weight.dtype),
        ],
        0,
    )


def on_device(
    tokens,
    seg_ids,
    first_gain,
    gelu_weight,
    gelu_bias,
    input_weight,
    input_bias,
    conv_weight,
    conv_bias,
    rate_weight,
    rate_bias,
    inflow_weight,
    inflow_bias,
    decay_param,
    mix_weight,
    second_gain,
    gate_weight,
    up_weight,
    down_weight,
    cotangent,
):
    f32, low = jnp.float32, jnp.bfloat16
    seg_row = seg_ids[0]
    rows = tokens.shape[0]
    model = tokens.shape[1]
    width = gelu_weight.shape[1]
    hidden_width = gate_weight.shape[1]
    size = rate_weight.shape[1]
    wide = -(-width // 128) * 128
    place = lax.axis_index("mp")
    ring, side = place // 2, place % 2
    offsets = jnp.stack(
        [
            (((ring + along + RING) % RING) * 2 + (side + across) % 2) * rows
            for along, across in PIECES
        ]
    ).astype(jnp.int32)

    def dot(left, right):
        return jnp.dot(left, right, preferred_element_type=f32)

    def dot_back(left, right):
        return lax.dot_general(left, right, (((1,), (1,)), ((), ())), preferred_element_type=f32)

    dp_side = (lax.axis_index("dp") // (2 * RING)).astype(jnp.int32).reshape(1)

    rows_in = tokens.astype(f32)
    first_scale_gain = first_gain.astype(f32)
    second_scale_gain = second_gain.astype(f32)
    cot_rows = cotangent.astype(f32)
    first_normed, first_scale = rms_forward(rows_in, first_scale_gain)
    normed_pieces, (cot_below, cot_above), _, _ = gather_pieces(
        first_normed.astype(low), (mp_shift(cotangent, 1, 0), mp_shift(cotangent, -1, 0))
    )

    keep_list = []
    for steps in (1, 2, 3):
        before = jnp.concatenate([jnp.full((steps,), -1, jnp.int32), seg_row[:-steps]])
        keep_list.append((before == seg_row).astype(f32))
    keep = jnp.stack(keep_list + [jnp.zeros_like(keep_list[0])] * 5, axis=1)
    decay_vals = jnp.pad(decay_param.astype(f32), (0, wide - width), constant_values=1.0)

    def row(values):
        return jnp.pad(values.astype(f32), (0, wide - width))

    params = jnp.stack(
        [row(gelu_bias), row(input_bias), row(conv_bias)]
        + [row(conv_weight[tap]) for tap in range(4)]
        + [
            row(rate_bias),
            row(inflow_bias),
            -DECAY_SCALE * jax.nn.softplus(-decay_vals),
            DECAY_SCALE * jax.nn.sigmoid(-decay_vals),
        ]
        + [jnp.zeros((wide,), f32)] * 5
    )
    lane_pad = ((0, 0), (0, wide - width))
    branch_weight = jnp.concatenate(
        [jnp.pad(gelu_weight, lane_pad), jnp.pad(input_weight, lane_pad)], 1
    )
    mix_wide = jnp.pad(mix_weight, ((0, wide - width), (0, 0)))
    gates_weight = jnp.concatenate(
        [block_diagonal(rate_weight, wide), block_diagonal(inflow_weight, wide)], 1
    )

    normed = join(normed_pieces)
    cot_across = mp_shift(tie(cotangent, normed_pieces[1]), 0, 1)
    cot_across, cot_below, cot_above = tie(
        (cot_across, cot_below, cot_above), normed_pieces[5:]
    )
    cot_moving = (
        mp_shift(halves(cot_below)[0], 1, 0),
        mp_shift(halves(cot_above)[1], -1, 0),
        mp_shift(cot_across, 1, 0),
        mp_shift(cot_across, -1, 0),
    )

    pre = [dot(pair, branch_weight) for pair in normed]
    gated, *kept = run_forward(offsets, pre, keep, params, gates_weight)
    gated, cot_moving = lax.optimization_barrier((gated, cot_moving))

    def piece_rows(values, first, last):
        return values[first * rows : last * rows]

    mixed = dot(piece_rows(gated, 5, 8), mix_wide).astype(low)
    side_down, side_up, far_in, _ = send_across(mixed)
    cot_far = jnp.concatenate(cot_moving[:2], 0)
    cot_far_across = mp_shift(tie(cot_far, side_down), 0, 1)
    mixed = dot(piece_rows(gated, 0, 5), mix_wide)
    top, bottom, _ = send_far(piece_rows(mixed, 4, 5), far_in)
    mixed, _ = send_near(
        piece_rows(mixed, 0, 2), piece_rows(mixed, 2, 4), side_down, side_up, top, bottom
    )
    middle = rows_in + mixed
    second_normed, second_scale = rms_forward(middle, second_scale_gain)
    second_low, cot_far_across = lax.optimization_barrier(
        (second_normed.astype(low), cot_far_across)
    )

    def group(pieces):
        return [
            jnp.concatenate(pieces[:2], 0),
            jnp.concatenate(pieces[2:4], 0),
            pieces[4],
            jnp.concatenate(pieces[5:], 0),
        ]

    cots = group(
        [cotangent, cot_across, cot_below, cot_above, cot_far, *cot_moving[2:], cot_far_across]
    )

    def feed(index, values):
        return run_feed_pair(values, cots[index], gate_weight, up_weight, down_weight)

    second_pieces, _, feed_zero, feed_one = gather_pieces(
        second_low,
        (),
        lambda pieces: feed(0, jnp.concatenate(pieces, 0)),
        lambda pieces: feed(1, jnp.concatenate(pieces, 0)),
    )
    second = group(second_pieces)
    feed_last = feed(3, second[3])
    second_far, second_last = lax.optimization_barrier((second[2], feed_last[3]))
    side_down, side_up, far_in, feed_far = send_across(second_last, lambda: feed(2, second_far))
    feeds = zip(feed_zero, feed_one, feed_far, feed_last)
    hiddens, gate_grads, up_grads, second_grads, downs = [list(values) for values in feeds]
    columns = 3 * hidden_width
    top, bottom, feed_sum = send_far(
        second_grads[2],
        far_in,
        lambda _: run_column_grads(dp_side, cots, hiddens, columns, 2),
    )
    second_grad, feed_sum = send_near(
        second_grads[0],
        second_grads[1],
        side_down,
        side_up,
        top,
        bottom,
        lambda: run_column_grads(
            dp_side, second, gate_grads + up_grads, columns, 0, [feed_sum]
        ),
    )
    feed_sum = half_dp_scatter(feed_sum)
    middle_grad = cot_rows + rms_backward(middle, second_scale, second_scale_gain, second_grad)
    second_gain_local = jnp.sum(second_grad * middle * second_scale, axis=0)
    mixer_pieces = gather_pieces(middle_grad.astype(low))[0]
    mixer = join(mixer_pieces)
    downs = tie(downs, mixer_pieces[5:])
    down_moving = (
        mp_shift(piece_rows(downs[3], 0, 1), -1, 0),
        mp_shift(piece_rows(downs[3], 1, 2), 1, 0),
        mp_shift(piece_rows(downs[3], 2, 3), 0, 1),
        mp_shift(halves(downs[1])[0], -1, 0),
        mp_shift(halves(downs[1])[1], 1, 0),
    )

    gated_grad = [dot_back(pair, mix_wide) for pair in mixer]
    branch_grad, gates_grad, sums = run_backward(
        offsets, gated_grad, pre, keep, params, gates_weight, kept
    )
    branch_grad, down_moving, feed_sum = lax.optimization_barrier(
        (branch_grad, down_moving, feed_sum)
    )
    gate_blocks = jnp.concatenate(
        [
            gates_grad[:size, :size],
            gates_grad[size : 2 * size, size : 2 * size],
            gates_grad[:size, wide : wide + size],
            gates_grad[size : 2 * size, wide + size : wide + 2 * size],
        ],
        1,
    )
    small = jnp.concatenate(
        [gate_blocks, jnp.pad(sums[:, :width], ((0, 0), (0, 4 * size - width)))], 0
    )

    first_last = dot_back(piece_rows(branch_grad, 5, 8), branch_weight).astype(low)
    branch_grad, first_last, down_far = lax.optimization_barrier(
        (branch_grad, first_last, down_moving[2])
    )

    def first_slot():
        top, bottom = halves(low_sum(downs[2], down_far))
        return (
            run_branch_grads(
                dp_side, normed, mixer, branch_grad, gated, branch_weight, width
            ),
            mp_shift(top, 1, 0),
            mp_shift(bottom, -1, 0),
        )

    side_down, side_up, far_in, first_done = send_across(first_last, first_slot)
    (branch_sum, gain_rows, first_grads), down_top, down_bottom = first_done
    branch_sum = half_dp_scatter(branch_sum)
    gains = jnp.stack([gain_rows[:, 0], second_gain_local])
    top, bottom, (gains, down_top, down_bottom) = send_far(
        piece_rows(first_grads, 4, 5),
        far_in,
        lambda ready: (
            core_sum(tie(gains, ready), False),
            mp_shift(tie(down_top, ready), 1, 0),
            mp_shift(tie(down_bottom, ready), -1, 0),
        ),
    )
    first_grad, (small, gains) = send_near(
        piece_rows(first_grads, 0, 2),
        piece_rows(first_grads, 2, 4),
        side_down,
        side_up,
        top,
        bottom,
        lambda: (core_sum(small, True), row_sum(gains, False, 2)),
    )
    tokens_grad = middle_grad + rms_backward(rows_in, first_scale, first_scale_gain, first_grad)
    small = side_sum(row_sum(row_sum(small, True, 2), True, 4), True)
    gains = side_sum(row_sum(gains, False, 4), False)
    gains, branch_sum = lax.optimization_barrier((gains, branch_sum))
    branch_sum = sides_sum(branch_sum)
    gains = pair_sum(gains, lambda part: mp_shift(part, 0, 1), False)
    gains, branch_sum = lax.optimization_barrier((gains, branch_sum))
    gains = ring_sum(gains, lambda part, along: mp_shift(part, along, 0), False)
    down_mine, down_other = halves(downs[0])
    down_other = tie(down_other, top)
    down_other = mp_shift(low_sum(down_other, down_moving[0], down_moving[1]), 0, 1)
    result = middle + down_mine.astype(f32) + down_other.astype(f32)
    result = result + down_moving[3].astype(f32) + down_moving[4].astype(f32)
    result = result + jnp.concatenate([down_top, down_bottom], 0).astype(f32)
    result = result.astype(low)
    feed_sum = sides_sum(tie(feed_sum, top))


    sums = small[size : size + 16, :width]
    return (
        result,
        tokens_grad,
        gains[0] / first_scale_gain,
        branch_sum[:, :width],
        sums[0],
        branch_sum[:, width : 2 * width],
        sums[1],
        sums[2:6],
        sums[6],
        jnp.stack([small[:size, :size], small[:size, size : 2 * size]]),
        sums[7],
        jnp.stack([small[:size, 2 * size : 3 * size], small[:size, 3 * size : 4 * size]]),
        sums[8],
        sums[9],
        branch_sum[:, 2 * width :].T,
        gains[1],
        feed_sum[:, :hidden_width],
        feed_sum[:, hidden_width : 2 * hidden_width],
        feed_sum[:, 2 * hidden_width :].T,
    )


def solution(mesh):
    return jax.shard_map(
        on_device,
        mesh=mesh,
        in_specs=(
            P(("dp", "mp"), None),
            P("dp", None),
            P(),
            P(None, "mp"),
            P("mp"),
            P(None, "mp"),
            P("mp"),
            P(None, "mp"),
            P("mp"),
            P("mp", None, None),
            P("mp"),
            P("mp", None, None),
            P("mp"),
            P("mp"),
            P("mp", None),
            P(),
            P(None, "mp"),
            P(None, "mp"),
            P("mp", None),
            P(("dp", "mp"), None),
        ),
        out_specs=(
            P(("dp", "mp"), None),
            P(("dp", "mp"), None),
            P(),
            P("dp", "mp"),
            P("mp"),
            P("dp", "mp"),
            P("mp"),
            P(None, "mp"),
            P("mp"),
            P("mp", None, None),
            P("mp"),
            P("mp", None, None),
            P("mp"),
            P("mp"),
            P("mp", "dp"),
            P(),
            P("dp", "mp"),
            P("dp", "mp"),
            P("mp", "dp"),
        ),
        check_vma=False,
    )
```

```python
import jax
import jax.numpy as jnp
from jax import lax
from jax.experimental import pallas as pl
from jax.experimental.layout import Layout, with_layout_constraint
from jax.experimental.pallas import tpu as pltpu
from jax.sharding import PartitionSpec as P

EPSILON = 1e-06
DECAY_SCALE = 8.0
GELU_SCALE = 0.7978845608028654
GELU_CUBE = 0.044715
CHUNK = 64
PARTS = 8


def one_minus_exp(double_rate, exp_square):
    y = -double_rate
    series = 1.0 - y * (1.0 / 7.0)
    for order in (6.0, 5.0, 4.0, 3.0, 2.0):
        series = 1.0 - y * (1.0 / order) * series
    return jnp.where(y < 0.5, y * series, 1.0 - exp_square)


def gelu_parts(values):
    square = values * values
    slope = GELU_SCALE + (GELU_SCALE * GELU_CUBE) * square
    bend = jnp.tanh(values * slope)
    half = 0.5 + 0.5 * bend
    return half, bend, square


def recurrent_forward(
    offsets, pre_one, pre_two, pre_three, pre_four, keep, params, gate_weight,
    gated, conv, rate, inflow, decay, root, state,
    padded, logits, decays, injects, products, ends,
):
    rows, width = conv.shape
    piece = rows // PARTS
    pairs = (pre_one, pre_two, pre_three, pre_four)

    padded[0:8, :] = jnp.zeros((8, width), jnp.float32)
    for part in range(PARTS):
        place = pl.multiple_of(offsets[part] + 8, 8)
        half = slice(part % 2 * piece, (part % 2 + 1) * piece)
        padded[pl.ds(place, piece), :] = pairs[part // 2][half, width:] + params[1:2, :]

    def conv_chunk(index, carry):
        base = pl.multiple_of(index * CHUNK, CHUNK)
        window = padded[pl.ds(base, CHUNK + 8), :]
        keeps = keep[pl.ds(base, CHUNK), :]
        total = params[2:3, :] + params[3:4, :] * window[8:, :]
        for steps in (1, 2, 3):
            shifted = window[8 - steps : 8 - steps + CHUNK, :]
            total = total + params[3 + steps : 4 + steps, :] * shifted * keeps[:, steps - 1 : steps]
        conv[pl.ds(base, CHUNK), :] = total.astype(jnp.bfloat16)
        return carry

    lax.fori_loop(0, rows // CHUNK, conv_chunk, 0)

    logits[...] = jnp.dot(conv[...], gate_weight[...], preferred_element_type=jnp.float32)

    def gate_chunk(index, carry):
        base = pl.multiple_of(index * CHUNK, CHUNK)
        here = pl.ds(base, CHUNK)
        kept = keep[here, 0:1]
        rate_sig = jax.nn.sigmoid(logits[here, :width] + params[7:8, :])
        inflow_sig = jax.nn.sigmoid(logits[here, width:] + params[8:9, :])
        log_rate = rate_sig * params[9:10, :]
        plain = jnp.exp(log_rate)
        hole = jnp.sqrt(one_minus_exp(2.0 * log_rate, plain * plain))
        factor = hole * kept + (1.0 - kept)
        rate[here, :] = rate_sig
        inflow[here, :] = inflow_sig
        decay[here, :] = plain
        root[here, :] = hole
        kept_decay = plain * kept
        inject = factor * inflow_sig * conv[here, :].astype(jnp.float32)
        for lane in range(width // 128):
            decays[lane, here, :] = kept_decay[:, lane * 128 : (lane + 1) * 128]
            injects[lane, here, :] = inject[:, lane * 128 : (lane + 1) * 128]
        return carry

    lax.fori_loop(0, rows // CHUNK, gate_chunk, 0)

    lanes = width // 128
    zero = jnp.zeros((PARTS, 128), jnp.float32)
    one = jnp.ones((PARTS, 128), jnp.float32)

    def scan_step(step, carry):
        result = []
        for lane in range(lanes):
            value, product = carry[lane]
            factor = decays[lane, pl.ds(step, PARTS, stride=piece), :]
            value = factor * value + injects[lane, pl.ds(step, PARTS, stride=piece), :]
            product = factor * product
            injects[lane, pl.ds(step, PARTS, stride=piece), :] = value
            products[lane, pl.ds(step, PARTS, stride=piece), :] = product
            result.append((value, product))
        return tuple(result)

    last = lax.fori_loop(0, piece, scan_step, ((zero, one),) * lanes, unroll=8)
    for lane in range(lanes):
        value, product = last[lane]
        entering = jnp.zeros((1, 128), jnp.float32)
        for part in range(PARTS):
            ends[part, 0:1, lane * 128 : (lane + 1) * 128] = entering
            entering = value[part : part + 1, :] + product[part : part + 1, :] * entering

    for part in range(PARTS):
        start = pl.multiple_of(offsets[part], piece)
        segment = offsets[part] // piece
        pre = pairs[part // 2]

        def finish_chunk(index, carry, part=part, start=start, segment=segment, pre=pre):
            there = pl.ds(pl.multiple_of(start + index * CHUNK, CHUNK), CHUNK)
            near = pl.ds(pl.multiple_of(part % 2 * piece + index * CHUNK, CHUNK), CHUNK)
            local = pl.ds(pl.multiple_of(part * piece + index * CHUNK, CHUNK), CHUNK)
            for lane in range(lanes):
                cols = slice(lane * 128, (lane + 1) * 128)
                whole = (
                    injects[lane, there, :]
                    + products[lane, there, :] * ends[segment, 0:1, cols]
                )
                state[there, cols] = whole
                values = pre[near, cols] + params[0:1, cols]
                act = values * gelu_parts(values)[0]
                gated[local, cols] = (act * whole).astype(jnp.bfloat16)
            return carry

        lax.fori_loop(0, piece // CHUNK, finish_chunk, 0)


def recurrent_backward(
    offsets, grad_one, grad_two, grad_three, grad_four, pre_one, pre_two, pre_three, pre_four,
    keep, params, gate_weight, conv, rate, inflow, decay, root, state,
    branch_grad, gate_grad, sums,
    padded, carried, decays, products, ends, before, logit_grad, conv_grad, shifted_grad,
):
    rows, width = conv.shape
    piece = rows // PARTS
    lanes = width // 128
    grad_pairs = (grad_one, grad_two, grad_three, grad_four)
    pre_pairs = (pre_one, pre_two, pre_three, pre_four)
    zero_rows = jnp.zeros((8, width), jnp.float32)

    padded[0:8, :] = zero_rows
    before[0:8, :] = zero_rows
    for lane in range(lanes):
        decays[lane, rows : rows + 8, :] = jnp.zeros((8, 128), jnp.float32)
    shifted_grad[:, rows : rows + 8, :] = jnp.zeros((3, 8, width), jnp.float32)

    gelu_sum = zero_rows
    for part in range(PARTS):
        start = pl.multiple_of(offsets[part], piece)
        pre, gated_grad = pre_pairs[part // 2], grad_pairs[part // 2]

        def enter_chunk(index, total, part=part, start=start, pre=pre, gated_grad=gated_grad):
            there = pl.ds(pl.multiple_of(start + index * CHUNK, CHUNK), CHUNK)
            ahead = pl.ds(pl.multiple_of(start + index * CHUNK + 8, 8), CHUNK)
            near = pl.ds(pl.multiple_of(part % 2 * piece + index * CHUNK, CHUNK), CHUNK)
            local = pl.ds(pl.multiple_of(part * piece + index * CHUNK, CHUNK), CHUNK)
            kept = keep[there, 0:1]
            padded[ahead, :] = pre[near, width:] + params[1:2, :]
            values = pre[near, :width] + params[0:1, :]
            upper, bend, square = gelu_parts(values)
            slope = upper + 0.5 * values * (1.0 - bend * bend) * (
                GELU_SCALE + (3.0 * GELU_SCALE * GELU_CUBE) * square
            )
            grad = gated_grad[near, :]
            here_state = state[there, :]
            before[ahead, :] = here_state
            gelu_grad = (grad * here_state * slope).astype(jnp.bfloat16)
            branch_grad[local, :width] = gelu_grad
            state_grad = grad * values * upper
            kept_decay = decay[there, :] * kept
            for lane in range(lanes):
                cols = slice(lane * 128, (lane + 1) * 128)
                carried[lane, there, :] = state_grad[:, cols]
                decays[lane, there, :] = kept_decay[:, cols]
            return total + jnp.sum(
                gelu_grad.astype(jnp.float32).reshape(CHUNK // 8, 8, width), axis=0
            )

        gelu_sum = lax.fori_loop(0, piece // CHUNK, enter_chunk, gelu_sum)

    zero = jnp.zeros((PARTS, 128), jnp.float32)
    one = jnp.ones((PARTS, 128), jnp.float32)

    def scan_step(count, carry):
        step = piece - 1 - count
        result = []
        for lane in range(lanes):
            value, product = carry[lane]
            factor = decays[lane, pl.ds(step + 1, PARTS, stride=piece), :]
            value = factor * value + carried[lane, pl.ds(step, PARTS, stride=piece), :]
            product = factor * product
            carried[lane, pl.ds(step, PARTS, stride=piece), :] = value
            products[lane, pl.ds(step, PARTS, stride=piece), :] = product
            result.append((value, product))
        return tuple(result)

    last = lax.fori_loop(0, piece, scan_step, ((zero, one),) * lanes, unroll=8)
    for lane in range(lanes):
        value, product = last[lane]
        entering = jnp.zeros((1, 128), jnp.float32)
        for part in range(PARTS - 1, -1, -1):
            ends[part, 0:1, lane * 128 : (lane + 1) * 128] = entering
            entering = value[part : part + 1, :] + product[part : part + 1, :] * entering

    def gate_chunk(index, totals):
        rate_sum, inflow_sum, decay_sum = totals
        base = pl.multiple_of(index * CHUNK, CHUNK)
        here = pl.ds(base, CHUNK)
        segment = base // piece
        kept = keep[here, 0:1]
        grad = jnp.concatenate(
            [
                carried[lane, here, :]
                + products[lane, here, :]
                * ends[segment, 0:1, lane * 128 : (lane + 1) * 128]
                for lane in range(lanes)
            ],
            axis=1,
        )
        earlier = before[pl.ds(base, CHUNK + 8), :][7 : 7 + CHUNK, :]
        plain = decay[here, :]
        hole = root[here, :]
        rate_sig = rate[here, :]
        inflow_sig = inflow[here, :]
        conv_vals = conv[here, :].astype(jnp.float32)
        factor = hole * kept + (1.0 - kept)
        scaled = grad * inflow_sig
        log_grad = (
            (grad * earlier * plain - scaled * conv_vals * (plain * plain) / hole) * kept
        )
        rate_low = (
            log_grad * params[9:10, :] * rate_sig * (1.0 - rate_sig)
        ).astype(jnp.bfloat16)
        elem = scaled * factor
        inflow_low = (elem * conv_vals * (1.0 - inflow_sig)).astype(jnp.bfloat16)
        logit_grad[here, :width] = rate_low
        logit_grad[here, width:] = inflow_low
        conv_grad[here, :] = elem

        def fold(values):
            return jnp.sum(values.reshape(CHUNK // 8, 8, width), axis=0)

        return (
            rate_sum + fold(rate_low.astype(jnp.float32)),
            inflow_sum + fold(inflow_low.astype(jnp.float32)),
            decay_sum + fold(log_grad * rate_sig),
        )

    rate_sum, inflow_sum, decay_sum = lax.fori_loop(
        0, rows // CHUNK, gate_chunk, (zero_rows, zero_rows, zero_rows)
    )

    conv_grad[...] += lax.dot_general(
        logit_grad[...],
        gate_weight[...],
        (((1,), (1,)), ((), ())),
        preferred_element_type=jnp.float32,
    )
    gate_grad[...] = lax.dot_general(
        conv[...],
        logit_grad[...],
        (((0,), (0,)), ((), ())),
        preferred_element_type=jnp.float32,
    )

    def tap_chunk(index, totals):
        base = pl.multiple_of(index * CHUNK, CHUNK)
        here = pl.ds(base, CHUNK)
        grad = conv_grad[here, :]
        keeps = keep[here, :]
        window = padded[pl.ds(base, CHUNK + 8), :]

        def fold(values):
            return jnp.sum(values.reshape(CHUNK // 8, 8, width), axis=0)

        result = [totals[0] + fold(grad), totals[1] + fold(grad * window[8:, :])]
        for steps in (1, 2, 3):
            kept_grad = grad * keeps[:, steps - 1 : steps]
            shifted_grad[steps - 1, here, :] = kept_grad
            result.append(
                totals[1 + steps] + fold(kept_grad * window[8 - steps : 8 - steps + CHUNK, :])
            )
        return tuple(result)

    taps = lax.fori_loop(0, rows // CHUNK, tap_chunk, (zero_rows,) * 5)

    def leave_part(part, total):
        start = pl.multiple_of(offsets[part], piece)
        for half in range(piece // CHUNK):
            base = pl.multiple_of(start + half * CHUNK, CHUNK)
            local = pl.ds(pl.multiple_of(part * piece + half * CHUNK, CHUNK), CHUNK)
            grad = params[3:4, :] * conv_grad[pl.ds(base, CHUNK), :]
            for steps in (1, 2, 3):
                window = shifted_grad[steps - 1, pl.ds(base, CHUNK + 8), :]
                grad = grad + params[3 + steps : 4 + steps, :] * window[steps : steps + CHUNK, :]
            low = grad.astype(jnp.bfloat16)
            branch_grad[local, width:] = low
            total = total + jnp.sum(low.astype(jnp.float32).reshape(CHUNK // 8, 8, width), axis=0)
        return total

    input_sum = lax.fori_loop(0, PARTS, leave_part, zero_rows)

    all_sums = (
        gelu_sum, input_sum, taps[1], taps[2], taps[3], taps[4], taps[0], rate_sum, inflow_sum,
    )
    for row, total in enumerate(all_sums):
        sums[row : row + 1, :] = jnp.sum(total, axis=0, keepdims=True)
    sums[9:10, :] = jnp.sum(decay_sum, axis=0, keepdims=True) * params[10:11, :]
    sums[10:16, :] = jnp.zeros((6, width), jnp.float32)


def dot_rows(left, right):
    return lax.dot_general(
        left, right, (((0,), (0,)), ((), ())), preferred_element_type=jnp.float32
    )


def dot_back(left, right):
    return lax.dot_general(
        left, right, (((1,), (1,)), ((), ())), preferred_element_type=jnp.float32
    )


def dot_plain(left, right):
    return jnp.dot(left, right, preferred_element_type=jnp.float32)


def feed_pair(
    second, cots, gate_weight, up_weight, down_weight, hidden, gate_grad, up_grad, back, down,
    back_total, down_total,
):
    step = pl.program_id(0)
    gate = dot_plain(second[...], gate_weight[...])
    up = dot_plain(second[...], up_weight[...])
    upper, bend, square = gelu_parts(gate)
    act = gate * upper
    low = (act * up).astype(jnp.bfloat16)
    hidden[...] = low
    grad = dot_back(cots[...], down_weight[...])
    slope = upper + 0.5 * gate * (1.0 - bend * bend) * (
        GELU_SCALE + (3.0 * GELU_SCALE * GELU_CUBE) * square
    )
    gate_low = (grad * up * slope).astype(jnp.bfloat16)
    up_low = (grad * act).astype(jnp.bfloat16)
    gate_grad[...] = gate_low
    up_grad[...] = up_low
    back_part = dot_back(gate_low, gate_weight[...]) + dot_back(up_low, up_weight[...])
    down_part = dot_plain(low, down_weight[...])

    @pl.when(step == 0)
    def _():
        back_total[...] = back_part
        down_total[...] = down_part

    @pl.when(step > 0)
    def _():
        back_total[...] += back_part
        down_total[...] += down_part

    @pl.when(step == pl.num_programs(0) - 1)
    def _():
        back[...] = back_total[...].astype(jnp.bfloat16)
        down[...] = down_total[...].astype(jnp.bfloat16)


def join_columns(pairs, joined, column=0):
    size, width = pairs[0].shape
    for index, pair in enumerate(pairs):
        joined[index * size : (index + 1) * size, column : column + width] = pair[...]


def split_cores(total, out):
    size = out.shape[3]
    for core in range(2):
        out[0, core, 0, :, :] = total[core * size : (core + 1) * size, :].astype(out.dtype)


def column_grads(side, *refs):
    left, right = refs[:4], refs[4:-3]
    out, left_rows, right_rows = refs[-3:]
    width = right[0].shape[1]

    @pl.when(pl.program_id(0) == 0)
    def _():
        for group in range(right_rows.shape[1] // width):
            join_columns(right[4 * group : 4 * group + 4], right_rows, group * width)

    join_columns(left, left_rows)
    split_cores(dot_rows(left_rows[...], right_rows[...]), out)


def branch_grads(side, *refs):
    normed, mixer, refs = refs[:4], refs[4:8], refs[8:]
    branch_grad, gated, weight, out, gain, back, normed_rows, mixer_rows = refs
    wide = gated.shape[1]
    width = out.shape[4] // 3
    join_columns(normed, normed_rows)
    join_columns(mixer, mixer_rows)
    back[...] = dot_back(branch_grad[: back.shape[0], :], weight[...]).astype(back.dtype)
    branch = dot_rows(normed_rows[...], branch_grad[...])
    mix = dot_rows(mixer_rows[...], gated[...])
    weighted = jnp.sum(branch * weight[...].astype(jnp.float32), axis=1, keepdims=True)
    gain[...] = jnp.broadcast_to(weighted, gain.shape)
    total = jnp.concatenate(
        [branch[:, :width], branch[:, wide : wide + width], mix[:, :width]], axis=1
    )
    split_cores(total, out)


VMEM_SPEC = pl.BlockSpec(memory_space=pltpu.VMEM)
SMEM_SPEC = pl.BlockSpec(memory_space=pltpu.SMEM)


MEGA = 1024 * 1024
TILE = 256


def run_forward(offsets, pre, keep, params, gate_weight):
    rows, width = 4 * pre[0].shape[0], pre[0].shape[1] // 2
    lanes = width // 128
    f32, low = jnp.float32, jnp.bfloat16
    full = jax.ShapeDtypeStruct((rows, width), f32)
    half = jax.ShapeDtypeStruct((rows, width), low)
    return pl.pallas_call(
        recurrent_forward,
        out_shape=(half, half, full, full, full, full, full),
        in_specs=[SMEM_SPEC] + [VMEM_SPEC] * 7,
        out_specs=(VMEM_SPEC,) * 7,
        scratch_shapes=[
            pltpu.VMEM((rows + 8, width), f32),
            pltpu.VMEM((rows, 2 * width), f32),
            pltpu.VMEM((lanes, rows, 128), f32),
            pltpu.VMEM((lanes, rows, 128), f32),
            pltpu.VMEM((lanes, rows, 128), f32),
            pltpu.VMEM((PARTS, 8, width), f32),
        ],
        compiler_params=pltpu.CompilerParams(vmem_limit_bytes=40 * MEGA),
    )(offsets, *pre, keep, params, gate_weight)


def run_backward(offsets, gated_grad, pre, keep, params, gate_weight, kept):
    rows, width = 4 * pre[0].shape[0], pre[0].shape[1] // 2
    lanes = width // 128
    f32, low = jnp.float32, jnp.bfloat16
    return pl.pallas_call(
        recurrent_backward,
        out_shape=(
            jax.ShapeDtypeStruct((rows, 2 * width), low),
            jax.ShapeDtypeStruct((width, 2 * width), f32),
            jax.ShapeDtypeStruct((16, width), f32),
        ),
        in_specs=[SMEM_SPEC] + [VMEM_SPEC] * 17,
        out_specs=(VMEM_SPEC,) * 3,
        scratch_shapes=[
            pltpu.VMEM((rows + 8, width), f32),
            pltpu.VMEM((lanes, rows, 128), f32),
            pltpu.VMEM((lanes, rows + 8, 128), f32),
            pltpu.VMEM((lanes, rows, 128), f32),
            pltpu.VMEM((PARTS, 8, width), f32),
            pltpu.VMEM((rows + 8, width), f32),
            pltpu.VMEM((rows, 2 * width), low),
            pltpu.VMEM((rows, width), f32),
            pltpu.VMEM((3, rows + 8, width), f32),
        ],
        compiler_params=pltpu.CompilerParams(vmem_limit_bytes=48 * MEGA),
    )(offsets, *gated_grad, *pre, keep, params, gate_weight, *kept)


def column_spec(rows):
    return pl.BlockSpec((rows, TILE), lambda step, side: (0, step))


def placed_spec(columns, column):
    return pl.BlockSpec(
        (1, 2, 1, TILE // 2, columns),
        lambda step, side: (step % 4, 0, (step // 4 + side[0]) % 2, 0, column),
    )


def placed_shape(model, columns):
    return pltpu.HBM((model // TILE // 2, 2, 2, TILE // 2, columns), jnp.bfloat16)


def whole_spec(array):
    return pl.BlockSpec(array.shape, lambda step, side: (0, 0))


def run_feed_pair(second, cots, gate_weight, up_weight, down_weight):
    size, model = second.shape
    width = gate_weight.shape[1]
    whole = pl.BlockSpec((size, model), lambda step: (0, 0))
    across = pl.BlockSpec((model, TILE), lambda step: (0, step))
    slim = pl.BlockSpec((size, TILE), lambda step: (0, step))
    narrow = jax.ShapeDtypeStruct((size, width), jnp.bfloat16)
    long = jax.ShapeDtypeStruct((size, model), jnp.bfloat16)
    return pl.pallas_call(
        feed_pair,
        grid=(width // TILE,),
        in_specs=[
            whole, whole, across, across, pl.BlockSpec((TILE, model), lambda step: (step, 0))
        ],
        out_specs=(slim, slim, slim, whole, whole),
        out_shape=(narrow, narrow, narrow, long, long),
        scratch_shapes=[pltpu.VMEM((size, model), jnp.float32)] * 2,
        compiler_params=pltpu.CompilerParams(vmem_limit_bytes=28 * MEGA),
    )(second, cots, gate_weight, up_weight, down_weight)


def run_column_grads(side, left, right, columns, column, earlier=()):
    size, model = left[0].shape
    width = len(right) // 4 * right[0].shape[1]
    return pl.pallas_call(
        column_grads,
        grid_spec=pltpu.PrefetchScalarGridSpec(
            num_scalar_prefetch=1,
            grid=(model // TILE,),
            in_specs=[column_spec(size)] * 4
            + [whole_spec(pair) for pair in right]
            + [pl.BlockSpec(memory_space=pl.ANY)] * len(earlier),
            out_specs=placed_spec(width, column),
            scratch_shapes=[
                pltpu.VMEM((4 * size, TILE), jnp.bfloat16),
                pltpu.VMEM((4 * size, width), jnp.bfloat16),
            ],
        ),
        out_shape=placed_shape(model, columns),
        input_output_aliases={5 + len(right): 0} if earlier else {},
        compiler_params=pltpu.CompilerParams(vmem_limit_bytes=28 * MEGA),
    )(side, *left, *right, *earlier)


def run_branch_grads(side, normed, mixer, branch_grad, gated, weight, width):
    size, model = normed[0].shape
    return pl.pallas_call(
        branch_grads,
        grid_spec=pltpu.PrefetchScalarGridSpec(
            num_scalar_prefetch=1,
            grid=(model // TILE,),
            in_specs=[column_spec(size)] * 8
            + [whole_spec(branch_grad), whole_spec(gated)]
            + [pl.BlockSpec((TILE, weight.shape[1]), lambda step, side: (step, 0))],
            out_specs=(
                placed_spec(3 * width, 0),
                pl.BlockSpec((TILE, 128), lambda step, side: (step, 0)),
                column_spec(3 * size),
            ),
            scratch_shapes=[pltpu.VMEM((4 * size, TILE), jnp.bfloat16)] * 2,
        ),
        out_shape=(
            placed_shape(model, 3 * width),
            pltpu.HBM((model, 128), jnp.float32),
            jax.ShapeDtypeStruct((3 * size, model), jnp.bfloat16),
        ),
        compiler_params=pltpu.CompilerParams(vmem_limit_bytes=28 * MEGA),
    )(side, *normed, *mixer, branch_grad, gated, weight)


RING = 4
PIECES = ((0, 0), (0, 1), (-1, 0), (-1, 1), (1, 0), (1, 1), (2, 0), (2, 1))


def mp_shift(values, along, across):
    pairs = [
        (ring * 2 + side, ((ring + along) % RING) * 2 + (side + across) % 2)
        for ring in range(RING)
        for side in range(2)
    ]
    return lax.ppermute(values, "mp", pairs)


def dp_shift(values, across, along, core):
    pairs = [
        (
            (side * RING + ring) * 2 + own,
            (((side + across) % 2) * RING + (ring + along) % RING) * 2 + (own + core) % 2,
        )
        for side in range(2)
        for ring in range(RING)
        for own in range(2)
    ]
    return lax.ppermute(values, "dp", pairs)


def half_dp_scatter(values):
    groups = [list(range(side * 2 * RING, (side + 1) * 2 * RING)) for side in range(2)]
    values = with_layout_constraint(values.reshape(-1, values.shape[-1]), Layout((0, 1)))
    total = lax.psum_scatter(
        values, "dp", scatter_dimension=0, tiled=True, axis_index_groups=groups
    )
    return with_layout_constraint(total, Layout((0, 1)))


def sides_sum(values):
    mine, other = halves(values)
    return mine.astype(jnp.float32) + dp_shift(other, 1, 0, 0).astype(jnp.float32)


def pair_sum(values, shift, low):
    values = values.astype(jnp.bfloat16) if low else values
    return values.astype(jnp.float32) + shift(values).astype(jnp.float32)


def ring_sum(values, shift, low):
    values = values.astype(jnp.bfloat16) if low else values
    one, two, three = [shift(values, along).astype(jnp.float32) for along in (1, 2, 3)]
    return (values.astype(jnp.float32) + two) + (one + three)


def core_sum(values, low):
    return pair_sum(values, lambda part: dp_shift(part, 0, 0, 1), low)


def row_sum(values, low, step):
    def swap(part):
        return lax.ppermute(part, "dp", [(place, place ^ step) for place in range(4 * RING)])

    return pair_sum(values, swap, low)


def side_sum(values, low):
    return pair_sum(values, lambda part: dp_shift(part, 1, 0, 0), low)


def join(values):
    return [jnp.concatenate(values[at : at + 2], 0) for at in range(0, len(values), 2)]


def gather_pieces(mine, second_work=None, third_work=None):
    across = mp_shift(mine, 0, 1)
    below = mp_shift(mine, 1, 0)
    above = mp_shift(mine, -1, 0)
    across, below, above = lax.optimization_barrier((across, below, above))
    below_across = mp_shift(across, 1, 0)
    above_across = mp_shift(across, -1, 0)
    done = second_work([mine, across]) if second_work else ()
    below_across, above_across, near_below, second_done = lax.optimization_barrier(
        (below_across, above_across, below, done)
    )
    far = mp_shift(near_below, 1, 0)
    far_across = mp_shift(above_across, -1, 0)
    done = third_work([below, below_across]) if third_work else ()
    far, far_across, third_done = lax.optimization_barrier((far, far_across, done))
    pieces = [mine, across, below, below_across, above, above_across, far, far_across]
    if second_work or third_work:
        return pieces, second_done, third_done
    return pieces


def halves(pair):
    rows = pair.shape[0] // 2
    return pair[:rows], pair[rows:]


def low_sum(*terms):
    total = terms[0].astype(jnp.float32)
    for term in terms[1:]:
        total = total + term.astype(jnp.float32)
    return total.astype(jnp.bfloat16)


def send_far(far):
    one, two = halves(far.astype(jnp.bfloat16))
    return mp_shift(one, 1, 0), mp_shift(two, -1, 0)


def send_middle(below, above, far_one, far_two, work=None):
    below, above, far_one, far_two = lax.optimization_barrier((below, above, far_one, far_two))
    side_down, joined_down = halves(below)
    joined_up, side_up = halves(above)
    side_up = mp_shift(low_sum(side_up), 1, 0)
    joined_down = mp_shift(low_sum(joined_down, far_two), -1, 0)
    joined_up, side_down = low_sum(joined_up, far_one), low_sum(side_down)
    done = work(joined_up) if work else ()
    side_up, joined_down, joined_up, side_down, done = lax.optimization_barrier(
        (side_up, joined_down, joined_up, side_down, done)
    )
    moved = side_up, mp_shift(side_down, -1, 0), joined_down, mp_shift(joined_up, 1, 0)
    return (moved, done) if work else moved


def send_near(near, side_up, side_down, joined_down, joined_up, work=None):
    f32 = jnp.float32
    mine, other = halves(near)
    other = mp_shift(low_sum(other, joined_down, side_up), 0, 1)
    done = work() if work else ()
    other, side_down, joined_up, done = lax.optimization_barrier(
        (other, side_down, joined_up, done)
    )
    total = (
        mine.astype(f32)
        + joined_up.astype(f32)
        + side_down.astype(f32)
        + other.astype(f32)
    )
    return (total, done) if work else total


def rms_forward(values, gain):
    scale = lax.rsqrt(jnp.mean(values * values, axis=-1, keepdims=True) + EPSILON)
    return (values * scale * gain, scale)


def rms_backward(values, scale, gain, grad):
    scaled_grad = grad * gain
    inner = jnp.mean(scaled_grad * values, axis=-1, keepdims=True)
    return scale * scaled_grad - values * scale * scale * scale * inner


def gelu_tanh(values):
    return jax.nn.gelu(values, approximate=True)


def tie(values, anchor):
    return lax.optimization_barrier((values, anchor))[0]


def block_diagonal(weight, width):
    size = weight.shape[1]
    return jnp.concatenate(
        [
            jnp.pad(weight[0], ((0, 0), (0, width - size))),
            jnp.pad(weight[1], ((0, 0), (size, width - 2 * size))),
            jnp.zeros((width - 2 * size, width), weight.dtype),
        ],
        0,
    )


def on_device(
    tokens,
    seg_ids,
    first_gain,
    gelu_weight,
    gelu_bias,
    input_weight,
    input_bias,
    conv_weight,
    conv_bias,
    rate_weight,
    rate_bias,
    inflow_weight,
    inflow_bias,
    decay_param,
    mix_weight,
    second_gain,
    gate_weight,
    up_weight,
    down_weight,
    cotangent,
):
    f32, low = jnp.float32, jnp.bfloat16
    seg_row = seg_ids[0]
    rows = tokens.shape[0]
    model = tokens.shape[1]
    width = gelu_weight.shape[1]
    hidden_width = gate_weight.shape[1]
    size = rate_weight.shape[1]
    wide = -(-width // 128) * 128
    place = lax.axis_index("mp")
    ring, side = place // 2, place % 2
    offsets = jnp.stack(
        [
            (((ring + along + RING) % RING) * 2 + (side + across) % 2) * rows
            for along, across in PIECES
        ]
    ).astype(jnp.int32)

    def dot(left, right):
        return jnp.dot(left, right, preferred_element_type=f32)

    def dot_back(left, right):
        return lax.dot_general(left, right, (((1,), (1,)), ((), ())), preferred_element_type=f32)

    dp_side = (lax.axis_index("dp") // (2 * RING)).astype(jnp.int32).reshape(1)

    rows_in = tokens.astype(f32)
    first_scale_gain = first_gain.astype(f32)
    second_scale_gain = second_gain.astype(f32)
    cot_rows = cotangent.astype(f32)
    first_normed, first_scale = rms_forward(rows_in, first_scale_gain)
    normed_pieces = gather_pieces(first_normed.astype(low))

    keep_list = []
    for steps in (1, 2, 3):
        before = jnp.concatenate([jnp.full((steps,), -1, jnp.int32), seg_row[:-steps]])
        keep_list.append((before == seg_row).astype(f32))
    keep = jnp.stack(keep_list + [jnp.zeros_like(keep_list[0])] * 5, axis=1)
    decay_vals = jnp.pad(decay_param.astype(f32), (0, wide - width), constant_values=1.0)

    def row(values):
        return jnp.pad(values.astype(f32), (0, wide - width))

    params = jnp.stack(
        [row(gelu_bias), row(input_bias), row(conv_bias)]
        + [row(conv_weight[tap]) for tap in range(4)]
        + [
            row(rate_bias),
            row(inflow_bias),
            -DECAY_SCALE * jax.nn.softplus(-decay_vals),
            DECAY_SCALE * jax.nn.sigmoid(-decay_vals),
        ]
        + [jnp.zeros((wide,), f32)] * 5
    )
    lane_pad = ((0, 0), (0, wide - width))
    branch_weight = jnp.concatenate(
        [jnp.pad(gelu_weight, lane_pad), jnp.pad(input_weight, lane_pad)], 1
    )
    mix_wide = jnp.pad(mix_weight, ((0, wide - width), (0, 0)))
    gates_weight = jnp.concatenate(
        [block_diagonal(rate_weight, wide), block_diagonal(inflow_weight, wide)], 1
    )

    normed = join(normed_pieces)
    cot_across = mp_shift(tie(cotangent, normed_pieces[1]), 0, 1)
    cot_mine, cot_across = tie((cotangent, cot_across), normed_pieces[6:])
    cots = [
        cot_mine,
        cot_across,
        mp_shift(cot_mine, 1, 0),
        mp_shift(cot_across, 1, 0),
        mp_shift(cot_mine, -1, 0),
        mp_shift(cot_across, -1, 0),
    ]

    pre = [dot(pair, branch_weight) for pair in normed]
    gated, *kept = run_forward(offsets, pre, keep, params, gates_weight)
    gated, cots = lax.optimization_barrier((gated, cots))

    def pair_rows(values, pair):
        return values[2 * pair * rows : 2 * (pair + 1) * rows]

    mixed = [dot(pair_rows(gated, pair), mix_wide) for pair in range(4)]
    mixed_far = send_far(mixed[3])
    cot_top, cot_bottom = tie((halves(cots[2])[0], halves(cots[4])[1]), mixed_far)
    cot_far = (mp_shift(cot_top, 1, 0), mp_shift(cot_bottom, -1, 0))
    mixed = send_near(mixed[0], *send_middle(mixed[1], mixed[2], *mixed_far))
    middle = rows_in + mixed
    second_normed, second_scale = rms_forward(middle, second_scale_gain)
    second_low, cot_far = lax.optimization_barrier((second_normed.astype(low), cot_far))
    cot_far = jnp.concatenate(cot_far, 0)
    cots = join(cots[:2] + [cots[2], cots[3], cots[4], cots[5]])

    def feed(pair, pieces):
        return run_feed_pair(
            jnp.concatenate(pieces, 0), cots[pair], gate_weight, up_weight, down_weight
        )

    second_pieces, (feed_zero, cot_far_across), feed_one = gather_pieces(
        second_low,
        lambda pieces: (feed(0, pieces), mp_shift(tie(cot_far, pieces), 0, 1)),
        lambda pieces: feed(1, pieces),
    )
    cots.append(jnp.concatenate([cot_far, cot_far_across], 0))
    feed_three = feed(3, second_pieces[6:])
    second_above, second_last = lax.optimization_barrier((second_pieces[4:6], feed_three[3]))
    second_far = send_far(second_last)
    feed_two = feed(2, second_above)
    feed_two, second_far = lax.optimization_barrier((feed_two, second_far))
    feeds = zip(feed_zero, feed_one, feed_two, feed_three)
    hiddens, gate_grads, up_grads, second_grads, downs = [list(values) for values in feeds]
    second = join(second_pieces)
    columns = 3 * hidden_width
    second_moved, feed_sum = send_middle(
        second_grads[1],
        second_grads[2],
        *second_far,
        lambda _: run_column_grads(dp_side, second, gate_grads + up_grads, columns, 0),
    )
    second_grad, feed_sum = send_near(
        second_grads[0],
        *second_moved,
        lambda: run_column_grads(dp_side, cots, hiddens, columns, 2, [feed_sum]),
    )
    feed_sum = half_dp_scatter(feed_sum)
    middle_grad = cot_rows + rms_backward(middle, second_scale, second_scale_gain, second_grad)
    second_gain_local = jnp.sum(second_grad * middle * second_scale, axis=0)
    mixer_pieces = gather_pieces(middle_grad.astype(low))
    mixer = join(mixer_pieces)
    downs = tie(downs, mixer_pieces[6:])
    down_up = mp_shift(jnp.concatenate([halves(downs[3])[0], halves(downs[2])[1]], 0), 1, 0)
    down_down = mp_shift(jnp.concatenate([halves(downs[3])[1], halves(downs[1])[0]], 0), -1, 0)

    gated_grad = [dot_back(pair, mix_wide) for pair in mixer]
    branch_grad, gates_grad, sums = run_backward(
        offsets, gated_grad, pre, keep, params, gates_weight, kept
    )
    branch_grad, down_up, down_down, feed_sum = lax.optimization_barrier(
        (branch_grad, down_up, down_down, feed_sum)
    )
    branch_grad, first_far, down_up, down_down = lax.optimization_barrier(
        (branch_grad, dot_back(pair_rows(branch_grad, 3), branch_weight), down_up, down_down)
    )
    far_one, down_up = halves(down_up)
    far_two, down_down = halves(down_down)
    first_far = send_far(first_far)
    joined = (
        mp_shift(low_sum(halves(downs[1])[1], far_two), -1, 0),
        mp_shift(low_sum(halves(downs[2])[0], far_one), 1, 0),
    )
    branch_parts = run_branch_grads(
        dp_side, normed, mixer, branch_grad, gated, branch_weight, width
    )
    feed_sum = sides_sum(tie(feed_sum, branch_grad))
    branch_parts, first_far, joined, feed_sum = lax.optimization_barrier(
        (branch_parts, first_far, joined, feed_sum)
    )
    branch_sum, gain_rows, first_grads = branch_parts
    branch_sum = half_dp_scatter(branch_sum)
    gains = jnp.stack([gain_rows[:, 0], second_gain_local])
    first_moved, gains = send_middle(
        pair_rows(first_grads, 1),
        pair_rows(first_grads, 2),
        *first_far,
        lambda ready: core_sum(tie(gains, ready), False),
    )
    first_grad, gains = send_near(
        pair_rows(first_grads, 0),
        *first_moved,
        lambda: row_sum(gains, False, 2),
    )
    tokens_grad = middle_grad + rms_backward(rows_in, first_scale, first_scale_gain, first_grad)
    gates_grad, sums = tie((gates_grad, sums), first_grad)
    gate_blocks = jnp.concatenate(
        [
            gates_grad[:size, :size],
            gates_grad[size : 2 * size, size : 2 * size],
            gates_grad[:size, wide : wide + size],
            gates_grad[size : 2 * size, wide + size : wide + 2 * size],
        ],
        1,
    )
    small = jnp.concatenate(
        [gate_blocks, jnp.pad(sums[:, :width], ((0, 0), (0, 4 * size - width)))], 0
    )
    joined = tie(joined, first_moved[0])
    down_total = send_near(downs[0], down_up, down_down, *joined)
    small, gains = core_sum(small, True), row_sum(gains, False, 4)
    small, gains, branch_sum = lax.optimization_barrier((small, gains, branch_sum))
    branch_sum = sides_sum(branch_sum)
    small = side_sum(row_sum(row_sum(small, True, 2), True, 4), True)
    gains = side_sum(gains, False)
    gains, branch_sum = lax.optimization_barrier((gains, branch_sum))
    gains = pair_sum(gains, lambda part: mp_shift(part, 0, 1), False)
    gains, down_total = lax.optimization_barrier((gains, down_total))
    result = (middle + down_total).astype(low)
    gains = ring_sum(gains, lambda part, along: mp_shift(part, along, 0), False)


    sums = small[size : size + 16, :width]
    return (
        result,
        tokens_grad,
        gains[0] / first_scale_gain,
        branch_sum[:, :width],
        sums[0],
        branch_sum[:, width : 2 * width],
        sums[1],
        sums[2:6],
        sums[6],
        jnp.stack([small[:size, :size], small[:size, size : 2 * size]]),
        sums[7],
        jnp.stack([small[:size, 2 * size : 3 * size], small[:size, 3 * size : 4 * size]]),
        sums[8],
        sums[9],
        branch_sum[:, 2 * width :].T,
        gains[1],
        feed_sum[:, :hidden_width],
        feed_sum[:, hidden_width : 2 * hidden_width],
        feed_sum[:, 2 * hidden_width :].T,
    )


def solution(mesh):
    return jax.shard_map(
        on_device,
        mesh=mesh,
        in_specs=(
            P(("dp", "mp"), None),
            P("dp", None),
            P(),
            P(None, "mp"),
            P("mp"),
            P(None, "mp"),
            P("mp"),
            P(None, "mp"),
            P("mp"),
            P("mp", None, None),
            P("mp"),
            P("mp", None, None),
            P("mp"),
            P("mp"),
            P("mp", None),
            P(),
            P(None, "mp"),
            P(None, "mp"),
            P("mp", None),
            P(("dp", "mp"), None),
        ),
        out_specs=(
            P(("dp", "mp"), None),
            P(("dp", "mp"), None),
            P(),
            P("dp", "mp"),
            P("mp"),
            P("dp", "mp"),
            P("mp"),
            P(None, "mp"),
            P("mp"),
            P("mp", None, None),
            P("mp"),
            P("mp", None, None),
            P("mp"),
            P("mp"),
            P("mp", "dp"),
            P(),
            P("dp", "mp"),
            P("dp", "mp"),
            P("mp", "dp"),
        ),
        check_vma=False,
    )
```

```python
import jax
import jax.numpy as jnp
from jax import lax
from jax.experimental import pallas as pl
from jax.experimental.layout import Layout, with_layout_constraint
from jax.experimental.pallas import tpu as pltpu
from jax.sharding import PartitionSpec as P

EPSILON = 1e-06
DECAY_SCALE = 8.0
GELU_SCALE = 0.7978845608028654
GELU_CUBE = 0.044715
CHUNK = 64
PARTS = 8


def one_minus_exp(double_rate, exp_square):
    y = -double_rate
    series = 1.0 - y * (1.0 / 7.0)
    for order in (6.0, 5.0, 4.0, 3.0, 2.0):
        series = 1.0 - y * (1.0 / order) * series
    return jnp.where(y < 0.5, y * series, 1.0 - exp_square)


def gelu_parts(values):
    square = values * values
    slope = GELU_SCALE + (GELU_SCALE * GELU_CUBE) * square
    bend = jnp.tanh(values * slope)
    half = 0.5 + 0.5 * bend
    return half, bend, square


def recurrent_forward(
    offsets, pre_one, pre_two, pre_three, pre_four, keep, params, gate_weight,
    gated, conv, rate, inflow, decay, root, state,
    padded, logits, decays, injects, products, ends,
):
    rows, width = conv.shape
    piece = rows // PARTS
    pairs = (pre_one, pre_two, pre_three, pre_four)

    padded[0:8, :] = jnp.zeros((8, width), jnp.float32)
    for part in range(PARTS):
        place = pl.multiple_of(offsets[part] + 8, 8)
        half = slice(part % 2 * piece, (part % 2 + 1) * piece)
        padded[pl.ds(place, piece), :] = pairs[part // 2][half, width:] + params[1:2, :]

    def conv_chunk(index, carry):
        base = pl.multiple_of(index * CHUNK, CHUNK)
        window = padded[pl.ds(base, CHUNK + 8), :]
        keeps = keep[pl.ds(base, CHUNK), :]
        total = params[2:3, :] + params[3:4, :] * window[8:, :]
        for steps in (1, 2, 3):
            shifted = window[8 - steps : 8 - steps + CHUNK, :]
            total = total + params[3 + steps : 4 + steps, :] * shifted * keeps[:, steps - 1 : steps]
        conv[pl.ds(base, CHUNK), :] = total.astype(jnp.bfloat16)
        return carry

    lax.fori_loop(0, rows // CHUNK, conv_chunk, 0)

    logits[...] = jnp.dot(conv[...], gate_weight[...], preferred_element_type=jnp.float32)

    def gate_chunk(index, carry):
        base = pl.multiple_of(index * CHUNK, CHUNK)
        here = pl.ds(base, CHUNK)
        kept = keep[here, 0:1]
        rate_sig = jax.nn.sigmoid(logits[here, :width] + params[7:8, :])
        inflow_sig = jax.nn.sigmoid(logits[here, width:] + params[8:9, :])
        log_rate = rate_sig * params[9:10, :]
        plain = jnp.exp(log_rate)
        hole = jnp.sqrt(one_minus_exp(2.0 * log_rate, plain * plain))
        factor = hole * kept + (1.0 - kept)
        rate[here, :] = rate_sig
        inflow[here, :] = inflow_sig
        decay[here, :] = plain
        root[here, :] = hole
        kept_decay = plain * kept
        inject = factor * inflow_sig * conv[here, :].astype(jnp.float32)
        for lane in range(width // 128):
            decays[lane, here, :] = kept_decay[:, lane * 128 : (lane + 1) * 128]
            injects[lane, here, :] = inject[:, lane * 128 : (lane + 1) * 128]
        return carry

    lax.fori_loop(0, rows // CHUNK, gate_chunk, 0)

    lanes = width // 128
    zero = jnp.zeros((PARTS, 128), jnp.float32)
    one = jnp.ones((PARTS, 128), jnp.float32)

    def scan_step(step, carry):
        result = []
        for lane in range(lanes):
            value, product = carry[lane]
            factor = decays[lane, pl.ds(step, PARTS, stride=piece), :]
            value = factor * value + injects[lane, pl.ds(step, PARTS, stride=piece), :]
            product = factor * product
            injects[lane, pl.ds(step, PARTS, stride=piece), :] = value
            products[lane, pl.ds(step, PARTS, stride=piece), :] = product
            result.append((value, product))
        return tuple(result)

    last = lax.fori_loop(0, piece, scan_step, ((zero, one),) * lanes, unroll=8)
    for lane in range(lanes):
        value, product = last[lane]
        entering = jnp.zeros((1, 128), jnp.float32)
        for part in range(PARTS):
            ends[part, 0:1, lane * 128 : (lane + 1) * 128] = entering
            entering = value[part : part + 1, :] + product[part : part + 1, :] * entering

    for part in range(PARTS):
        start = pl.multiple_of(offsets[part], piece)
        segment = offsets[part] // piece
        pre = pairs[part // 2]

        def finish_chunk(index, carry, part=part, start=start, segment=segment, pre=pre):
            there = pl.ds(pl.multiple_of(start + index * CHUNK, CHUNK), CHUNK)
            near = pl.ds(pl.multiple_of(part % 2 * piece + index * CHUNK, CHUNK), CHUNK)
            local = pl.ds(pl.multiple_of(part * piece + index * CHUNK, CHUNK), CHUNK)
            for lane in range(lanes):
                cols = slice(lane * 128, (lane + 1) * 128)
                whole = (
                    injects[lane, there, :]
                    + products[lane, there, :] * ends[segment, 0:1, cols]
                )
                state[there, cols] = whole
                values = pre[near, cols] + params[0:1, cols]
                act = values * gelu_parts(values)[0]
                gated[local, cols] = (act * whole).astype(jnp.bfloat16)
            return carry

        lax.fori_loop(0, piece // CHUNK, finish_chunk, 0)


def recurrent_backward(
    offsets, grad_one, grad_two, grad_three, grad_four, pre_one, pre_two, pre_three, pre_four,
    keep, params, gate_weight, conv, rate, inflow, decay, root, state,
    branch_grad, gate_grad, sums,
    padded, carried, decays, products, ends, before, logit_grad, conv_grad, shifted_grad,
):
    rows, width = conv.shape
    piece = rows // PARTS
    lanes = width // 128
    grad_pairs = (grad_one, grad_two, grad_three, grad_four)
    pre_pairs = (pre_one, pre_two, pre_three, pre_four)
    zero_rows = jnp.zeros((8, width), jnp.float32)

    padded[0:8, :] = zero_rows
    before[0:8, :] = zero_rows
    for lane in range(lanes):
        decays[lane, rows : rows + 8, :] = jnp.zeros((8, 128), jnp.float32)
    shifted_grad[:, rows : rows + 8, :] = jnp.zeros((3, 8, width), jnp.float32)

    gelu_sum = zero_rows
    for part in range(PARTS):
        start = pl.multiple_of(offsets[part], piece)
        pre, gated_grad = pre_pairs[part // 2], grad_pairs[part // 2]

        def enter_chunk(index, total, part=part, start=start, pre=pre, gated_grad=gated_grad):
            there = pl.ds(pl.multiple_of(start + index * CHUNK, CHUNK), CHUNK)
            ahead = pl.ds(pl.multiple_of(start + index * CHUNK + 8, 8), CHUNK)
            near = pl.ds(pl.multiple_of(part % 2 * piece + index * CHUNK, CHUNK), CHUNK)
            local = pl.ds(pl.multiple_of(part * piece + index * CHUNK, CHUNK), CHUNK)
            kept = keep[there, 0:1]
            padded[ahead, :] = pre[near, width:] + params[1:2, :]
            values = pre[near, :width] + params[0:1, :]
            upper, bend, square = gelu_parts(values)
            slope = upper + 0.5 * values * (1.0 - bend * bend) * (
                GELU_SCALE + (3.0 * GELU_SCALE * GELU_CUBE) * square
            )
            grad = gated_grad[near, :]
            here_state = state[there, :]
            before[ahead, :] = here_state
            gelu_grad = (grad * here_state * slope).astype(jnp.bfloat16)
            branch_grad[local, :width] = gelu_grad
            state_grad = grad * values * upper
            kept_decay = decay[there, :] * kept
            for lane in range(lanes):
                cols = slice(lane * 128, (lane + 1) * 128)
                carried[lane, there, :] = state_grad[:, cols]
                decays[lane, there, :] = kept_decay[:, cols]
            return total + jnp.sum(
                gelu_grad.astype(jnp.float32).reshape(CHUNK // 8, 8, width), axis=0
            )

        gelu_sum = lax.fori_loop(0, piece // CHUNK, enter_chunk, gelu_sum)

    zero = jnp.zeros((PARTS, 128), jnp.float32)
    one = jnp.ones((PARTS, 128), jnp.float32)

    def scan_step(count, carry):
        step = piece - 1 - count
        result = []
        for lane in range(lanes):
            value, product = carry[lane]
            factor = decays[lane, pl.ds(step + 1, PARTS, stride=piece), :]
            value = factor * value + carried[lane, pl.ds(step, PARTS, stride=piece), :]
            product = factor * product
            carried[lane, pl.ds(step, PARTS, stride=piece), :] = value
            products[lane, pl.ds(step, PARTS, stride=piece), :] = product
            result.append((value, product))
        return tuple(result)

    last = lax.fori_loop(0, piece, scan_step, ((zero, one),) * lanes, unroll=8)
    for lane in range(lanes):
        value, product = last[lane]
        entering = jnp.zeros((1, 128), jnp.float32)
        for part in range(PARTS - 1, -1, -1):
            ends[part, 0:1, lane * 128 : (lane + 1) * 128] = entering
            entering = value[part : part + 1, :] + product[part : part + 1, :] * entering

    def gate_chunk(index, totals):
        rate_sum, inflow_sum, decay_sum = totals
        base = pl.multiple_of(index * CHUNK, CHUNK)
        here = pl.ds(base, CHUNK)
        segment = base // piece
        kept = keep[here, 0:1]
        grad = jnp.concatenate(
            [
                carried[lane, here, :]
                + products[lane, here, :]
                * ends[segment, 0:1, lane * 128 : (lane + 1) * 128]
                for lane in range(lanes)
            ],
            axis=1,
        )
        earlier = before[pl.ds(base, CHUNK + 8), :][7 : 7 + CHUNK, :]
        plain = decay[here, :]
        hole = root[here, :]
        rate_sig = rate[here, :]
        inflow_sig = inflow[here, :]
        conv_vals = conv[here, :].astype(jnp.float32)
        factor = hole * kept + (1.0 - kept)
        scaled = grad * inflow_sig
        log_grad = (
            (grad * earlier * plain - scaled * conv_vals * (plain * plain) / hole) * kept
        )
        rate_low = (
            log_grad * params[9:10, :] * rate_sig * (1.0 - rate_sig)
        ).astype(jnp.bfloat16)
        elem = scaled * factor
        inflow_low = (elem * conv_vals * (1.0 - inflow_sig)).astype(jnp.bfloat16)
        logit_grad[here, :width] = rate_low
        logit_grad[here, width:] = inflow_low
        conv_grad[here, :] = elem

        def fold(values):
            return jnp.sum(values.reshape(CHUNK // 8, 8, width), axis=0)

        return (
            rate_sum + fold(rate_low.astype(jnp.float32)),
            inflow_sum + fold(inflow_low.astype(jnp.float32)),
            decay_sum + fold(log_grad * rate_sig),
        )

    rate_sum, inflow_sum, decay_sum = lax.fori_loop(
        0, rows // CHUNK, gate_chunk, (zero_rows, zero_rows, zero_rows)
    )

    conv_grad[...] += lax.dot_general(
        logit_grad[...],
        gate_weight[...],
        (((1,), (1,)), ((), ())),
        preferred_element_type=jnp.float32,
    )
    gate_grad[...] = lax.dot_general(
        conv[...],
        logit_grad[...],
        (((0,), (0,)), ((), ())),
        preferred_element_type=jnp.float32,
    )

    def tap_chunk(index, totals):
        base = pl.multiple_of(index * CHUNK, CHUNK)
        here = pl.ds(base, CHUNK)
        grad = conv_grad[here, :]
        keeps = keep[here, :]
        window = padded[pl.ds(base, CHUNK + 8), :]

        def fold(values):
            return jnp.sum(values.reshape(CHUNK // 8, 8, width), axis=0)

        result = [totals[0] + fold(grad), totals[1] + fold(grad * window[8:, :])]
        for steps in (1, 2, 3):
            kept_grad = grad * keeps[:, steps - 1 : steps]
            shifted_grad[steps - 1, here, :] = kept_grad
            result.append(
                totals[1 + steps] + fold(kept_grad * window[8 - steps : 8 - steps + CHUNK, :])
            )
        return tuple(result)

    taps = lax.fori_loop(0, rows // CHUNK, tap_chunk, (zero_rows,) * 5)

    def leave_part(part, total):
        start = pl.multiple_of(offsets[part], piece)
        for half in range(piece // CHUNK):
            base = pl.multiple_of(start + half * CHUNK, CHUNK)
            local = pl.ds(pl.multiple_of(part * piece + half * CHUNK, CHUNK), CHUNK)
            grad = params[3:4, :] * conv_grad[pl.ds(base, CHUNK), :]
            for steps in (1, 2, 3):
                window = shifted_grad[steps - 1, pl.ds(base, CHUNK + 8), :]
                grad = grad + params[3 + steps : 4 + steps, :] * window[steps : steps + CHUNK, :]
            low = grad.astype(jnp.bfloat16)
            branch_grad[local, width:] = low
            total = total + jnp.sum(low.astype(jnp.float32).reshape(CHUNK // 8, 8, width), axis=0)
        return total

    input_sum = lax.fori_loop(0, PARTS, leave_part, zero_rows)

    all_sums = (
        gelu_sum, input_sum, taps[1], taps[2], taps[3], taps[4], taps[0], rate_sum, inflow_sum,
    )
    for row, total in enumerate(all_sums):
        sums[row : row + 1, :] = jnp.sum(total, axis=0, keepdims=True)
    sums[9:10, :] = jnp.sum(decay_sum, axis=0, keepdims=True) * params[10:11, :]
    sums[10:16, :] = jnp.zeros((6, width), jnp.float32)


def dot_rows(left, right):
    return lax.dot_general(
        left, right, (((0,), (0,)), ((), ())), preferred_element_type=jnp.float32
    )


def dot_back(left, right):
    return lax.dot_general(
        left, right, (((1,), (1,)), ((), ())), preferred_element_type=jnp.float32
    )


def dot_plain(left, right):
    return jnp.dot(left, right, preferred_element_type=jnp.float32)


def feed_pair(
    second, cots, gate_weight, up_weight, down_weight, hidden, gate_grad, up_grad, back, down,
    back_total, down_total,
):
    step = pl.program_id(0)
    gate = dot_plain(second[...], gate_weight[...])
    up = dot_plain(second[...], up_weight[...])
    upper, bend, square = gelu_parts(gate)
    act = gate * upper
    low = (act * up).astype(jnp.bfloat16)
    hidden[...] = low
    grad = dot_back(cots[...], down_weight[...])
    slope = upper + 0.5 * gate * (1.0 - bend * bend) * (
        GELU_SCALE + (3.0 * GELU_SCALE * GELU_CUBE) * square
    )
    gate_low = (grad * up * slope).astype(jnp.bfloat16)
    up_low = (grad * act).astype(jnp.bfloat16)
    gate_grad[...] = gate_low
    up_grad[...] = up_low
    back_part = dot_back(gate_low, gate_weight[...]) + dot_back(up_low, up_weight[...])
    down_part = dot_plain(low, down_weight[...])

    @pl.when(step == 0)
    def _():
        back_total[...] = back_part
        down_total[...] = down_part

    @pl.when(step > 0)
    def _():
        back_total[...] += back_part
        down_total[...] += down_part

    @pl.when(step == pl.num_programs(0) - 1)
    def _():
        back[...] = back_total[...].astype(jnp.bfloat16)
        down[...] = down_total[...].astype(jnp.bfloat16)


def join_columns(pairs, joined, column=0):
    size, width = pairs[0].shape
    for index, pair in enumerate(pairs):
        joined[index * size : (index + 1) * size, column : column + width] = pair[...]


def split_cores(total, out):
    size = out.shape[3]
    for core in range(2):
        out[0, core, 0, :, :] = total[core * size : (core + 1) * size, :].astype(out.dtype)


def column_grads(side, *refs):
    left, right = refs[:4], refs[4:-3]
    out, left_rows, right_rows = refs[-3:]
    width = right[0].shape[1]

    @pl.when(pl.program_id(0) == 0)
    def _():
        for group in range(right_rows.shape[1] // width):
            join_columns(right[4 * group : 4 * group + 4], right_rows, group * width)

    join_columns(left, left_rows)
    split_cores(dot_rows(left_rows[...], right_rows[...]), out)


def branch_grads(side, *refs):
    normed, mixer, refs = refs[:4], refs[4:8], refs[8:]
    branch_grad, gated, weight, out, gain = refs[:5]
    backs, normed_rows, mixer_rows = refs[5:-2], refs[-2], refs[-1]
    wide = gated.shape[1]
    width = out.shape[4] // 3
    join_columns(normed, normed_rows)
    join_columns(mixer, mixer_rows)
    size = backs[0].shape[0]
    back = dot_back(branch_grad[: len(backs) * size, :], weight[...]).astype(jnp.bfloat16)
    for index, part in enumerate(backs):
        part[...] = back[index * size : (index + 1) * size, :]
    branch = dot_rows(normed_rows[...], branch_grad[...])
    mix = dot_rows(mixer_rows[...], gated[...])
    weighted = jnp.sum(branch * weight[...].astype(jnp.float32), axis=1, keepdims=True)
    gain[...] = jnp.broadcast_to(weighted, gain.shape)
    total = jnp.concatenate(
        [branch[:, :width], branch[:, wide : wide + width], mix[:, :width]], axis=1
    )
    split_cores(total, out)


VMEM_SPEC = pl.BlockSpec(memory_space=pltpu.VMEM)
SMEM_SPEC = pl.BlockSpec(memory_space=pltpu.SMEM)


MEGA = 1024 * 1024
TILE = 256


def run_forward(offsets, pre, keep, params, gate_weight):
    rows, width = 4 * pre[0].shape[0], pre[0].shape[1] // 2
    lanes = width // 128
    f32, low = jnp.float32, jnp.bfloat16
    full = jax.ShapeDtypeStruct((rows, width), f32)
    half = jax.ShapeDtypeStruct((rows, width), low)
    return pl.pallas_call(
        recurrent_forward,
        out_shape=(half, half, full, full, full, full, full),
        in_specs=[SMEM_SPEC] + [VMEM_SPEC] * 7,
        out_specs=(VMEM_SPEC,) * 7,
        scratch_shapes=[
            pltpu.VMEM((rows + 8, width), f32),
            pltpu.VMEM((rows, 2 * width), f32),
            pltpu.VMEM((lanes, rows, 128), f32),
            pltpu.VMEM((lanes, rows, 128), f32),
            pltpu.VMEM((lanes, rows, 128), f32),
            pltpu.VMEM((PARTS, 8, width), f32),
        ],
        compiler_params=pltpu.CompilerParams(vmem_limit_bytes=40 * MEGA),
    )(offsets, *pre, keep, params, gate_weight)


def run_backward(offsets, gated_grad, pre, keep, params, gate_weight, kept):
    rows, width = 4 * pre[0].shape[0], pre[0].shape[1] // 2
    lanes = width // 128
    f32, low = jnp.float32, jnp.bfloat16
    return pl.pallas_call(
        recurrent_backward,
        out_shape=(
            jax.ShapeDtypeStruct((rows, 2 * width), low),
            jax.ShapeDtypeStruct((width, 2 * width), f32),
            jax.ShapeDtypeStruct((16, width), f32),
        ),
        in_specs=[SMEM_SPEC] + [VMEM_SPEC] * 17,
        out_specs=(VMEM_SPEC,) * 3,
        scratch_shapes=[
            pltpu.VMEM((rows + 8, width), f32),
            pltpu.VMEM((lanes, rows, 128), f32),
            pltpu.VMEM((lanes, rows + 8, 128), f32),
            pltpu.VMEM((lanes, rows, 128), f32),
            pltpu.VMEM((PARTS, 8, width), f32),
            pltpu.VMEM((rows + 8, width), f32),
            pltpu.VMEM((rows, 2 * width), low),
            pltpu.VMEM((rows, width), f32),
            pltpu.VMEM((3, rows + 8, width), f32),
        ],
        compiler_params=pltpu.CompilerParams(vmem_limit_bytes=48 * MEGA),
    )(offsets, *gated_grad, *pre, keep, params, gate_weight, *kept)


def column_spec(rows):
    return pl.BlockSpec((rows, TILE), lambda step, side: (0, step))


def placed_spec(columns, column):
    return pl.BlockSpec(
        (1, 2, 1, TILE // 2, columns),
        lambda step, side: (step % 4, 0, (step // 4 + side[0]) % 2, 0, column),
    )


def placed_shape(model, columns):
    return pltpu.HBM((model // TILE // 2, 2, 2, TILE // 2, columns), jnp.bfloat16)


def whole_spec(array):
    return pl.BlockSpec(array.shape, lambda step, side: (0, 0))


def run_feed_pair(second, cots, gate_weight, up_weight, down_weight):
    size, model = second.shape
    width = gate_weight.shape[1]
    whole = pl.BlockSpec((size, model), lambda step: (0, 0))
    across = pl.BlockSpec((model, TILE), lambda step: (0, step))
    slim = pl.BlockSpec((size, TILE), lambda step: (0, step))
    narrow = jax.ShapeDtypeStruct((size, width), jnp.bfloat16)
    long = jax.ShapeDtypeStruct((size, model), jnp.bfloat16)
    return pl.pallas_call(
        feed_pair,
        grid=(width // TILE,),
        in_specs=[
            whole, whole, across, across, pl.BlockSpec((TILE, model), lambda step: (step, 0))
        ],
        out_specs=(slim, slim, slim, whole, whole),
        out_shape=(narrow, narrow, narrow, long, long),
        scratch_shapes=[pltpu.VMEM((size, model), jnp.float32)] * 2,
        compiler_params=pltpu.CompilerParams(vmem_limit_bytes=28 * MEGA),
    )(second, cots, gate_weight, up_weight, down_weight)


def run_column_grads(side, left, right, columns, column, earlier=()):
    size, model = left[0].shape
    width = len(right) // 4 * right[0].shape[1]
    return pl.pallas_call(
        column_grads,
        grid_spec=pltpu.PrefetchScalarGridSpec(
            num_scalar_prefetch=1,
            grid=(model // TILE,),
            in_specs=[column_spec(size)] * 4
            + [whole_spec(pair) for pair in right]
            + [pl.BlockSpec(memory_space=pl.ANY)] * len(earlier),
            out_specs=placed_spec(width, column),
            scratch_shapes=[
                pltpu.VMEM((4 * size, TILE), jnp.bfloat16),
                pltpu.VMEM((4 * size, width), jnp.bfloat16),
            ],
        ),
        out_shape=placed_shape(model, columns),
        input_output_aliases={5 + len(right): 0} if earlier else {},
        compiler_params=pltpu.CompilerParams(vmem_limit_bytes=28 * MEGA),
    )(side, *left, *right, *earlier)


def run_branch_grads(side, normed, mixer, branch_grad, gated, weight, width):
    size, model = normed[0].shape
    return pl.pallas_call(
        branch_grads,
        grid_spec=pltpu.PrefetchScalarGridSpec(
            num_scalar_prefetch=1,
            grid=(model // TILE,),
            in_specs=[column_spec(size)] * 8
            + [whole_spec(branch_grad), whole_spec(gated)]
            + [pl.BlockSpec((TILE, weight.shape[1]), lambda step, side: (step, 0))],
            out_specs=(
                placed_spec(3 * width, 0),
                pl.BlockSpec((TILE, 128), lambda step, side: (step, 0)),
            )
            + (column_spec(size // 2),) * 6,
            scratch_shapes=[pltpu.VMEM((4 * size, TILE), jnp.bfloat16)] * 2,
        ),
        out_shape=(
            placed_shape(model, 3 * width),
            pltpu.HBM((model, 128), jnp.float32),
        )
        + (pltpu.HBM((size // 2, model), jnp.bfloat16),) * 6,
        compiler_params=pltpu.CompilerParams(vmem_limit_bytes=28 * MEGA),
    )(side, *normed, *mixer, branch_grad, gated, weight)


RING = 4
PIECES = ((0, 0), (0, 1), (-1, 0), (-1, 1), (1, 0), (1, 1), (2, 0), (2, 1))


def mp_shift(values, along, across):
    pairs = [
        (ring * 2 + side, ((ring + along) % RING) * 2 + (side + across) % 2)
        for ring in range(RING)
        for side in range(2)
    ]
    return lax.ppermute(values, "mp", pairs)


def dp_shift(values, across, along, core):
    pairs = [
        (
            (side * RING + ring) * 2 + own,
            (((side + across) % 2) * RING + (ring + along) % RING) * 2 + (own + core) % 2,
        )
        for side in range(2)
        for ring in range(RING)
        for own in range(2)
    ]
    return lax.ppermute(values, "dp", pairs)


def half_dp_scatter(values):
    groups = [list(range(side * 2 * RING, (side + 1) * 2 * RING)) for side in range(2)]
    values = with_layout_constraint(values.reshape(-1, values.shape[-1]), Layout((0, 1)))
    total = lax.psum_scatter(
        values, "dp", scatter_dimension=0, tiled=True, axis_index_groups=groups
    )
    return with_layout_constraint(total, Layout((0, 1)))


def sides_sum(values):
    mine, other = halves(values)
    return mine.astype(jnp.float32) + dp_shift(other, 1, 0, 0).astype(jnp.float32)


def pair_sum(values, shift, low):
    values = values.astype(jnp.bfloat16) if low else values
    return values.astype(jnp.float32) + shift(values).astype(jnp.float32)


def ring_sum(values, shift, low):
    values = values.astype(jnp.bfloat16) if low else values
    one, two, three = [shift(values, along).astype(jnp.float32) for along in (1, 2, 3)]
    return (values.astype(jnp.float32) + two) + (one + three)


def core_sum(values, low):
    return pair_sum(values, lambda part: dp_shift(part, 0, 0, 1), low)


def row_sum(values, low, step):
    def swap(part):
        return lax.ppermute(part, "dp", [(place, place ^ step) for place in range(4 * RING)])

    return pair_sum(values, swap, low)


def side_sum(values, low):
    return pair_sum(values, lambda part: dp_shift(part, 1, 0, 0), low)


def join(values):
    return [jnp.concatenate(values[at : at + 2], 0) for at in range(0, len(values), 2)]


def gather_pieces(mine, second_work=None, third_work=None):
    across = mp_shift(mine, 0, 1)
    below = mp_shift(mine, 1, 0)
    above = mp_shift(mine, -1, 0)
    across, below, above = lax.optimization_barrier((across, below, above))
    below_across = mp_shift(across, 1, 0)
    above_across = mp_shift(across, -1, 0)
    done = second_work([mine, across]) if second_work else ()
    below_across, above_across, near_below, second_done = lax.optimization_barrier(
        (below_across, above_across, below, done)
    )
    far = mp_shift(near_below, 1, 0)
    far_across = mp_shift(above_across, -1, 0)
    done = third_work([below, below_across]) if third_work else ()
    far, far_across, third_done = lax.optimization_barrier((far, far_across, done))
    pieces = [mine, across, below, below_across, above, above_across, far, far_across]
    if second_work or third_work:
        return pieces, second_done, third_done
    return pieces


def halves(pair):
    if isinstance(pair, (tuple, list)):
        return pair
    rows = pair.shape[0] // 2
    return pair[:rows], pair[rows:]


def low_sum(*terms):
    total = terms[0].astype(jnp.float32)
    for term in terms[1:]:
        total = total + term.astype(jnp.float32)
    return total.astype(jnp.bfloat16)


def send_far(far):
    one, two = halves(far.astype(jnp.bfloat16))
    return mp_shift(one, 1, 0), mp_shift(two, -1, 0)


def send_middle(below, above, far_one, far_two, work=None):
    below, above, far_one, far_two = lax.optimization_barrier((below, above, far_one, far_two))
    side_down, joined_down = halves(below)
    joined_up, side_up = halves(above)
    side_up = mp_shift(low_sum(side_up), 1, 0)
    joined_down = mp_shift(low_sum(joined_down, far_two), -1, 0)
    joined_up, side_down = low_sum(joined_up, far_one), low_sum(side_down)
    done = work(joined_up) if work else ()
    side_up, joined_down, joined_up, side_down, done = lax.optimization_barrier(
        (side_up, joined_down, joined_up, side_down, done)
    )
    moved = side_up, mp_shift(side_down, -1, 0), joined_down, mp_shift(joined_up, 1, 0)
    return (moved, done) if work else moved


def send_near(near, side_up, side_down, joined_down, joined_up, work=None):
    f32 = jnp.float32
    mine, other = halves(near)
    other = mp_shift(low_sum(other, joined_down, side_up), 0, 1)
    done = work() if work else ()
    other, side_down, joined_up, done = lax.optimization_barrier(
        (other, side_down, joined_up, done)
    )
    total = (
        mine.astype(f32)
        + joined_up.astype(f32)
        + side_down.astype(f32)
        + other.astype(f32)
    )
    return (total, done) if work else total


def rms_forward(values, gain):
    scale = lax.rsqrt(jnp.mean(values * values, axis=-1, keepdims=True) + EPSILON)
    return (values * scale * gain, scale)


def rms_backward(values, scale, gain, grad):
    scaled_grad = grad * gain
    inner = jnp.mean(scaled_grad * values, axis=-1, keepdims=True)
    return scale * scaled_grad - values * scale * scale * scale * inner


def gelu_tanh(values):
    return jax.nn.gelu(values, approximate=True)


def tie(values, anchor):
    return lax.optimization_barrier((values, anchor))[0]


def block_diagonal(weight, width):
    size = weight.shape[1]
    return jnp.concatenate(
        [
            jnp.pad(weight[0], ((0, 0), (0, width - size))),
            jnp.pad(weight[1], ((0, 0), (size, width - 2 * size))),
            jnp.zeros((width - 2 * size, width), weight.dtype),
        ],
        0,
    )


def on_device(
    tokens,
    seg_ids,
    first_gain,
    gelu_weight,
    gelu_bias,
    input_weight,
    input_bias,
    conv_weight,
    conv_bias,
    rate_weight,
    rate_bias,
    inflow_weight,
    inflow_bias,
    decay_param,
    mix_weight,
    second_gain,
    gate_weight,
    up_weight,
    down_weight,
    cotangent,
):
    f32, low = jnp.float32, jnp.bfloat16
    seg_row = seg_ids[0]
    rows = tokens.shape[0]
    model = tokens.shape[1]
    width = gelu_weight.shape[1]
    hidden_width = gate_weight.shape[1]
    size = rate_weight.shape[1]
    wide = -(-width // 128) * 128
    place = lax.axis_index("mp")
    ring, side = place // 2, place % 2
    offsets = jnp.stack(
        [
            (((ring + along + RING) % RING) * 2 + (side + across) % 2) * rows
            for along, across in PIECES
        ]
    ).astype(jnp.int32)

    def dot(left, right):
        return jnp.dot(left, right, preferred_element_type=f32)

    def dot_back(left, right):
        return lax.dot_general(left, right, (((1,), (1,)), ((), ())), preferred_element_type=f32)

    dp_side = (lax.axis_index("dp") // (2 * RING)).astype(jnp.int32).reshape(1)

    rows_in = tokens.astype(f32)
    first_scale_gain = first_gain.astype(f32)
    second_scale_gain = second_gain.astype(f32)
    cot_rows = cotangent.astype(f32)
    first_normed, first_scale = rms_forward(rows_in, first_scale_gain)
    normed_pieces = gather_pieces(first_normed.astype(low))

    keep_list = []
    for steps in (1, 2, 3):
        before = jnp.concatenate([jnp.full((steps,), -1, jnp.int32), seg_row[:-steps]])
        keep_list.append((before == seg_row).astype(f32))
    keep = jnp.stack(keep_list + [jnp.zeros_like(keep_list[0])] * 5, axis=1)
    decay_vals = jnp.pad(decay_param.astype(f32), (0, wide - width), constant_values=1.0)

    def row(values):
        return jnp.pad(values.astype(f32), (0, wide - width))

    params = jnp.stack(
        [row(gelu_bias), row(input_bias), row(conv_bias)]
        + [row(conv_weight[tap]) for tap in range(4)]
        + [
            row(rate_bias),
            row(inflow_bias),
            -DECAY_SCALE * jax.nn.softplus(-decay_vals),
            DECAY_SCALE * jax.nn.sigmoid(-decay_vals),
        ]
        + [jnp.zeros((wide,), f32)] * 5
    )
    lane_pad = ((0, 0), (0, wide - width))
    branch_weight = jnp.concatenate(
        [jnp.pad(gelu_weight, lane_pad), jnp.pad(input_weight, lane_pad)], 1
    )
    mix_wide = jnp.pad(mix_weight, ((0, wide - width), (0, 0)))
    gates_weight = jnp.concatenate(
        [block_diagonal(rate_weight, wide), block_diagonal(inflow_weight, wide)], 1
    )

    normed = join(normed_pieces)
    cot_across = mp_shift(tie(cotangent, normed_pieces[1]), 0, 1)
    cot_mine, cot_across = tie((cotangent, cot_across), normed_pieces[6:])
    cots = [
        cot_mine,
        cot_across,
        mp_shift(cot_mine, 1, 0),
        mp_shift(cot_across, 1, 0),
        mp_shift(cot_mine, -1, 0),
        mp_shift(cot_across, -1, 0),
    ]

    pre = [dot(pair, branch_weight) for pair in normed]
    gated, *kept = run_forward(offsets, pre, keep, params, gates_weight)
    gated, cots = lax.optimization_barrier((gated, cots))

    def pair_rows(values, pair):
        return values[2 * pair * rows : 2 * (pair + 1) * rows]

    mixed = [dot(pair_rows(gated, pair), mix_wide) for pair in range(4)]
    mixed_far = send_far(mixed[3])
    cot_top, cot_bottom = tie((halves(cots[2])[0], halves(cots[4])[1]), mixed_far)
    cot_far = (mp_shift(cot_top, 1, 0), mp_shift(cot_bottom, -1, 0))
    mixed = send_near(mixed[0], *send_middle(mixed[1], mixed[2], *mixed_far))
    middle = rows_in + mixed
    second_normed, second_scale = rms_forward(middle, second_scale_gain)
    second_low, cot_far = lax.optimization_barrier((second_normed.astype(low), cot_far))
    cot_far = jnp.concatenate(cot_far, 0)
    cots = join(cots[:2] + [cots[2], cots[3], cots[4], cots[5]])

    def feed(pair, pieces):
        return run_feed_pair(
            jnp.concatenate(pieces, 0), cots[pair], gate_weight, up_weight, down_weight
        )

    second_pieces, (feed_zero, cot_far_across), feed_one = gather_pieces(
        second_low,
        lambda pieces: (feed(0, pieces), mp_shift(tie(cot_far, pieces), 0, 1)),
        lambda pieces: feed(1, pieces),
    )
    cots.append(jnp.concatenate([cot_far, cot_far_across], 0))
    feed_three = feed(3, second_pieces[6:])
    second_above, second_last = lax.optimization_barrier((second_pieces[4:6], feed_three[3]))
    second_far = send_far(second_last)
    feed_two = feed(2, second_above)
    feed_two, second_far = lax.optimization_barrier((feed_two, second_far))
    feeds = zip(feed_zero, feed_one, feed_two, feed_three)
    hiddens, gate_grads, up_grads, second_grads, downs = [list(values) for values in feeds]
    second = join(second_pieces)
    columns = 3 * hidden_width
    second_moved, feed_sum = send_middle(
        second_grads[1],
        second_grads[2],
        *second_far,
        lambda _: run_column_grads(dp_side, second, gate_grads + up_grads, columns, 0),
    )
    second_grad, feed_sum = send_near(
        second_grads[0],
        *second_moved,
        lambda: run_column_grads(dp_side, cots, hiddens, columns, 2, [feed_sum]),
    )
    feed_sum = half_dp_scatter(feed_sum)
    middle_grad = cot_rows + rms_backward(middle, second_scale, second_scale_gain, second_grad)
    second_gain_local = jnp.sum(second_grad * middle * second_scale, axis=0)
    mixer_pieces = gather_pieces(middle_grad.astype(low))
    mixer = join(mixer_pieces)
    downs = tie(downs, mixer_pieces[6:])
    down_up = mp_shift(jnp.concatenate([halves(downs[3])[0], halves(downs[2])[1]], 0), 1, 0)
    down_down = mp_shift(jnp.concatenate([halves(downs[3])[1], halves(downs[1])[0]], 0), -1, 0)

    gated_grad = [dot_back(pair, mix_wide) for pair in mixer]
    branch_grad, gates_grad, sums = run_backward(
        offsets, gated_grad, pre, keep, params, gates_weight, kept
    )
    branch_grad, down_up, down_down, feed_sum = lax.optimization_barrier(
        (branch_grad, down_up, down_down, feed_sum)
    )
    branch_grad, first_far, down_up, down_down = lax.optimization_barrier(
        (branch_grad, dot_back(pair_rows(branch_grad, 3), branch_weight), down_up, down_down)
    )
    far_one, down_up = halves(down_up)
    far_two, down_down = halves(down_down)
    first_far = send_far(first_far)
    joined = (
        mp_shift(low_sum(halves(downs[1])[1], far_two), -1, 0),
        mp_shift(low_sum(halves(downs[2])[0], far_one), 1, 0),
    )
    branch_parts = run_branch_grads(
        dp_side, normed, mixer, branch_grad, gated, branch_weight, width
    )
    feed_sum = sides_sum(tie(feed_sum, branch_grad))
    branch_parts, first_far, joined, feed_sum = lax.optimization_barrier(
        (branch_parts, first_far, joined, feed_sum)
    )
    branch_sum, gain_rows, *first_grads = branch_parts
    branch_sum = half_dp_scatter(branch_sum)
    gains = jnp.stack([gain_rows[:, 0], second_gain_local])
    first_moved, gains = send_middle(
        first_grads[2:4],
        first_grads[4:6],
        *first_far,
        lambda ready: core_sum(tie(gains, ready), False),
    )
    first_grad, gains = send_near(
        first_grads[:2],
        *first_moved,
        lambda: row_sum(gains, False, 2),
    )
    tokens_grad = middle_grad + rms_backward(rows_in, first_scale, first_scale_gain, first_grad)
    gates_grad, sums = tie((gates_grad, sums), first_grad)
    gate_blocks = jnp.concatenate(
        [
            gates_grad[:size, :size],
            gates_grad[size : 2 * size, size : 2 * size],
            gates_grad[:size, wide : wide + size],
            gates_grad[size : 2 * size, wide + size : wide + 2 * size],
        ],
        1,
    )
    small = jnp.concatenate(
        [gate_blocks, jnp.pad(sums[:, :width], ((0, 0), (0, 4 * size - width)))], 0
    )
    joined = tie(joined, first_moved[0])
    down_total = send_near(downs[0], down_up, down_down, *joined)
    small, gains = core_sum(small, True), row_sum(gains, False, 4)
    small, gains, branch_sum = lax.optimization_barrier((small, gains, branch_sum))
    branch_sum = sides_sum(branch_sum)
    small = side_sum(row_sum(row_sum(small, True, 2), True, 4), True)
    gains = side_sum(gains, False)
    gains, branch_sum = lax.optimization_barrier((gains, branch_sum))
    gains = pair_sum(gains, lambda part: mp_shift(part, 0, 1), False)
    gains, down_total = lax.optimization_barrier((gains, down_total))
    result = (middle + down_total).astype(low)
    gains = ring_sum(gains, lambda part, along: mp_shift(part, along, 0), False)


    sums = small[size : size + 16, :width]
    return (
        result,
        tokens_grad,
        gains[0] / first_scale_gain,
        branch_sum[:, :width],
        sums[0],
        branch_sum[:, width : 2 * width],
        sums[1],
        sums[2:6],
        sums[6],
        jnp.stack([small[:size, :size], small[:size, size : 2 * size]]),
        sums[7],
        jnp.stack([small[:size, 2 * size : 3 * size], small[:size, 3 * size : 4 * size]]),
        sums[8],
        sums[9],
        branch_sum[:, 2 * width :].T,
        gains[1],
        feed_sum[:, :hidden_width],
        feed_sum[:, hidden_width : 2 * hidden_width],
        feed_sum[:, 2 * hidden_width :].T,
    )


def solution(mesh):
    return jax.shard_map(
        on_device,
        mesh=mesh,
        in_specs=(
            P(("dp", "mp"), None),
            P("dp", None),
            P(),
            P(None, "mp"),
            P("mp"),
            P(None, "mp"),
            P("mp"),
            P(None, "mp"),
            P("mp"),
            P("mp", None, None),
            P("mp"),
            P("mp", None, None),
            P("mp"),
            P("mp"),
            P("mp", None),
            P(),
            P(None, "mp"),
            P(None, "mp"),
            P("mp", None),
            P(("dp", "mp"), None),
        ),
        out_specs=(
            P(("dp", "mp"), None),
            P(("dp", "mp"), None),
            P(),
            P("dp", "mp"),
            P("mp"),
            P("dp", "mp"),
            P("mp"),
            P(None, "mp"),
            P("mp"),
            P("mp", None, None),
            P("mp"),
            P("mp", None, None),
            P("mp"),
            P("mp"),
            P("mp", "dp"),
            P(),
            P("dp", "mp"),
            P("dp", "mp"),
            P("mp", "dp"),
        ),
        check_vma=False,
    )
```
